128 devices in a mesh: gx: 16 (over z, y), gy: 8 (over x, core).
Axes of the slice: x: 4, y: 4, z: 4, core: 2. Of those that a mesh axis runs over, the one named last changes fastest.
Arguments:
- features: bfloat16 [1024, 512, 256], P('gx', 'gy'), may hold values from -6 to 6
- occupied: int32 [1024, 512], P('gx', 'gy'), may hold values from 0 to 1, as said below
- voxel_order: int32 [128, 4096], P(('gx', 'gy')), may hold values from 0 to 4095, as said below
- conv_weight: bfloat16 [9, 256, 256], replicated, may hold values from -0.21875 to 0.21875
- cpe_linear: bfloat16 [256, 256], replicated, may hold values from -0.375 to 0.375
- qkv_weight: bfloat16 [256, 768], replicated
- proj_weight: bfloat16 [256, 256], replicated, may hold values from -0.375 to 0.375
- up_weight: bfloat16 [256, 1024], replicated, may hold values from -0.375 to 0.375
- down_weight: bfloat16 [1024, 256], replicated, may hold values from -0.1875 to 0.1875
Outputs:
- block_out: bfloat16 [262144, 256], P(('gx', 'gy'))
The draws below stay inside these ranges and needn't reach their ends.
Inputs may be any that keep to these rules, and one draw needn't show every extreme that they name: Each block holds from 1536 to 2560 occupied voxels, 2048 times 128 in all; for every p, the occupied voxels of the devices at curve positions below p number p * 2048 plus at most 256 in size either way, and exactly p * 2048 + 256 for some p. `voxel_order`: each row is a permutation of 0 to 4095 that follows a Hilbert curve through the block.
All inputs are finite; a program needn't handle non-finite values.
Results may differ from the reference program's by a relative error of at most 0.006.
Values may be sent and summed in bfloat16 or wider, within the bound.
A program may use at most 128 MiB of HBM per device.

```python
import math
import jax
import jax.numpy as jnp
from jax import lax

D = 256
HEADS = 8
HID = 1024
PATCH = 1024
SIDE = 64
LIVE = 2048
CAP = 256
HD = 32
NX = 1024
NY = 512
N_GX = 16
N_GY = 8
DEVICES = 128


def hilbert_points_drawn(side):
    index = jnp.arange(side * side, dtype=jnp.int32)
    coord_x = jnp.zeros((side * side,), jnp.int32)
    coord_y = jnp.zeros((side * side,), jnp.int32)
    remain = index
    level = 1
    while level < side:
        bit_x = remain // 2 % 2
        bit_y = jnp.bitwise_xor(remain, bit_x) % 2
        mirror = (bit_y == 0) & (bit_x == 1)
        moved_x = jnp.where(mirror, level - 1 - coord_x, coord_x)
        moved_y = jnp.where(mirror, level - 1 - coord_y, coord_y)
        turned = bit_y == 0
        coord_x = jnp.where(turned, moved_y, moved_x) + level * bit_x
        coord_y = jnp.where(turned, moved_x, moved_y) + level * bit_y
        remain = remain // 4
        level = level * 2
    return (coord_x, coord_y)


def curve_positions():
    square = N_GY * N_GY
    position = jnp.arange(DEVICES, dtype=jnp.int32)
    half = position // square
    inner_x, inner_y = hilbert_points_drawn(N_GY)
    along_x = inner_x[position % square] + half * N_GY
    along_y = inner_y[position % square]
    device = along_x * N_GY + along_y
    return jnp.zeros((DEVICES,), jnp.int32).at[device].set(position)


def draw_occupied(key, part):
    ranks = curve_positions()
    walk = jax.random.randint(jax.random.fold_in(key, 12), (DEVICES + 1,), -CAP, CAP + 1)
    peak = jax.random.randint(jax.random.fold_in(key, 13), (), 1, DEVICES)
    marker = jnp.arange(DEVICES + 1, dtype=jnp.int32)
    walk = jnp.where(marker == peak, CAP, walk)
    walk = jnp.where((marker == 0) | (marker == DEVICES), 0, walk)
    by_position = LIVE + walk[1:] - walk[:-1]
    counts = by_position[ranks]
    cells = SIDE * SIDE
    subkeys = jax.random.split(jax.random.fold_in(key, 14), DEVICES)
    shuffles = jax.vmap(lambda one: jax.random.permutation(one, cells))(subkeys)
    marks = (shuffles < counts[:, None]).astype(jnp.int32)
    return marks.reshape(N_GX, N_GY, SIDE, SIDE).transpose(0, 2, 1, 3).reshape(NX, NY)


def draw_voxel_order(key, part):
    coord_x, coord_y = hilbert_points_drawn(SIDE)
    flags = jax.random.randint(key, (DEVICES, 3), 0, 2)
    first = jnp.where(flags[:, 0:1] == 1, SIDE - 1 - coord_x[None, :], coord_x[None, :])
    second = jnp.where(flags[:, 1:2] == 1, SIDE - 1 - coord_y[None, :], coord_y[None, :])
    row_of = jnp.where(flags[:, 2:3] == 1, second, first)
    col_of = jnp.where(flags[:, 2:3] == 1, first, second)
    return (row_of * SIDE + col_of).astype(jnp.int32)


def draw_qkv_weight(key, part):
    values = jax.random.normal(key, (D, 3 * D), jnp.float32) * (1.0 / math.sqrt(D))
    return values.astype(jnp.bfloat16)


def level_of(stream_key, extent, pieces, least, high):
    loudness, own = 1.0, jax.random.fold_in(stream_key, 6)
    for dim, blocks in pieces:
        steps = jnp.exp(jax.random.uniform(jax.random.fold_in(own, dim), (blocks,), jnp.float32, least / len(pieces), high / len(pieces)))
        loudness = loudness * jnp.repeat(steps, extent[dim] // blocks).reshape([-1 if axis == dim else 1 for axis in range(len(extent))])
    return loudness


def centred(own_key, dims, scale, reach, cuts=(), held_as=jnp.bfloat16):
    factor_of = level_of(own_key, dims, cuts, -0.22, 0.18) if cuts else 1.0
    array = jax.random.normal(own_key, dims, jnp.float32) * scale * factor_of
    return jnp.minimum(jnp.maximum(array, -reach), reach).astype(held_as)


def setup_inputs(seed: int = 0) -> dict:
    keys = jax.random.split(jax.random.key(seed), 10)
    return {
        "features": centred(keys[0], (NX, NY, D), 1.0, 6.0, ((0, 16), (1, 8))),
        "occupied": draw_occupied(jax.random.fold_in(keys[9], 71), 0),
        "voxel_order": draw_voxel_order(jax.random.fold_in(keys[9], 71), 0),
        "conv_weight": centred(keys[3], (9, D, D), (3 * D) ** -0.5, 0.21875),
        "cpe_linear": centred(keys[4], (D, D), D ** -0.5, 0.375),
        "qkv_weight": draw_qkv_weight(jax.random.fold_in(keys[9], 71), 0),
        "proj_weight": centred(keys[6], (D, D), D ** -0.5, 0.375),
        "up_weight": centred(keys[7], (D, HID), D ** -0.5, 0.375),
        "down_weight": centred(keys[8], (HID, D), HID ** -0.5, 0.1875),
    }


def hilbert_points(side):
    index = jnp.arange(side * side, dtype=jnp.int32)
    coord_x = jnp.zeros((side * side,), jnp.int32)
    coord_y = jnp.zeros((side * side,), jnp.int32)
    remain = index
    level = 1
    while level < side:
        bit_x = remain // 2 % 2
        bit_y = jnp.bitwise_xor(remain, bit_x) % 2
        mirror = (bit_y == 0) & (bit_x == 1)
        moved_x = jnp.where(mirror, level - 1 - coord_x, coord_x)
        moved_y = jnp.where(mirror, level - 1 - coord_y, coord_y)
        turned = bit_y == 0
        coord_x = jnp.where(turned, moved_y, moved_x) + level * bit_x
        coord_y = jnp.where(turned, moved_x, moved_y) + level * bit_y
        remain = remain // 4
        level = level * 2
    return (coord_x, coord_y)

def block_curve(count_x, count_y):
    total = count_x * count_y
    square = count_y * count_y
    position = jnp.arange(total, dtype=jnp.int32)
    half = position // square
    inner_x, inner_y = hilbert_points(count_y)
    along_x = inner_x[position % square] + half * count_y
    along_y = inner_y[position % square]
    device = along_x * count_y + along_y
    return jnp.zeros((total,), jnp.int32).at[device].set(position)

def layer_norm(values):
    centre = values - lax.optimization_barrier(jnp.mean(values, axis=-1, keepdims=True))
    spread = lax.optimization_barrier(jnp.mean(centre * centre, axis=-1, keepdims=True))
    return centre * lax.rsqrt(spread + 1e-05)

def attend_patch(rows, qkv_weight, proj_weight, up_weight, down_weight):
    base = rows.astype(jnp.float32)
    normed = layer_norm(base).astype(jnp.bfloat16)
    projected = jnp.dot(normed, qkv_weight, preferred_element_type=jnp.float32).astype(jnp.bfloat16)
    width = rows.shape[1]
    count = rows.shape[0]
    query = projected[:, :width].reshape(count, HEADS, HD).astype(jnp.float32)
    keyset = projected[:, width:2 * width].reshape(count, HEADS, HD).astype(jnp.float32)
    valueset = projected[:, 2 * width:].reshape(count, HEADS, HD).astype(jnp.float32)
    scores = jnp.einsum('qhd,khd->hqk', query, keyset) * (1.0 / math.sqrt(HD))
    largest = lax.optimization_barrier(jnp.max(scores, axis=-1, keepdims=True))
    expo = jnp.exp(scores - largest)
    weights = (expo / lax.optimization_barrier(jnp.sum(expo, axis=-1, keepdims=True))).astype(jnp.bfloat16)
    attended = jnp.einsum('hqk,khd->qhd', weights.astype(jnp.float32), valueset).astype(jnp.bfloat16)
    middle = base + jnp.dot(attended.reshape(count, width), proj_weight, preferred_element_type=jnp.float32)
    second = layer_norm(middle).astype(jnp.bfloat16)
    hidden = jax.nn.gelu(jnp.dot(second, up_weight, preferred_element_type=jnp.float32), approximate=True).astype(jnp.bfloat16)
    final = middle + jnp.dot(hidden, down_weight, preferred_element_type=jnp.float32)
    return final.astype(jnp.bfloat16)

def reference(features, occupied, voxel_order, conv_weight, cpe_linear, qkv_weight, proj_weight, up_weight, down_weight):
    width = features.shape[2]
    masked = features * occupied[:, :, None].astype(jnp.bfloat16)
    padded = jnp.pad(masked, ((1, 1), (1, 1), (0, 0)))
    total = jnp.zeros((NX * NY, width), jnp.float32)
    for offset in range(9):
        step_x = offset // 3
        step_y = offset % 3
        window = padded[step_x:step_x + NX, step_y:step_y + NY].reshape(NX * NY, width)
        total = total + jnp.dot(window, conv_weight[offset], preferred_element_type=jnp.float32)
    conv = total.astype(jnp.bfloat16)
    linear = jnp.dot(conv, cpe_linear, preferred_element_type=jnp.float32)
    encoded = (features.reshape(NX * NY, width).astype(jnp.float32) + layer_norm(linear)).astype(jnp.bfloat16)
    blocks = encoded.reshape(N_GX, SIDE, N_GY, SIDE, width).transpose(0, 2, 1, 3, 4).reshape(DEVICES, SIDE * SIDE, width)
    marks = occupied.astype(jnp.int32).reshape(N_GX, SIDE, N_GY, SIDE).transpose(0, 2, 1, 3).reshape(DEVICES, SIDE * SIDE)
    order = voxel_order.astype(jnp.int32)
    ordered = jnp.take_along_axis(blocks, order[:, :, None], axis=1)
    live = jnp.take_along_axis(marks, order, axis=1)
    counts = lax.optimization_barrier(jnp.sum(live, axis=1, dtype=jnp.int32))
    ranks = block_curve(N_GX, N_GY)
    by_position = jnp.zeros((DEVICES,), jnp.int32).at[ranks].set(counts)
    starts = jnp.cumsum(by_position, dtype=jnp.int32) - by_position
    offsets = starts[ranks]
    local = jnp.cumsum(live, axis=1, dtype=jnp.int32) - 1
    target = jnp.where(live > 0, offsets[:, None] + local, DEVICES * LIVE).astype(jnp.int32)
    serial = jnp.zeros((DEVICES * LIVE, width), jnp.bfloat16).at[target.reshape(-1)].set(ordered.reshape(-1, width), mode='drop')
    owned = serial.reshape(DEVICES, LIVE, width)[ranks]
    patches = owned.reshape(DEVICES * LIVE // PATCH, PATCH, width)

    def one_patch(rows):
        return attend_patch(rows, qkv_weight, proj_weight, up_weight, down_weight)
    outputs = lax.map(one_patch, patches)
    return outputs.reshape(DEVICES * LIVE, width)
```

```python
import math

import jax
import jax.numpy as jnp
from jax import lax
from jax.experimental import pallas as pl
from jax.experimental.pallas import tpu as pltpu
from jax.sharding import PartitionSpec as P

HEADS = 8
PATCH = 1024
LIVE = 2048
CAP = 256
HD = 32


def with_halo(block, sides, width):
    for axis, dim in sides:
        count = lax.axis_size(axis)
        forward = [(i, i + 1) for i in range(count - 1)]
        backward = [(target, source) for source, target in forward]
        low = lax.ppermute(
            lax.slice_in_dim(block, block.shape[dim] - width, None, axis=dim), axis, forward
        )
        high = lax.ppermute(lax.slice_in_dim(block, 0, width, axis=dim), axis, backward)
        block = jnp.concatenate([low, block, high], axis=dim)
    return block


def passed_along(block, axis, distance):
    devices = range(lax.axis_size(axis))
    route = [(i - distance, i) for i in devices if i - distance in devices]
    return lax.ppermute(block, axis, route)


def hilbert_points(side):
    index = jnp.arange(side * side, dtype=jnp.int32)
    coord_x = jnp.zeros((side * side,), jnp.int32)
    coord_y = jnp.zeros((side * side,), jnp.int32)
    remain = index
    level = 1
    while level < side:
        bit_x = remain // 2 % 2
        bit_y = jnp.bitwise_xor(remain, bit_x) % 2
        mirror = (bit_y == 0) & (bit_x == 1)
        moved_x = jnp.where(mirror, level - 1 - coord_x, coord_x)
        moved_y = jnp.where(mirror, level - 1 - coord_y, coord_y)
        turned = bit_y == 0
        coord_x = jnp.where(turned, moved_y, moved_x) + level * bit_x
        coord_y = jnp.where(turned, moved_x, moved_y) + level * bit_y
        remain = remain // 4
        level = level * 2
    return (coord_x, coord_y)


def block_curve(count_x, count_y):
    total = count_x * count_y
    square = count_y * count_y
    position = jnp.arange(total, dtype=jnp.int32)
    half = position // square
    inner_x, inner_y = hilbert_points(count_y)
    along_x = inner_x[position % square] + half * count_y
    along_y = inner_y[position % square]
    device = along_x * count_y + along_y
    return jnp.zeros((total,), jnp.int32).at[device].set(position)


def layer_norm(values):
    centre = values - jnp.mean(values, axis=-1, keepdims=True)
    spread = jnp.mean(centre * centre, axis=-1, keepdims=True)
    return centre * lax.rsqrt(spread + 1e-05)


def attend_patch(rows, qkv_weight, proj_weight, up_weight, down_weight):
    base = rows.astype(jnp.float32)
    normed = layer_norm(base).astype(jnp.bfloat16)
    projected = jnp.dot(normed, qkv_weight, preferred_element_type=jnp.float32).astype(jnp.bfloat16)
    width = rows.shape[1]
    count = rows.shape[0]
    query = projected[:, :width].reshape(count, HEADS, HD)
    keyset = projected[:, width : 2 * width].reshape(count, HEADS, HD)
    valueset = projected[:, 2 * width :].reshape(count, HEADS, HD)
    scores = jnp.einsum("qhd,khd->hqk", query, keyset, preferred_element_type=jnp.float32) * (
        1.0 / math.sqrt(HD)
    )
    largest = jnp.max(scores, axis=-1, keepdims=True)
    expo = jnp.exp(scores - largest)
    weights = (expo / jnp.sum(expo, axis=-1, keepdims=True)).astype(jnp.bfloat16)
    attended = jnp.einsum(
        "hqk,khd->qhd", weights, valueset, preferred_element_type=jnp.float32
    ).astype(jnp.bfloat16)
    middle = base + jnp.dot(
        attended.reshape(count, width), proj_weight, preferred_element_type=jnp.float32
    )
    second = layer_norm(middle).astype(jnp.bfloat16)
    hidden = jax.nn.gelu(
        jnp.dot(second, up_weight, preferred_element_type=jnp.float32), approximate=True
    ).astype(jnp.bfloat16)
    final = middle + jnp.dot(hidden, down_weight, preferred_element_type=jnp.float32)
    return final.astype(jnp.bfloat16)


def onehot_gather_kernel(index_ref, table_ref, out_ref, acc_ref):
    rows = index_ref.shape[0]
    chunk = 512
    wanted = index_ref[...]
    acc_ref[...] = jnp.zeros_like(acc_ref)
    for part in range(table_ref.shape[0] // chunk):
        ids = lax.broadcasted_iota(jnp.int32, (rows, chunk), 1) + part * chunk
        pick = jnp.where(wanted == ids, 1.0, 0.0).astype(jnp.bfloat16)
        acc_ref[...] += jnp.dot(
            pick, table_ref[pl.ds(part * chunk, chunk), :], preferred_element_type=jnp.float32
        )
    out_ref[...] = acc_ref[...].astype(out_ref.dtype)


def onehot_gather(table, index):
    count = index.shape[0]
    width = table.shape[1]
    tile = 256
    return pl.pallas_call(
        onehot_gather_kernel,
        grid=(count // tile,),
        in_specs=[
            pl.BlockSpec((tile, 1), lambda i: (i, 0)),
            pl.BlockSpec(table.shape, lambda i: (0, 0)),
        ],
        out_specs=pl.BlockSpec((tile, width), lambda i: (i, 0)),
        out_shape=jax.ShapeDtypeStruct((count, width), table.dtype),
        scratch_shapes=[pltpu.VMEM((tile, width), jnp.float32)],
    )(index.reshape(count, 1), table)


def shards(
    features,
    occupied,
    voxel_order,
    conv_weight,
    cpe_linear,
    qkv_weight,
    proj_weight,
    up_weight,
    down_weight,
):
    span_x, span_y, width = features.shape
    cells = span_x * span_y
    occ_flat = occupied.reshape(cells)
    mine = jnp.sum(occ_flat, dtype=jnp.int32)
    counts = lax.all_gather(
        mine.astype(jnp.float32).reshape(1), ("gx", "gy"), axis=0, tiled=True
    ).astype(jnp.int32)
    masked = features * occupied[:, :, None].astype(jnp.bfloat16)
    padded = with_halo(masked, (("gx", 0), ("gy", 1)), 1)
    total = jnp.zeros((cells, width), jnp.float32)
    for offset in range(9):
        step_x = offset // 3
        step_y = offset % 3
        window = padded[step_x : step_x + span_x, step_y : step_y + span_y].reshape(cells, width)
        total = total + jnp.dot(window, conv_weight[offset], preferred_element_type=jnp.float32)
    conv = total.astype(jnp.bfloat16)
    linear = jnp.dot(conv, cpe_linear, preferred_element_type=jnp.float32)
    encoded = (features.reshape(cells, width).astype(jnp.float32) + layer_norm(linear)).astype(
        jnp.bfloat16
    )
    order = voxel_order[0]
    voxel = jnp.arange(cells, dtype=jnp.int32)
    _, rank_of = lax.sort_key_val(order, voxel)
    key = (1 - occ_flat) * cells + rank_of
    _, listed_voxel = lax.sort_key_val(key, voxel)
    devices = counts.shape[0]
    count_x = lax.axis_size("gx")
    count_y = lax.axis_size("gy")
    here_x = lax.axis_index("gx")
    here_y = lax.axis_index("gy")
    ranks = block_curve(count_x, count_y)
    position = ranks[here_x * count_y + here_y]
    by_position = jnp.zeros((devices,), jnp.int32).at[ranks].set(counts)
    starts = jnp.cumsum(by_position, dtype=jnp.int32) - by_position
    start_here = starts[position]
    excess = start_here - position * LIVE
    beyond = start_here + mine - (position + 1) * LIVE
    capacity = CAP
    slot = jnp.arange(capacity, dtype=jnp.int32)
    row = jnp.arange(LIVE, dtype=jnp.int32)
    own_item = row - excess
    own_ok = (own_item >= 0) & (own_item < mine)
    prev_item = slot
    prev_ok = slot < -excess
    next_item = LIVE - excess + slot
    next_ok = slot < beyond
    items = jnp.concatenate([own_item, prev_item, next_item])
    ok = jnp.concatenate([own_ok, prev_ok, next_ok])
    picked = jnp.where(ok, listed_voxel[jnp.clip(items, 0, cells - 1)], -1)
    gathered = onehot_gather(encoded, picked)
    mine_rows = gathered[:LIVE]
    to_prev = gathered[LIVE : LIVE + capacity]
    to_next = gathered[LIVE + capacity :]
    empty = jnp.zeros((capacity, width), jnp.bfloat16)
    device_of = jnp.zeros((devices,), jnp.int32).at[ranks].set(jnp.arange(devices, dtype=jnp.int32))
    prev_device = device_of[jnp.maximum(position - 1, 0)]
    next_device = device_of[jnp.minimum(position + 1, devices - 1)]
    prev_x = prev_device // count_y
    prev_y = prev_device % count_y
    next_x = next_device // count_y
    next_y = next_device % count_y
    from_prev = empty
    from_next = empty

    def outgoing(target_x, target_y):
        toward_next = (next_x == target_x) & (next_y == target_y)
        toward_prev = (prev_x == target_x) & (prev_y == target_y)
        return jnp.where(toward_next, to_next, jnp.where(toward_prev, to_prev, empty))

    for step in (1, -1):
        got = passed_along(outgoing(here_x + step, here_y), "gx", step)
        source_x = here_x - step
        from_prev = jnp.where((prev_x == source_x) & (prev_y == here_y), got, from_prev)
        from_next = jnp.where((next_x == source_x) & (next_y == here_y), got, from_next)
    for step in (1, -1):
        got = passed_along(outgoing(here_x, here_y + step), "gy", step)
        source_y = here_y - step
        from_prev = jnp.where((prev_x == here_x) & (prev_y == source_y), got, from_prev)
        from_next = jnp.where((next_x == here_x) & (next_y == source_y), got, from_next)
    from_prev = jnp.where((slot < excess)[:, None], from_prev, empty)
    from_next = jnp.where((slot < -beyond)[:, None], from_next, empty)
    leading = jnp.concatenate(
        [from_prev, jnp.zeros((LIVE - capacity, width), jnp.bfloat16)], axis=0
    )
    trailing = lax.dynamic_slice_in_dim(
        jnp.concatenate([jnp.zeros((LIVE, width), jnp.bfloat16), from_next], axis=0),
        -beyond,
        LIVE,
        0,
    )
    owned = mine_rows + leading + trailing
    patches = owned.reshape(LIVE // PATCH, PATCH, width)

    def one_patch(rows):
        return attend_patch(rows, qkv_weight, proj_weight, up_weight, down_weight)

    outputs = lax.map(one_patch, patches)
    return outputs.reshape(LIVE, width)


def solution(mesh):
    return jax.shard_map(
        shards,
        mesh=mesh,
        in_specs=(
            P("gx", "gy", None),
            P("gx", "gy"),
            P(("gx", "gy"), None),
            P(),
            P(),
            P(),
            P(),
            P(),
            P(),
        ),
        out_specs=P(("gx", "gy"), None),
        check_vma=False,
    )
```

```python
import functools
import math

import jax
import jax.numpy as jnp
from jax import lax
from jax.experimental import pallas as pl
from jax.experimental.pallas import tpu as pltpu
from jax.sharding import PartitionSpec as P

HEADS = 8
PATCH = 1024
LIVE = 2048
CAP = 256
HD = 32


def with_halo(block, sides, width):
    for axis, dim in sides:
        count = lax.axis_size(axis)
        forward = [(i, i + 1) for i in range(count - 1)]
        backward = [(target, source) for source, target in forward]
        low = lax.ppermute(
            lax.slice_in_dim(block, block.shape[dim] - width, None, axis=dim), axis, forward
        )
        high = lax.ppermute(lax.slice_in_dim(block, 0, width, axis=dim), axis, backward)
        block = jnp.concatenate([low, block, high], axis=dim)
    return block


def passed_along(block, axis, distance):
    devices = range(lax.axis_size(axis))
    route = [(i - distance, i) for i in devices if i - distance in devices]
    return lax.ppermute(block, axis, route)


def hilbert_points(side):
    index = jnp.arange(side * side, dtype=jnp.int32)
    coord_x = jnp.zeros((side * side,), jnp.int32)
    coord_y = jnp.zeros((side * side,), jnp.int32)
    remain = index
    level = 1
    while level < side:
        bit_x = remain // 2 % 2
        bit_y = jnp.bitwise_xor(remain, bit_x) % 2
        mirror = (bit_y == 0) & (bit_x == 1)
        moved_x = jnp.where(mirror, level - 1 - coord_x, coord_x)
        moved_y = jnp.where(mirror, level - 1 - coord_y, coord_y)
        turned = bit_y == 0
        coord_x = jnp.where(turned, moved_y, moved_x) + level * bit_x
        coord_y = jnp.where(turned, moved_x, moved_y) + level * bit_y
        remain = remain // 4
        level = level * 2
    return (coord_x, coord_y)


def block_curve(count_x, count_y):
    total = count_x * count_y
    square = count_y * count_y
    position = jnp.arange(total, dtype=jnp.int32)
    half = position // square
    inner_x, inner_y = hilbert_points(count_y)
    along_x = inner_x[position % square] + half * count_y
    along_y = inner_y[position % square]
    device = along_x * count_y + along_y
    return jnp.zeros((total,), jnp.int32).at[device].set(position)


def layer_norm(values):
    centre = values - jnp.mean(values, axis=-1, keepdims=True)
    spread = jnp.mean(centre * centre, axis=-1, keepdims=True)
    return centre * lax.rsqrt(spread + 1e-05)


def attend_patch(rows, qkv_weight, proj_weight, up_weight, down_weight):
    base = rows.astype(jnp.float32)
    normed = layer_norm(base).astype(jnp.bfloat16)
    projected = jnp.dot(normed, qkv_weight, preferred_element_type=jnp.float32).astype(jnp.bfloat16)
    width = rows.shape[1]
    count = rows.shape[0]
    query = projected[:, :width].reshape(count, HEADS, HD)
    keyset = projected[:, width : 2 * width].reshape(count, HEADS, HD)
    valueset = projected[:, 2 * width :].reshape(count, HEADS, HD)
    scores = jnp.einsum("qhd,khd->hqk", query, keyset, preferred_element_type=jnp.float32) * (
        1.0 / math.sqrt(HD)
    )
    largest = jnp.max(scores, axis=-1, keepdims=True)
    expo = jnp.exp(scores - largest)
    weights = (expo / jnp.sum(expo, axis=-1, keepdims=True)).astype(jnp.bfloat16)
    attended = jnp.einsum(
        "hqk,khd->qhd", weights, valueset, preferred_element_type=jnp.float32
    ).astype(jnp.bfloat16)
    middle = base + jnp.dot(
        attended.reshape(count, width), proj_weight, preferred_element_type=jnp.float32
    )
    second = layer_norm(middle).astype(jnp.bfloat16)
    hidden = jax.nn.gelu(
        jnp.dot(second, up_weight, preferred_element_type=jnp.float32), approximate=True
    ).astype(jnp.bfloat16)
    final = middle + jnp.dot(hidden, down_weight, preferred_element_type=jnp.float32)
    return final.astype(jnp.bfloat16)


def onehot_gather_kernel(index_ref, table_ref, out_ref, acc_ref):
    rows = index_ref.shape[0]
    chunk = 512
    wanted = index_ref[...]
    acc_ref[...] = jnp.zeros_like(acc_ref)
    for part in range(table_ref.shape[0] // chunk):
        ids = lax.broadcasted_iota(jnp.int32, (rows, chunk), 1) + part * chunk
        pick = jnp.where(wanted == ids, 1.0, 0.0).astype(jnp.bfloat16)
        acc_ref[...] += jnp.dot(
            pick, table_ref[pl.ds(part * chunk, chunk), :], preferred_element_type=jnp.float32
        )
    out_ref[...] = acc_ref[...].astype(out_ref.dtype)


def onehot_gather(table, index):
    count = index.shape[0]
    width = table.shape[1]
    tile = 256
    return pl.pallas_call(
        onehot_gather_kernel,
        grid=(count // tile,),
        in_specs=[
            pl.BlockSpec((tile, 1), lambda i: (i, 0)),
            pl.BlockSpec(table.shape, lambda i: (0, 0)),
        ],
        out_specs=pl.BlockSpec((tile, width), lambda i: (i, 0)),
        out_shape=jax.ShapeDtypeStruct((count, width), table.dtype),
        scratch_shapes=[pltpu.VMEM((tile, width), jnp.float32)],
    )(index.reshape(count, 1), table)


MESH = pl.DeviceIdType.MESH


def count_gather_kernel(nx, ny, mine_ref, out_ref, row_buf, grid_buf, send1, recv1, send2, recv2, own_sem):
    me_x = lax.axis_index("gx")
    me_y = lax.axis_index("gy")
    barrier = pltpu.get_barrier_semaphore()
    for k in range(1, ny):
        pl.semaphore_signal(
            barrier, inc=1, device_id=(me_x, lax.rem(me_y + k, ny)), device_id_type=MESH
        )
    for k in range(1, nx):
        pl.semaphore_signal(
            barrier, inc=1, device_id=(lax.rem(me_x + k, nx), me_y), device_id_type=MESH
        )
    pl.semaphore_wait(barrier, nx + ny - 2)

    own = pltpu.make_async_copy(mine_ref, row_buf.at[pl.ds(me_y, 1)], own_sem.at[0])
    own.start()
    for k in range(1, ny):
        pltpu.make_async_remote_copy(
            src_ref=mine_ref,
            dst_ref=row_buf.at[pl.ds(me_y, 1)],
            send_sem=send1.at[k],
            recv_sem=recv1.at[k],
            device_id=(me_x, lax.rem(me_y + k, ny)),
            device_id_type=MESH,
        ).start()
    own.wait()
    for k in range(1, ny):
        sender = lax.rem(me_y - k + ny, ny)
        copy = pltpu.make_async_remote_copy(
            src_ref=mine_ref,
            dst_ref=row_buf.at[pl.ds(sender, 1)],
            send_sem=send1.at[k],
            recv_sem=recv1.at[k],
            device_id=(me_x, sender),
            device_id_type=MESH,
        )
        copy.wait_send()
        copy.wait_recv()

    own = pltpu.make_async_copy(row_buf, grid_buf.at[me_x], own_sem.at[1])
    own.start()
    for k in range(1, nx):
        pltpu.make_async_remote_copy(
            src_ref=row_buf,
            dst_ref=grid_buf.at[me_x],
            send_sem=send2.at[k],
            recv_sem=recv2.at[k],
            device_id=(lax.rem(me_x + k, nx), me_y),
            device_id_type=MESH,
        ).start()
    own.wait()
    for k in range(1, nx):
        sender = lax.rem(me_x - k + nx, nx)
        copy = pltpu.make_async_remote_copy(
            src_ref=row_buf,
            dst_ref=grid_buf.at[sender],
            send_sem=send2.at[k],
            recv_sem=recv2.at[k],
            device_id=(sender, me_y),
            device_id_type=MESH,
        )
        copy.wait_send()
        copy.wait_recv()
    out_ref[...] = grid_buf[...]


def gather_counts(mine):
    nx = lax.axis_size("gx")
    ny = lax.axis_size("gy")
    lanes = 128
    grid = pl.pallas_call(
        functools.partial(count_gather_kernel, nx, ny),
        out_shape=jax.ShapeDtypeStruct((nx, ny, lanes), jnp.int32),
        in_specs=[pl.BlockSpec(memory_space=pltpu.VMEM)],
        out_specs=pl.BlockSpec(memory_space=pltpu.VMEM),
        scratch_shapes=[
            pltpu.VMEM((ny, lanes), jnp.int32),
            pltpu.VMEM((nx, ny, lanes), jnp.int32),
            pltpu.SemaphoreType.DMA((ny,)),
            pltpu.SemaphoreType.DMA((ny,)),
            pltpu.SemaphoreType.DMA((nx,)),
            pltpu.SemaphoreType.DMA((nx,)),
            pltpu.SemaphoreType.DMA((2,)),
        ],
        compiler_params=pltpu.CompilerParams(collective_id=0, has_side_effects=True),
    )(jnp.broadcast_to(mine, (1, lanes)))
    return grid[:, :, 0].reshape(nx * ny)


def shards(
    features,
    occupied,
    voxel_order,
    conv_weight,
    cpe_linear,
    qkv_weight,
    proj_weight,
    up_weight,
    down_weight,
):
    span_x, span_y, width = features.shape
    cells = span_x * span_y
    occ_flat = occupied.reshape(cells)
    mine = jnp.sum(occ_flat, dtype=jnp.int32)
    counts = gather_counts(mine)
    masked = features * occupied[:, :, None].astype(jnp.bfloat16)
    padded = with_halo(masked, (("gx", 0), ("gy", 1)), 1)
    total = jnp.zeros((cells, width), jnp.float32)
    for offset in range(9):
        step_x = offset // 3
        step_y = offset % 3
        window = padded[step_x : step_x + span_x, step_y : step_y + span_y].reshape(cells, width)
        total = total + jnp.dot(window, conv_weight[offset], preferred_element_type=jnp.float32)
    conv = total.astype(jnp.bfloat16)
    linear = jnp.dot(conv, cpe_linear, preferred_element_type=jnp.float32)
    encoded = (features.reshape(cells, width).astype(jnp.float32) + layer_norm(linear)).astype(
        jnp.bfloat16
    )
    order = voxel_order[0]
    voxel = jnp.arange(cells, dtype=jnp.int32)
    _, rank_of = lax.sort_key_val(order, voxel)
    key = (1 - occ_flat) * cells + rank_of
    _, listed_voxel = lax.sort_key_val(key, voxel)
    devices = counts.shape[0]
    count_x = lax.axis_size("gx")
    count_y = lax.axis_size("gy")
    here_x = lax.axis_index("gx")
    here_y = lax.axis_index("gy")
    ranks = block_curve(count_x, count_y)
    position = ranks[here_x * count_y + here_y]
    by_position = jnp.zeros((devices,), jnp.int32).at[ranks].set(counts)
    starts = jnp.cumsum(by_position, dtype=jnp.int32) - by_position
    start_here = starts[position]
    excess = start_here - position * LIVE
    beyond = start_here + mine - (position + 1) * LIVE
    capacity = CAP
    slot = jnp.arange(capacity, dtype=jnp.int32)
    row = jnp.arange(LIVE, dtype=jnp.int32)
    own_item = row - excess
    own_ok = (own_item >= 0) & (own_item < mine)
    prev_ok = slot < -excess
    next_ok = slot < beyond
    spare = jnp.zeros((capacity,), jnp.int32)
    extended = jnp.concatenate([spare, listed_voxel, spare])
    own_src = lax.dynamic_slice_in_dim(extended, capacity - excess, LIVE, 0)
    next_src = lax.dynamic_slice_in_dim(listed_voxel, LIVE - excess, capacity, 0)
    items = jnp.concatenate([own_src, listed_voxel[:capacity], next_src])
    ok = jnp.concatenate([own_ok, prev_ok, next_ok])
    picked = jnp.where(ok, items, -1)
    gathered = onehot_gather(encoded, picked)
    mine_rows = gathered[:LIVE]
    to_prev = gathered[LIVE : LIVE + capacity]
    to_next = gathered[LIVE + capacity :]
    empty = jnp.zeros((capacity, width), jnp.bfloat16)
    device_of = jnp.zeros((devices,), jnp.int32).at[ranks].set(jnp.arange(devices, dtype=jnp.int32))
    prev_device = device_of[jnp.maximum(position - 1, 0)]
    next_device = device_of[jnp.minimum(position + 1, devices - 1)]
    prev_x = prev_device // count_y
    prev_y = prev_device % count_y
    next_x = next_device // count_y
    next_y = next_device % count_y
    from_prev = empty
    from_next = empty

    def outgoing(target_x, target_y):
        toward_next = (next_x == target_x) & (next_y == target_y)
        toward_prev = (prev_x == target_x) & (prev_y == target_y)
        return jnp.where(toward_next, to_next, jnp.where(toward_prev, to_prev, empty))

    for step in (1, -1):
        got = passed_along(outgoing(here_x + step, here_y), "gx", step)
        source_x = here_x - step
        from_prev = jnp.where((prev_x == source_x) & (prev_y == here_y), got, from_prev)
        from_next = jnp.where((next_x == source_x) & (next_y == here_y), got, from_next)
    for step in (1, -1):
        got = passed_along(outgoing(here_x, here_y + step), "gy", step)
        source_y = here_y - step
        from_prev = jnp.where((prev_x == here_x) & (prev_y == source_y), got, from_prev)
        from_next = jnp.where((next_x == here_x) & (next_y == source_y), got, from_next)
    from_prev = jnp.where((slot < excess)[:, None], from_prev, empty)
    from_next = jnp.where((slot < -beyond)[:, None], from_next, empty)
    leading = jnp.concatenate(
        [from_prev, jnp.zeros((LIVE - capacity, width), jnp.bfloat16)], axis=0
    )
    trailing = lax.dynamic_slice_in_dim(
        jnp.concatenate([jnp.zeros((LIVE, width), jnp.bfloat16), from_next], axis=0),
        -beyond,
        LIVE,
        0,
    )
    owned = mine_rows + leading + trailing
    patches = owned.reshape(LIVE // PATCH, PATCH, width)

    def one_patch(rows):
        return attend_patch(rows, qkv_weight, proj_weight, up_weight, down_weight)

    outputs = lax.map(one_patch, patches)
    return outputs.reshape(LIVE, width)


def solution(mesh):
    return jax.shard_map(
        shards,
        mesh=mesh,
        in_specs=(
            P("gx", "gy", None),
            P("gx", "gy"),
            P(("gx", "gy"), None),
            P(),
            P(),
            P(),
            P(),
            P(),
            P(),
        ),
        out_specs=P(("gx", "gy"), None),
        check_vma=False,
    )
```

```python
import functools
import math

import jax
import jax.numpy as jnp
from jax import lax
from jax.experimental import pallas as pl
from jax.experimental.pallas import tpu as pltpu
from jax.sharding import PartitionSpec as P

HEADS = 8
PATCH = 1024
LIVE = 2048
CAP = 256
HD = 32


def with_halo(block, sides, width):
    for axis, dim in sides:
        count = lax.axis_size(axis)
        forward = [(i, i + 1) for i in range(count - 1)]
        backward = [(target, source) for source, target in forward]
        low = lax.ppermute(
            lax.slice_in_dim(block, block.shape[dim] - width, None, axis=dim), axis, forward
        )
        high = lax.ppermute(lax.slice_in_dim(block, 0, width, axis=dim), axis, backward)
        block = jnp.concatenate([low, block, high], axis=dim)
    return block


def passed_along(block, axis, distance):
    devices = range(lax.axis_size(axis))
    route = [(i - distance, i) for i in devices if i - distance in devices]
    return lax.ppermute(block, axis, route)


def hilbert_points(side):
    index = jnp.arange(side * side, dtype=jnp.int32)
    coord_x = jnp.zeros((side * side,), jnp.int32)
    coord_y = jnp.zeros((side * side,), jnp.int32)
    remain = index
    level = 1
    while level < side:
        bit_x = remain // 2 % 2
        bit_y = jnp.bitwise_xor(remain, bit_x) % 2
        mirror = (bit_y == 0) & (bit_x == 1)
        moved_x = jnp.where(mirror, level - 1 - coord_x, coord_x)
        moved_y = jnp.where(mirror, level - 1 - coord_y, coord_y)
        turned = bit_y == 0
        coord_x = jnp.where(turned, moved_y, moved_x) + level * bit_x
        coord_y = jnp.where(turned, moved_x, moved_y) + level * bit_y
        remain = remain // 4
        level = level * 2
    return (coord_x, coord_y)


def block_curve(count_x, count_y):
    total = count_x * count_y
    square = count_y * count_y
    position = jnp.arange(total, dtype=jnp.int32)
    half = position // square
    inner_x, inner_y = hilbert_points(count_y)
    along_x = inner_x[position % square] + half * count_y
    along_y = inner_y[position % square]
    device = along_x * count_y + along_y
    return jnp.zeros((total,), jnp.int32).at[device].set(position)


def layer_norm(values):
    centre = values - jnp.mean(values, axis=-1, keepdims=True)
    spread = jnp.mean(centre * centre, axis=-1, keepdims=True)
    return centre * lax.rsqrt(spread + 1e-05)


def attend_patch(rows, qkv_weight, proj_weight, up_weight, down_weight):
    base = rows.astype(jnp.float32)
    normed = layer_norm(base).astype(jnp.bfloat16)
    projected = jnp.dot(normed, qkv_weight, preferred_element_type=jnp.float32).astype(jnp.bfloat16)
    width = rows.shape[1]
    count = rows.shape[0]
    query = projected[:, :width].reshape(count, HEADS, HD)
    keyset = projected[:, width : 2 * width].reshape(count, HEADS, HD)
    valueset = projected[:, 2 * width :].reshape(count, HEADS, HD)
    scores = jnp.einsum("qhd,khd->hqk", query, keyset, preferred_element_type=jnp.float32) * (
        1.0 / math.sqrt(HD)
    )
    largest = jnp.max(scores, axis=-1, keepdims=True)
    expo = jnp.exp(scores - largest)
    weights = (expo / jnp.sum(expo, axis=-1, keepdims=True)).astype(jnp.bfloat16)
    attended = jnp.einsum(
        "hqk,khd->qhd", weights, valueset, preferred_element_type=jnp.float32
    ).astype(jnp.bfloat16)
    middle = base + jnp.dot(
        attended.reshape(count, width), proj_weight, preferred_element_type=jnp.float32
    )
    second = layer_norm(middle).astype(jnp.bfloat16)
    hidden = jax.nn.gelu(
        jnp.dot(second, up_weight, preferred_element_type=jnp.float32), approximate=True
    ).astype(jnp.bfloat16)
    final = middle + jnp.dot(hidden, down_weight, preferred_element_type=jnp.float32)
    return final.astype(jnp.bfloat16)


def onehot_gather_kernel(index_ref, table_ref, out_ref, acc_ref):
    rows = index_ref.shape[0]
    chunk = 512
    wanted = index_ref[...]
    acc_ref[...] = jnp.zeros_like(acc_ref)
    for part in range(table_ref.shape[0] // chunk):
        ids = lax.broadcasted_iota(jnp.int32, (rows, chunk), 1) + part * chunk
        pick = jnp.where(wanted == ids, 1.0, 0.0).astype(jnp.bfloat16)
        acc_ref[...] += jnp.dot(
            pick, table_ref[pl.ds(part * chunk, chunk), :], preferred_element_type=jnp.float32
        )
    out_ref[...] = acc_ref[...].astype(out_ref.dtype)


def onehot_gather(table, index):
    count = index.shape[0]
    width = table.shape[1]
    tile = 256
    return pl.pallas_call(
        onehot_gather_kernel,
        grid=(count // tile,),
        in_specs=[
            pl.BlockSpec((tile, 1), lambda i: (i, 0)),
            pl.BlockSpec(table.shape, lambda i: (0, 0)),
        ],
        out_specs=pl.BlockSpec((tile, width), lambda i: (i, 0)),
        out_shape=jax.ShapeDtypeStruct((count, width), table.dtype),
        scratch_shapes=[pltpu.VMEM((tile, width), jnp.float32)],
    )(index.reshape(count, 1), table)


MESH = pl.DeviceIdType.MESH


def count_gather_kernel(nx, ny, mine_ref, out_ref, row_buf, grid_buf, send1, recv1, send2, recv2, own_sem):
    me_x = lax.axis_index("gx")
    me_y = lax.axis_index("gy")
    barrier = pltpu.get_barrier_semaphore()
    for k in range(1, ny):
        pl.semaphore_signal(
            barrier, inc=1, device_id=(me_x, lax.rem(me_y + k, ny)), device_id_type=MESH
        )
    for k in range(1, nx):
        pl.semaphore_signal(
            barrier, inc=1, device_id=(lax.rem(me_x + k, nx), me_y), device_id_type=MESH
        )
    pl.semaphore_wait(barrier, nx + ny - 2)

    own = pltpu.make_async_copy(mine_ref, row_buf.at[pl.ds(me_y, 1)], own_sem.at[0])
    own.start()
    for k in range(1, ny):
        pltpu.make_async_remote_copy(
            src_ref=mine_ref,
            dst_ref=row_buf.at[pl.ds(me_y, 1)],
            send_sem=send1.at[k],
            recv_sem=recv1.at[k],
            device_id=(me_x, lax.rem(me_y + k, ny)),
            device_id_type=MESH,
        ).start()
    own.wait()
    for k in range(1, ny):
        sender = lax.rem(me_y - k + ny, ny)
        copy = pltpu.make_async_remote_copy(
            src_ref=mine_ref,
            dst_ref=row_buf.at[pl.ds(sender, 1)],
            send_sem=send1.at[k],
            recv_sem=recv1.at[k],
            device_id=(me_x, sender),
            device_id_type=MESH,
        )
        copy.wait_send()
        copy.wait_recv()

    own = pltpu.make_async_copy(row_buf, grid_buf.at[me_x], own_sem.at[1])
    own.start()
    for k in range(1, nx):
        pltpu.make_async_remote_copy(
            src_ref=row_buf,
            dst_ref=grid_buf.at[me_x],
            send_sem=send2.at[k],
            recv_sem=recv2.at[k],
            device_id=(lax.rem(me_x + k, nx), me_y),
            device_id_type=MESH,
        ).start()
    own.wait()
    for k in range(1, nx):
        sender = lax.rem(me_x - k + nx, nx)
        copy = pltpu.make_async_remote_copy(
            src_ref=row_buf,
            dst_ref=grid_buf.at[sender],
            send_sem=send2.at[k],
            recv_sem=recv2.at[k],
            device_id=(sender, me_y),
            device_id_type=MESH,
        )
        copy.wait_send()
        copy.wait_recv()
    out_ref[...] = grid_buf[...]


def gather_counts(mine):
    nx = lax.axis_size("gx")
    ny = lax.axis_size("gy")
    lanes = 128
    grid = pl.pallas_call(
        functools.partial(count_gather_kernel, nx, ny),
        out_shape=jax.ShapeDtypeStruct((nx, ny, lanes), jnp.int32),
        in_specs=[pl.BlockSpec(memory_space=pltpu.VMEM)],
        out_specs=pl.BlockSpec(memory_space=pltpu.VMEM),
        scratch_shapes=[
            pltpu.VMEM((ny, lanes), jnp.int32),
            pltpu.VMEM((nx, ny, lanes), jnp.int32),
            pltpu.SemaphoreType.DMA((ny,)),
            pltpu.SemaphoreType.DMA((ny,)),
            pltpu.SemaphoreType.DMA((nx,)),
            pltpu.SemaphoreType.DMA((nx,)),
            pltpu.SemaphoreType.DMA((2,)),
        ],
        compiler_params=pltpu.CompilerParams(collective_id=0, has_side_effects=True),
    )(jnp.broadcast_to(mine, (1, lanes)))
    return grid[:, :, 0].reshape(nx * ny)


def attention_kernel(q_ref, k_ref, v_ref, base_ref, proj_ref, out_ref):
    head = pl.program_id(2)

    @pl.when(head == 0)
    def _():
        out_ref[...] = base_ref[...].astype(jnp.float32)

    query = q_ref[0, 0]
    keyset = k_ref[0, 0]
    scores = lax.dot_general(
        query, keyset, (((1,), (1,)), ((), ())), preferred_element_type=jnp.float32
    ) * (1.0 / math.sqrt(HD))
    largest = jnp.max(scores, axis=-1, keepdims=True)
    expo = jnp.exp(scores - largest)
    weights = (expo * (1.0 / jnp.sum(expo, axis=-1, keepdims=True))).astype(jnp.bfloat16)
    attended = jnp.dot(weights, v_ref[0, 0], preferred_element_type=jnp.float32).astype(
        jnp.bfloat16
    )
    out_ref[...] += jnp.dot(attended, proj_ref[0], preferred_element_type=jnp.float32)


def attention_mid(rows, qkv_weight, proj_weight):
    count, width = rows.shape
    base = rows.astype(jnp.float32)
    normed = layer_norm(base).astype(jnp.bfloat16)
    projected = jnp.dot(normed, qkv_weight, preferred_element_type=jnp.float32).astype(jnp.bfloat16)
    heads = projected.reshape(count, 3, HEADS, HD).transpose(1, 2, 0, 3)
    tile = 256
    tiles = PATCH // tile
    grid = (count // PATCH, tiles, HEADS)
    return pl.pallas_call(
        attention_kernel,
        grid=grid,
        in_specs=[
            pl.BlockSpec((1, 1, tile, HD), lambda p, t, h: (0, h, p * tiles + t, 0)),
            pl.BlockSpec((1, 1, PATCH, HD), lambda p, t, h: (1, h, p, 0)),
            pl.BlockSpec((1, 1, PATCH, HD), lambda p, t, h: (2, h, p, 0)),
            pl.BlockSpec((tile, width), lambda p, t, h: (p * tiles + t, 0)),
            pl.BlockSpec((1, HD, width), lambda p, t, h: (h, 0, 0)),
        ],
        out_specs=pl.BlockSpec((tile, width), lambda p, t, h: (p * tiles + t, 0)),
        out_shape=jax.ShapeDtypeStruct((count, width), jnp.float32),
    )(heads, heads, heads, rows, proj_weight.reshape(HEADS, HD, width))


def feed_forward(middle, up_weight, down_weight):
    second = layer_norm(middle).astype(jnp.bfloat16)
    hidden = jax.nn.gelu(
        jnp.dot(second, up_weight, preferred_element_type=jnp.float32), approximate=True
    ).astype(jnp.bfloat16)
    final = middle + jnp.dot(hidden, down_weight, preferred_element_type=jnp.float32)
    return final.astype(jnp.bfloat16)


def shards(
    features,
    occupied,
    voxel_order,
    conv_weight,
    cpe_linear,
    qkv_weight,
    proj_weight,
    up_weight,
    down_weight,
):
    span_x, span_y, width = features.shape
    cells = span_x * span_y
    occ_flat = occupied.reshape(cells)
    mine = jnp.sum(occ_flat, dtype=jnp.int32)
    counts = gather_counts(mine)
    masked = features * occupied[:, :, None].astype(jnp.bfloat16)
    padded = with_halo(masked, (("gx", 0), ("gy", 1)), 1)
    total = jnp.zeros((cells, width), jnp.float32)
    for offset in range(9):
        step_x = offset // 3
        step_y = offset % 3
        window = padded[step_x : step_x + span_x, step_y : step_y + span_y].reshape(cells, width)
        total = total + jnp.dot(window, conv_weight[offset], preferred_element_type=jnp.float32)
    conv = total.astype(jnp.bfloat16)
    linear = jnp.dot(conv, cpe_linear, preferred_element_type=jnp.float32)
    encoded = (features.reshape(cells, width).astype(jnp.float32) + layer_norm(linear)).astype(
        jnp.bfloat16
    )
    order = voxel_order[0]
    voxel = jnp.arange(cells, dtype=jnp.int32)
    _, rank_of = lax.sort_key_val(order, voxel)
    key = (1 - occ_flat) * cells + rank_of
    _, listed_voxel = lax.sort_key_val(key, voxel)
    devices = counts.shape[0]
    count_x = lax.axis_size("gx")
    count_y = lax.axis_size("gy")
    here_x = lax.axis_index("gx")
    here_y = lax.axis_index("gy")
    ranks = block_curve(count_x, count_y)
    position = ranks[here_x * count_y + here_y]
    by_position = jnp.zeros((devices,), jnp.int32).at[ranks].set(counts)
    starts = jnp.cumsum(by_position, dtype=jnp.int32) - by_position
    start_here = starts[position]
    excess = start_here - position * LIVE
    beyond = start_here + mine - (position + 1) * LIVE
    capacity = CAP
    slot = jnp.arange(capacity, dtype=jnp.int32)
    row = jnp.arange(LIVE, dtype=jnp.int32)
    own_item = row - excess
    own_ok = (own_item >= 0) & (own_item < mine)
    prev_ok = slot < -excess
    next_ok = slot < beyond
    spare = jnp.zeros((capacity,), jnp.int32)
    extended = jnp.concatenate([spare, listed_voxel, spare])
    own_src = lax.dynamic_slice_in_dim(extended, capacity - excess, LIVE, 0)
    next_src = lax.dynamic_slice_in_dim(listed_voxel, LIVE - excess, capacity, 0)
    items = jnp.concatenate([own_src, listed_voxel[:capacity], next_src])
    ok = jnp.concatenate([own_ok, prev_ok, next_ok])
    picked = jnp.where(ok, items, -1)
    gathered = onehot_gather(encoded, picked)
    mine_rows = gathered[:LIVE]
    to_prev = gathered[LIVE : LIVE + capacity]
    to_next = gathered[LIVE + capacity :]
    empty = jnp.zeros((capacity, width), jnp.bfloat16)
    device_of = jnp.zeros((devices,), jnp.int32).at[ranks].set(jnp.arange(devices, dtype=jnp.int32))
    prev_device = device_of[jnp.maximum(position - 1, 0)]
    next_device = device_of[jnp.minimum(position + 1, devices - 1)]
    prev_x = prev_device // count_y
    prev_y = prev_device % count_y
    next_x = next_device // count_y
    next_y = next_device % count_y
    from_prev = empty
    from_next = empty

    def outgoing(target_x, target_y):
        toward_next = (next_x == target_x) & (next_y == target_y)
        toward_prev = (prev_x == target_x) & (prev_y == target_y)
        return jnp.where(toward_next, to_next, jnp.where(toward_prev, to_prev, empty))

    for step in (1, -1):
        got = passed_along(outgoing(here_x + step, here_y), "gx", step)
        source_x = here_x - step
        from_prev = jnp.where((prev_x == source_x) & (prev_y == here_y), got, from_prev)
        from_next = jnp.where((next_x == source_x) & (next_y == here_y), got, from_next)
    for step in (1, -1):
        got = passed_along(outgoing(here_x, here_y + step), "gy", step)
        source_y = here_y - step
        from_prev = jnp.where((prev_x == here_x) & (prev_y == source_y), got, from_prev)
        from_next = jnp.where((next_x == here_x) & (next_y == source_y), got, from_next)
    from_prev = jnp.where((slot < excess)[:, None], from_prev, empty)
    from_next = jnp.where((slot < -beyond)[:, None], from_next, empty)
    leading = jnp.concatenate(
        [from_prev, jnp.zeros((LIVE - capacity, width), jnp.bfloat16)], axis=0
    )
    trailing = lax.dynamic_slice_in_dim(
        jnp.concatenate([jnp.zeros((LIVE, width), jnp.bfloat16), from_next], axis=0),
        -beyond,
        LIVE,
        0,
    )
    owned = mine_rows + leading + trailing
    middle = attention_mid(owned, qkv_weight, proj_weight)
    return feed_forward(middle, up_weight, down_weight)


def solution(mesh):
    return jax.shard_map(
        shards,
        mesh=mesh,
        in_specs=(
            P("gx", "gy", None),
            P("gx", "gy"),
            P(("gx", "gy"), None),
            P(),
            P(),
            P(),
            P(),
            P(),
            P(),
        ),
        out_specs=P(("gx", "gy"), None),
        check_vma=False,
    )
```

```python
import functools
import math

import jax
import jax.numpy as jnp
from jax import lax
from jax.experimental import pallas as pl
from jax.experimental.pallas import tpu as pltpu
from jax.sharding import PartitionSpec as P

HEADS = 8
PATCH = 1024
LIVE = 2048
CAP = 256
HD = 32


def with_halo(block, sides, width):
    for axis, dim in sides:
        count = lax.axis_size(axis)
        forward = [(i, i + 1) for i in range(count - 1)]
        backward = [(target, source) for source, target in forward]
        low = lax.ppermute(
            lax.slice_in_dim(block, block.shape[dim] - width, None, axis=dim), axis, forward
        )
        high = lax.ppermute(lax.slice_in_dim(block, 0, width, axis=dim), axis, backward)
        block = jnp.concatenate([low, block, high], axis=dim)
    return block


def passed_along(block, axis, distance):
    devices = range(lax.axis_size(axis))
    route = [(i - distance, i) for i in devices if i - distance in devices]
    return lax.ppermute(block, axis, route)


def hilbert_points(side):
    index = jnp.arange(side * side, dtype=jnp.int32)
    coord_x = jnp.zeros((side * side,), jnp.int32)
    coord_y = jnp.zeros((side * side,), jnp.int32)
    remain = index
    level = 1
    while level < side:
        bit_x = remain // 2 % 2
        bit_y = jnp.bitwise_xor(remain, bit_x) % 2
        mirror = (bit_y == 0) & (bit_x == 1)
        moved_x = jnp.where(mirror, level - 1 - coord_x, coord_x)
        moved_y = jnp.where(mirror, level - 1 - coord_y, coord_y)
        turned = bit_y == 0
        coord_x = jnp.where(turned, moved_y, moved_x) + level * bit_x
        coord_y = jnp.where(turned, moved_x, moved_y) + level * bit_y
        remain = remain // 4
        level = level * 2
    return (coord_x, coord_y)


def block_curve(count_x, count_y):
    total = count_x * count_y
    square = count_y * count_y
    position = jnp.arange(total, dtype=jnp.int32)
    half = position // square
    inner_x, inner_y = hilbert_points(count_y)
    along_x = inner_x[position % square] + half * count_y
    along_y = inner_y[position % square]
    device = along_x * count_y + along_y
    return jnp.zeros((total,), jnp.int32).at[device].set(position)


def layer_norm(values):
    centre = values - jnp.mean(values, axis=-1, keepdims=True)
    spread = jnp.mean(centre * centre, axis=-1, keepdims=True)
    return centre * lax.rsqrt(spread + 1e-05)


def attend_patch(rows, qkv_weight, proj_weight, up_weight, down_weight):
    base = rows.astype(jnp.float32)
    normed = layer_norm(base).astype(jnp.bfloat16)
    projected = jnp.dot(normed, qkv_weight, preferred_element_type=jnp.float32).astype(jnp.bfloat16)
    width = rows.shape[1]
    count = rows.shape[0]
    query = projected[:, :width].reshape(count, HEADS, HD)
    keyset = projected[:, width : 2 * width].reshape(count, HEADS, HD)
    valueset = projected[:, 2 * width :].reshape(count, HEADS, HD)
    scores = jnp.einsum("qhd,khd->hqk", query, keyset, preferred_element_type=jnp.float32) * (
        1.0 / math.sqrt(HD)
    )
    largest = jnp.max(scores, axis=-1, keepdims=True)
    expo = jnp.exp(scores - largest)
    weights = (expo / jnp.sum(expo, axis=-1, keepdims=True)).astype(jnp.bfloat16)
    attended = jnp.einsum(
        "hqk,khd->qhd", weights, valueset, preferred_element_type=jnp.float32
    ).astype(jnp.bfloat16)
    middle = base + jnp.dot(
        attended.reshape(count, width), proj_weight, preferred_element_type=jnp.float32
    )
    second = layer_norm(middle).astype(jnp.bfloat16)
    hidden = jax.nn.gelu(
        jnp.dot(second, up_weight, preferred_element_type=jnp.float32), approximate=True
    ).astype(jnp.bfloat16)
    final = middle + jnp.dot(hidden, down_weight, preferred_element_type=jnp.float32)
    return final.astype(jnp.bfloat16)


def onehot_gather_kernel(index_ref, table_ref, out_ref, acc_ref):
    rows = index_ref.shape[0]
    chunk = 512
    wanted = index_ref[...]
    acc_ref[...] = jnp.zeros_like(acc_ref)
    for part in range(table_ref.shape[0] // chunk):
        ids = lax.broadcasted_iota(jnp.int32, (rows, chunk), 1) + part * chunk
        pick = jnp.where(wanted == ids, 1.0, 0.0).astype(jnp.bfloat16)
        acc_ref[...] += jnp.dot(
            pick, table_ref[pl.ds(part * chunk, chunk), :], preferred_element_type=jnp.float32
        )
    out_ref[...] = acc_ref[...].astype(out_ref.dtype)


def onehot_gather(table, index):
    count = index.shape[0]
    width = table.shape[1]
    tile = 256
    return pl.pallas_call(
        onehot_gather_kernel,
        grid=(count // tile,),
        in_specs=[
            pl.BlockSpec((tile, 1), lambda i: (i, 0)),
            pl.BlockSpec(table.shape, lambda i: (0, 0)),
        ],
        out_specs=pl.BlockSpec((tile, width), lambda i: (i, 0)),
        out_shape=jax.ShapeDtypeStruct((count, width), table.dtype),
        scratch_shapes=[pltpu.VMEM((tile, width), jnp.float32)],
    )(index.reshape(count, 1), table)


MESH = pl.DeviceIdType.MESH


def count_gather_kernel(nx, ny, mine_ref, out_ref, row_buf, grid_buf, send1, recv1, send2, recv2, own_sem):
    me_x = lax.axis_index("gx")
    me_y = lax.axis_index("gy")
    barrier = pltpu.get_barrier_semaphore()
    for k in range(1, ny):
        pl.semaphore_signal(
            barrier, inc=1, device_id=(me_x, lax.rem(me_y + k, ny)), device_id_type=MESH
        )
    for k in range(1, nx):
        pl.semaphore_signal(
            barrier, inc=1, device_id=(lax.rem(me_x + k, nx), me_y), device_id_type=MESH
        )
    pl.semaphore_wait(barrier, nx + ny - 2)

    own = pltpu.make_async_copy(mine_ref, row_buf.at[pl.ds(me_y, 1)], own_sem.at[0])
    own.start()
    for k in range(1, ny):
        pltpu.make_async_remote_copy(
            src_ref=mine_ref,
            dst_ref=row_buf.at[pl.ds(me_y, 1)],
            send_sem=send1.at[k],
            recv_sem=recv1.at[k],
            device_id=(me_x, lax.rem(me_y + k, ny)),
            device_id_type=MESH,
        ).start()
    own.wait()
    for k in range(1, ny):
        sender = lax.rem(me_y - k + ny, ny)
        copy = pltpu.make_async_remote_copy(
            src_ref=mine_ref,
            dst_ref=row_buf.at[pl.ds(sender, 1)],
            send_sem=send1.at[k],
            recv_sem=recv1.at[k],
            device_id=(me_x, sender),
            device_id_type=MESH,
        )
        copy.wait_send()
        copy.wait_recv()

    own = pltpu.make_async_copy(row_buf, grid_buf.at[me_x], own_sem.at[1])
    own.start()
    for k in range(1, nx):
        pltpu.make_async_remote_copy(
            src_ref=row_buf,
            dst_ref=grid_buf.at[me_x],
            send_sem=send2.at[k],
            recv_sem=recv2.at[k],
            device_id=(lax.rem(me_x + k, nx), me_y),
            device_id_type=MESH,
        ).start()
    own.wait()
    for k in range(1, nx):
        sender = lax.rem(me_x - k + nx, nx)
        copy = pltpu.make_async_remote_copy(
            src_ref=row_buf,
            dst_ref=grid_buf.at[sender],
            send_sem=send2.at[k],
            recv_sem=recv2.at[k],
            device_id=(sender, me_y),
            device_id_type=MESH,
        )
        copy.wait_send()
        copy.wait_recv()
    out_ref[...] = grid_buf[...]


def gather_counts(mine):
    nx = lax.axis_size("gx")
    ny = lax.axis_size("gy")
    lanes = 128
    grid = pl.pallas_call(
        functools.partial(count_gather_kernel, nx, ny),
        out_shape=jax.ShapeDtypeStruct((nx, ny, lanes), jnp.int32),
        in_specs=[pl.BlockSpec(memory_space=pltpu.VMEM)],
        out_specs=pl.BlockSpec(memory_space=pltpu.VMEM),
        scratch_shapes=[
            pltpu.VMEM((ny, lanes), jnp.int32),
            pltpu.VMEM((nx, ny, lanes), jnp.int32),
            pltpu.SemaphoreType.DMA((ny,)),
            pltpu.SemaphoreType.DMA((ny,)),
            pltpu.SemaphoreType.DMA((nx,)),
            pltpu.SemaphoreType.DMA((nx,)),
            pltpu.SemaphoreType.DMA((2,)),
        ],
        compiler_params=pltpu.CompilerParams(collective_id=0, has_side_effects=True),
    )(jnp.broadcast_to(mine, (1, lanes)))
    return grid[:, :, 0].reshape(nx * ny)


def attention_kernel(q_ref, k_ref, v_ref, base_ref, proj_ref, out_ref):
    query = q_ref[...]
    keyset = k_ref[...]
    valueset = v_ref[...]
    width = query.shape[1]
    head_of = lax.broadcasted_iota(jnp.int32, (1, width), 1) // HD
    attended = jnp.zeros((query.shape[0], width), jnp.float32)
    for head in range(HEADS):
        mine = head_of == head
        scores = lax.dot_general(
            jnp.where(mine, query, jnp.zeros_like(query)),
            keyset,
            (((1,), (1,)), ((), ())),
            preferred_element_type=jnp.float32,
        ) * (1.0 / math.sqrt(HD))
        largest = jnp.max(scores, axis=-1, keepdims=True)
        expo = jnp.exp(scores - largest)
        weights = (expo * (1.0 / jnp.sum(expo, axis=-1, keepdims=True))).astype(jnp.bfloat16)
        mixed = jnp.dot(weights, valueset, preferred_element_type=jnp.float32)
        attended = jnp.where(mine, mixed, attended)
    out_ref[...] = base_ref[...].astype(jnp.float32) + jnp.dot(
        attended.astype(jnp.bfloat16), proj_ref[...], preferred_element_type=jnp.float32
    )


def attention_mid(rows, qkv_weight, proj_weight):
    count, width = rows.shape
    base = rows.astype(jnp.float32)
    normed = layer_norm(base).astype(jnp.bfloat16)
    projected = jnp.dot(normed, qkv_weight, preferred_element_type=jnp.float32).astype(jnp.bfloat16)
    tile = 256
    tiles = PATCH // tile
    grid = (count // PATCH, tiles)
    return pl.pallas_call(
        attention_kernel,
        grid=grid,
        in_specs=[
            pl.BlockSpec((tile, width), lambda p, t: (p * tiles + t, 0)),
            pl.BlockSpec((PATCH, width), lambda p, t: (p, 1)),
            pl.BlockSpec((PATCH, width), lambda p, t: (p, 2)),
            pl.BlockSpec((tile, width), lambda p, t: (p * tiles + t, 0)),
            pl.BlockSpec((width, width), lambda p, t: (0, 0)),
        ],
        out_specs=pl.BlockSpec((tile, width), lambda p, t: (p * tiles + t, 0)),
        out_shape=jax.ShapeDtypeStruct((count, width), jnp.float32),
    )(projected, projected, projected, rows, proj_weight)


def feed_forward(middle, up_weight, down_weight):
    second = layer_norm(middle).astype(jnp.bfloat16)
    hidden = jax.nn.gelu(
        jnp.dot(second, up_weight, preferred_element_type=jnp.float32), approximate=True
    ).astype(jnp.bfloat16)
    final = middle + jnp.dot(hidden, down_weight, preferred_element_type=jnp.float32)
    return final.astype(jnp.bfloat16)


def shards(
    features,
    occupied,
    voxel_order,
    conv_weight,
    cpe_linear,
    qkv_weight,
    proj_weight,
    up_weight,
    down_weight,
):
    span_x, span_y, width = features.shape
    cells = span_x * span_y
    occ_flat = occupied.reshape(cells)
    mine = jnp.sum(occ_flat, dtype=jnp.int32)
    counts = gather_counts(mine)
    masked = features * occupied[:, :, None].astype(jnp.bfloat16)
    padded = with_halo(masked, (("gx", 0), ("gy", 1)), 1)
    total = jnp.zeros((cells, width), jnp.float32)
    for offset in range(9):
        step_x = offset // 3
        step_y = offset % 3
        window = padded[step_x : step_x + span_x, step_y : step_y + span_y].reshape(cells, width)
        total = total + jnp.dot(window, conv_weight[offset], preferred_element_type=jnp.float32)
    conv = total.astype(jnp.bfloat16)
    linear = jnp.dot(conv, cpe_linear, preferred_element_type=jnp.float32)
    encoded = (features.reshape(cells, width).astype(jnp.float32) + layer_norm(linear)).astype(
        jnp.bfloat16
    )
    order = voxel_order[0]
    voxel = jnp.arange(cells, dtype=jnp.int32)
    _, rank_of = lax.sort_key_val(order, voxel)
    key = (1 - occ_flat) * cells + rank_of
    _, listed_voxel = lax.sort_key_val(key, voxel)
    devices = counts.shape[0]
    count_x = lax.axis_size("gx")
    count_y = lax.axis_size("gy")
    here_x = lax.axis_index("gx")
    here_y = lax.axis_index("gy")
    ranks = block_curve(count_x, count_y)
    position = ranks[here_x * count_y + here_y]
    by_position = jnp.zeros((devices,), jnp.int32).at[ranks].set(counts)
    starts = jnp.cumsum(by_position, dtype=jnp.int32) - by_position
    start_here = starts[position]
    excess = start_here - position * LIVE
    beyond = start_here + mine - (position + 1) * LIVE
    capacity = CAP
    slot = jnp.arange(capacity, dtype=jnp.int32)
    row = jnp.arange(LIVE, dtype=jnp.int32)
    own_item = row - excess
    own_ok = (own_item >= 0) & (own_item < mine)
    prev_ok = slot < -excess
    next_ok = slot < beyond
    spare = jnp.zeros((capacity,), jnp.int32)
    extended = jnp.concatenate([spare, listed_voxel, spare])
    own_src = lax.dynamic_slice_in_dim(extended, capacity - excess, LIVE, 0)
    next_src = lax.dynamic_slice_in_dim(listed_voxel, LIVE - excess, capacity, 0)
    items = jnp.concatenate([own_src, listed_voxel[:capacity], next_src])
    ok = jnp.concatenate([own_ok, prev_ok, next_ok])
    picked = jnp.where(ok, items, -1)
    gathered = onehot_gather(encoded, picked)
    mine_rows = gathered[:LIVE]
    to_prev = gathered[LIVE : LIVE + capacity]
    to_next = gathered[LIVE + capacity :]
    empty = jnp.zeros((capacity, width), jnp.bfloat16)
    device_of = jnp.zeros((devices,), jnp.int32).at[ranks].set(jnp.arange(devices, dtype=jnp.int32))
    prev_device = device_of[jnp.maximum(position - 1, 0)]
    next_device = device_of[jnp.minimum(position + 1, devices - 1)]
    prev_x = prev_device // count_y
    prev_y = prev_device % count_y
    next_x = next_device // count_y
    next_y = next_device % count_y
    from_prev = empty
    from_next = empty

    def outgoing(target_x, target_y):
        toward_next = (next_x == target_x) & (next_y == target_y)
        toward_prev = (prev_x == target_x) & (prev_y == target_y)
        return jnp.where(toward_next, to_next, jnp.where(toward_prev, to_prev, empty))

    for step in (1, -1):
        got = passed_along(outgoing(here_x + step, here_y), "gx", step)
        source_x = here_x - step
        from_prev = jnp.where((prev_x == source_x) & (prev_y == here_y), got, from_prev)
        from_next = jnp.where((next_x == source_x) & (next_y == here_y), got, from_next)
    for step in (1, -1):
        got = passed_along(outgoing(here_x, here_y + step), "gy", step)
        source_y = here_y - step
        from_prev = jnp.where((prev_x == here_x) & (prev_y == source_y), got, from_prev)
        from_next = jnp.where((next_x == here_x) & (next_y == source_y), got, from_next)
    from_prev = jnp.where((slot < excess)[:, None], from_prev, empty)
    from_next = jnp.where((slot < -beyond)[:, None], from_next, empty)
    leading = jnp.concatenate(
        [from_prev, jnp.zeros((LIVE - capacity, width), jnp.bfloat16)], axis=0
    )
    trailing = lax.dynamic_slice_in_dim(
        jnp.concatenate([jnp.zeros((LIVE, width), jnp.bfloat16), from_next], axis=0),
        -beyond,
        LIVE,
        0,
    )
    owned = mine_rows + leading + trailing
    middle = attention_mid(owned, qkv_weight, proj_weight)
    return feed_forward(middle, up_weight, down_weight)


def solution(mesh):
    return jax.shard_map(
        shards,
        mesh=mesh,
        in_specs=(
            P("gx", "gy", None),
            P("gx", "gy"),
            P(("gx", "gy"), None),
            P(),
            P(),
            P(),
            P(),
            P(),
            P(),
        ),
        out_specs=P(("gx", "gy"), None),
        check_vma=False,
    )
```

```python
import functools
import math

import jax
import numpy as np
import jax.numpy as jnp
from jax import lax
from jax.experimental import pallas as pl
from jax.experimental.pallas import tpu as pltpu
from jax.sharding import PartitionSpec as P

HEADS = 8
PATCH = 1024
LIVE = 2048
CAP = 256
HD = 32


def with_halo(block, sides, width):
    for axis, dim in sides:
        count = lax.axis_size(axis)
        forward = [(i, i + 1) for i in range(count - 1)]
        backward = [(target, source) for source, target in forward]
        low = lax.ppermute(
            lax.slice_in_dim(block, block.shape[dim] - width, None, axis=dim), axis, forward
        )
        high = lax.ppermute(lax.slice_in_dim(block, 0, width, axis=dim), axis, backward)
        block = jnp.concatenate([low, block, high], axis=dim)
    return block


def passed_along(block, axis, distance):
    devices = range(lax.axis_size(axis))
    route = [(i - distance, i) for i in devices if i - distance in devices]
    return lax.ppermute(block, axis, route)


def hilbert_points(side):
    index = jnp.arange(side * side, dtype=jnp.int32)
    coord_x = jnp.zeros((side * side,), jnp.int32)
    coord_y = jnp.zeros((side * side,), jnp.int32)
    remain = index
    level = 1
    while level < side:
        bit_x = remain // 2 % 2
        bit_y = jnp.bitwise_xor(remain, bit_x) % 2
        mirror = (bit_y == 0) & (bit_x == 1)
        moved_x = jnp.where(mirror, level - 1 - coord_x, coord_x)
        moved_y = jnp.where(mirror, level - 1 - coord_y, coord_y)
        turned = bit_y == 0
        coord_x = jnp.where(turned, moved_y, moved_x) + level * bit_x
        coord_y = jnp.where(turned, moved_x, moved_y) + level * bit_y
        remain = remain // 4
        level = level * 2
    return (coord_x, coord_y)


def block_curve(count_x, count_y):
    total = count_x * count_y
    square = count_y * count_y
    position = jnp.arange(total, dtype=jnp.int32)
    half = position // square
    inner_x, inner_y = hilbert_points(count_y)
    along_x = inner_x[position % square] + half * count_y
    along_y = inner_y[position % square]
    device = along_x * count_y + along_y
    return jnp.zeros((total,), jnp.int32).at[device].set(position)


def layer_norm(values):
    centre = values - jnp.mean(values, axis=-1, keepdims=True)
    spread = jnp.mean(centre * centre, axis=-1, keepdims=True)
    return centre * lax.rsqrt(spread + 1e-05)


def attend_patch(rows, qkv_weight, proj_weight, up_weight, down_weight):
    base = rows.astype(jnp.float32)
    normed = layer_norm(base).astype(jnp.bfloat16)
    projected = jnp.dot(normed, qkv_weight, preferred_element_type=jnp.float32).astype(jnp.bfloat16)
    width = rows.shape[1]
    count = rows.shape[0]
    query = projected[:, :width].reshape(count, HEADS, HD)
    keyset = projected[:, width : 2 * width].reshape(count, HEADS, HD)
    valueset = projected[:, 2 * width :].reshape(count, HEADS, HD)
    scores = jnp.einsum("qhd,khd->hqk", query, keyset, preferred_element_type=jnp.float32) * (
        1.0 / math.sqrt(HD)
    )
    largest = jnp.max(scores, axis=-1, keepdims=True)
    expo = jnp.exp(scores - largest)
    weights = (expo / jnp.sum(expo, axis=-1, keepdims=True)).astype(jnp.bfloat16)
    attended = jnp.einsum(
        "hqk,khd->qhd", weights, valueset, preferred_element_type=jnp.float32
    ).astype(jnp.bfloat16)
    middle = base + jnp.dot(
        attended.reshape(count, width), proj_weight, preferred_element_type=jnp.float32
    )
    second = layer_norm(middle).astype(jnp.bfloat16)
    hidden = jax.nn.gelu(
        jnp.dot(second, up_weight, preferred_element_type=jnp.float32), approximate=True
    ).astype(jnp.bfloat16)
    final = middle + jnp.dot(hidden, down_weight, preferred_element_type=jnp.float32)
    return final.astype(jnp.bfloat16)


def onehot_gather_kernel(index_ref, table_ref, out_ref, acc_ref):
    rows = index_ref.shape[0]
    chunk = 512
    wanted = index_ref[...]
    acc_ref[...] = jnp.zeros_like(acc_ref)
    for part in range(table_ref.shape[0] // chunk):
        ids = lax.broadcasted_iota(jnp.int32, (rows, chunk), 1) + part * chunk
        pick = jnp.where(wanted == ids, 1.0, 0.0).astype(jnp.bfloat16)
        acc_ref[...] += jnp.dot(
            pick, table_ref[pl.ds(part * chunk, chunk), :], preferred_element_type=jnp.float32
        )
    out_ref[...] = acc_ref[...].astype(out_ref.dtype)


def onehot_gather(table, index):
    count = index.shape[0]
    width = table.shape[1]
    tile = 256
    return pl.pallas_call(
        onehot_gather_kernel,
        grid=(count // tile,),
        in_specs=[
            pl.BlockSpec((tile, 1), lambda i: (i, 0)),
            pl.BlockSpec(table.shape, lambda i: (0, 0)),
        ],
        out_specs=pl.BlockSpec((tile, width), lambda i: (i, 0)),
        out_shape=jax.ShapeDtypeStruct((count, width), table.dtype),
        scratch_shapes=[pltpu.VMEM((tile, width), jnp.float32)],
    )(index.reshape(count, 1), table)


MESH = pl.DeviceIdType.MESH


def count_gather_kernel(nx, ny, mine_ref, out_ref, row_buf, grid_buf, send1, recv1, send2, recv2, own_sem):
    me_x = lax.axis_index("gx")
    me_y = lax.axis_index("gy")
    barrier = pltpu.get_barrier_semaphore()
    for k in range(1, ny):
        pl.semaphore_signal(
            barrier, inc=1, device_id=(me_x, lax.rem(me_y + k, ny)), device_id_type=MESH
        )
    for k in range(1, nx):
        pl.semaphore_signal(
            barrier, inc=1, device_id=(lax.rem(me_x + k, nx), me_y), device_id_type=MESH
        )
    pl.semaphore_wait(barrier, nx + ny - 2)

    own = pltpu.make_async_copy(mine_ref, row_buf.at[pl.ds(me_y, 1)], own_sem.at[0])
    own.start()
    for k in range(1, ny):
        pltpu.make_async_remote_copy(
            src_ref=mine_ref,
            dst_ref=row_buf.at[pl.ds(me_y, 1)],
            send_sem=send1.at[k],
            recv_sem=recv1.at[k],
            device_id=(me_x, lax.rem(me_y + k, ny)),
            device_id_type=MESH,
        ).start()
    own.wait()
    for k in range(1, ny):
        sender = lax.rem(me_y - k + ny, ny)
        copy = pltpu.make_async_remote_copy(
            src_ref=mine_ref,
            dst_ref=row_buf.at[pl.ds(sender, 1)],
            send_sem=send1.at[k],
            recv_sem=recv1.at[k],
            device_id=(me_x, sender),
            device_id_type=MESH,
        )
        copy.wait_send()
        copy.wait_recv()

    own = pltpu.make_async_copy(row_buf, grid_buf.at[me_x], own_sem.at[1])
    own.start()
    for k in range(1, nx):
        pltpu.make_async_remote_copy(
            src_ref=row_buf,
            dst_ref=grid_buf.at[me_x],
            send_sem=send2.at[k],
            recv_sem=recv2.at[k],
            device_id=(lax.rem(me_x + k, nx), me_y),
            device_id_type=MESH,
        ).start()
    own.wait()
    for k in range(1, nx):
        sender = lax.rem(me_x - k + nx, nx)
        copy = pltpu.make_async_remote_copy(
            src_ref=row_buf,
            dst_ref=grid_buf.at[sender],
            send_sem=send2.at[k],
            recv_sem=recv2.at[k],
            device_id=(sender, me_y),
            device_id_type=MESH,
        )
        copy.wait_send()
        copy.wait_recv()
    out_ref[...] = grid_buf[...]


def gather_counts(mine):
    nx = lax.axis_size("gx")
    ny = lax.axis_size("gy")
    lanes = 128
    grid = pl.pallas_call(
        functools.partial(count_gather_kernel, nx, ny),
        out_shape=jax.ShapeDtypeStruct((nx, ny, lanes), jnp.int32),
        in_specs=[pl.BlockSpec(memory_space=pltpu.VMEM)],
        out_specs=pl.BlockSpec(memory_space=pltpu.VMEM),
        scratch_shapes=[
            pltpu.VMEM((ny, lanes), jnp.int32),
            pltpu.VMEM((nx, ny, lanes), jnp.int32),
            pltpu.SemaphoreType.DMA((ny,)),
            pltpu.SemaphoreType.DMA((ny,)),
            pltpu.SemaphoreType.DMA((nx,)),
            pltpu.SemaphoreType.DMA((nx,)),
            pltpu.SemaphoreType.DMA((2,)),
        ],
        compiler_params=pltpu.CompilerParams(collective_id=0, has_side_effects=True),
    )(jnp.broadcast_to(mine, (1, lanes)))
    return grid[:, :, 0].reshape(nx * ny)


def attention_kernel(q_ref, k_ref, v_ref, base_ref, proj_ref, out_ref):
    query = q_ref[...]
    keyset = k_ref[...]
    valueset = v_ref[...]
    width = query.shape[1]
    head_of = lax.broadcasted_iota(jnp.int32, (1, width), 1) // HD
    attended = jnp.zeros((query.shape[0], width), jnp.float32)
    for head in range(HEADS):
        mine = head_of == head
        scores = lax.dot_general(
            jnp.where(mine, query, jnp.zeros_like(query)),
            keyset,
            (((1,), (1,)), ((), ())),
            preferred_element_type=jnp.float32,
        ) * (1.0 / math.sqrt(HD))
        largest = jnp.max(scores, axis=-1, keepdims=True)
        expo = jnp.exp(scores - largest)
        weights = (expo * (1.0 / jnp.sum(expo, axis=-1, keepdims=True))).astype(jnp.bfloat16)
        mixed = jnp.dot(weights, valueset, preferred_element_type=jnp.float32)
        attended = jnp.where(mine, mixed, attended)
    out_ref[...] = base_ref[...].astype(jnp.float32) + jnp.dot(
        attended.astype(jnp.bfloat16), proj_ref[...], preferred_element_type=jnp.float32
    )


def attention_mid(rows, qkv_weight, proj_weight):
    count, width = rows.shape
    base = rows.astype(jnp.float32)
    normed = layer_norm(base).astype(jnp.bfloat16)
    projected = jnp.dot(normed, qkv_weight, preferred_element_type=jnp.float32).astype(jnp.bfloat16)
    tile = 256
    tiles = PATCH // tile
    grid = (count // PATCH, tiles)
    return pl.pallas_call(
        attention_kernel,
        grid=grid,
        in_specs=[
            pl.BlockSpec((tile, width), lambda p, t: (p * tiles + t, 0)),
            pl.BlockSpec((PATCH, width), lambda p, t: (p, 1)),
            pl.BlockSpec((PATCH, width), lambda p, t: (p, 2)),
            pl.BlockSpec((tile, width), lambda p, t: (p * tiles + t, 0)),
            pl.BlockSpec((width, width), lambda p, t: (0, 0)),
        ],
        out_specs=pl.BlockSpec((tile, width), lambda p, t: (p * tiles + t, 0)),
        out_shape=jax.ShapeDtypeStruct((count, width), jnp.float32),
    )(projected, projected, projected, rows, proj_weight)


def feed_forward(middle, up_weight, down_weight):
    second = layer_norm(middle).astype(jnp.bfloat16)
    hidden = jax.nn.gelu(
        jnp.dot(second, up_weight, preferred_element_type=jnp.float32), approximate=True
    ).astype(jnp.bfloat16)
    final = middle + jnp.dot(hidden, down_weight, preferred_element_type=jnp.float32)
    return final.astype(jnp.bfloat16)


def curve_tables(count_x, count_y):
    square = count_y * count_y
    index = np.arange(square)
    coord_x = np.zeros(square, np.int64)
    coord_y = np.zeros(square, np.int64)
    remain = index.copy()
    level = 1
    while level < count_y:
        bit_x = remain // 2 % 2
        bit_y = np.bitwise_xor(remain, bit_x) % 2
        mirror = (bit_y == 0) & (bit_x == 1)
        moved_x = np.where(mirror, level - 1 - coord_x, coord_x)
        moved_y = np.where(mirror, level - 1 - coord_y, coord_y)
        turned = bit_y == 0
        coord_x = np.where(turned, moved_y, moved_x) + level * bit_x
        coord_y = np.where(turned, moved_x, moved_y) + level * bit_y
        remain = remain // 4
        level = level * 2
    position = np.arange(count_x * count_y)
    along_x = coord_x[position % square] + (position // square) * count_y
    along_y = coord_y[position % square]
    return [int(d) for d in along_x * count_y + along_y]


def shards(
    features,
    occupied,
    voxel_order,
    conv_weight,
    cpe_linear,
    qkv_weight,
    proj_weight,
    up_weight,
    down_weight,
):
    span_x, span_y, width = features.shape
    cells = span_x * span_y
    occ_flat = occupied.reshape(cells)
    mine = jnp.sum(occ_flat, dtype=jnp.int32)
    counts = gather_counts(mine)
    masked = features * occupied[:, :, None].astype(jnp.bfloat16)
    padded = with_halo(masked, (("gx", 0), ("gy", 1)), 1)
    total = jnp.zeros((cells, width), jnp.float32)
    for offset in range(9):
        step_x = offset // 3
        step_y = offset % 3
        window = padded[step_x : step_x + span_x, step_y : step_y + span_y].reshape(cells, width)
        total = total + jnp.dot(window, conv_weight[offset], preferred_element_type=jnp.float32)
    conv = total.astype(jnp.bfloat16)
    linear = jnp.dot(conv, cpe_linear, preferred_element_type=jnp.float32)
    encoded = (features.reshape(cells, width).astype(jnp.float32) + layer_norm(linear)).astype(
        jnp.bfloat16
    )
    order = voxel_order[0]
    voxel = jnp.arange(cells, dtype=jnp.int32)
    _, rank_of = lax.sort_key_val(order, voxel)
    key = (1 - occ_flat) * cells + rank_of
    _, listed_voxel = lax.sort_key_val(key, voxel)
    devices = counts.shape[0]
    count_x = lax.axis_size("gx")
    count_y = lax.axis_size("gy")
    here_x = lax.axis_index("gx")
    here_y = lax.axis_index("gy")
    ranks = block_curve(count_x, count_y)
    position = ranks[here_x * count_y + here_y]
    by_position = jnp.zeros((devices,), jnp.int32).at[ranks].set(counts)
    starts = jnp.cumsum(by_position, dtype=jnp.int32) - by_position
    start_here = starts[position]
    excess = start_here - position * LIVE
    beyond = start_here + mine - (position + 1) * LIVE
    capacity = CAP
    slot = jnp.arange(capacity, dtype=jnp.int32)
    row = jnp.arange(LIVE, dtype=jnp.int32)
    own_item = row - excess
    own_ok = (own_item >= 0) & (own_item < mine)
    prev_ok = slot < -excess
    next_ok = slot < beyond
    spare = jnp.zeros((capacity,), jnp.int32)
    extended = jnp.concatenate([spare, listed_voxel, spare])
    own_src = lax.dynamic_slice_in_dim(extended, capacity - excess, LIVE, 0)
    next_src = lax.dynamic_slice_in_dim(listed_voxel, LIVE - excess, capacity, 0)
    items = jnp.concatenate([own_src, listed_voxel[:capacity], next_src])
    ok = jnp.concatenate([own_ok, prev_ok, next_ok])
    picked = jnp.where(ok, items, -1)
    gathered = onehot_gather(encoded, picked)
    mine_rows = gathered[:LIVE]
    to_prev = gathered[LIVE : LIVE + capacity]
    to_next = gathered[LIVE + capacity :]
    empty = jnp.zeros((capacity, width), jnp.bfloat16)
    device_at = curve_tables(count_x, count_y)
    forward = [(device_at[p], device_at[p + 1]) for p in range(devices - 1)]
    backward = [(target, source) for source, target in forward]
    from_prev = lax.ppermute(to_next, ("gx", "gy"), forward)
    from_next = lax.ppermute(to_prev, ("gx", "gy"), backward)
    from_prev = jnp.where((slot < excess)[:, None], from_prev, empty)
    from_next = jnp.where((slot < -beyond)[:, None], from_next, empty)
    leading = jnp.concatenate(
        [from_prev, jnp.zeros((LIVE - capacity, width), jnp.bfloat16)], axis=0
    )
    trailing = lax.dynamic_slice_in_dim(
        jnp.concatenate([jnp.zeros((LIVE, width), jnp.bfloat16), from_next], axis=0),
        -beyond,
        LIVE,
        0,
    )
    owned = mine_rows + leading + trailing
    middle = attention_mid(owned, qkv_weight, proj_weight)
    return feed_forward(middle, up_weight, down_weight)


def solution(mesh):
    return jax.shard_map(
        shards,
        mesh=mesh,
        in_specs=(
            P("gx", "gy", None),
            P("gx", "gy"),
            P(("gx", "gy"), None),
            P(),
            P(),
            P(),
            P(),
            P(),
            P(),
        ),
        out_specs=P(("gx", "gy"), None),
        check_vma=False,
    )
```

```python
import functools
import math

import jax
import numpy as np
import jax.numpy as jnp
from jax import lax
from jax.experimental import pallas as pl
from jax.experimental.pallas import tpu as pltpu
from jax.sharding import PartitionSpec as P

HEADS = 8
PATCH = 1024
LIVE = 2048
CAP = 256
HD = 32


def with_halo(block, sides, width):
    for axis, dim in sides:
        count = lax.axis_size(axis)
        forward = [(i, i + 1) for i in range(count - 1)]
        backward = [(target, source) for source, target in forward]
        low = lax.ppermute(
            lax.slice_in_dim(block, block.shape[dim] - width, None, axis=dim), axis, forward
        )
        high = lax.ppermute(lax.slice_in_dim(block, 0, width, axis=dim), axis, backward)
        block = jnp.concatenate([low, block, high], axis=dim)
    return block


def passed_along(block, axis, distance):
    devices = range(lax.axis_size(axis))
    route = [(i - distance, i) for i in devices if i - distance in devices]
    return lax.ppermute(block, axis, route)


def hilbert_points(side):
    index = jnp.arange(side * side, dtype=jnp.int32)
    coord_x = jnp.zeros((side * side,), jnp.int32)
    coord_y = jnp.zeros((side * side,), jnp.int32)
    remain = index
    level = 1
    while level < side:
        bit_x = remain // 2 % 2
        bit_y = jnp.bitwise_xor(remain, bit_x) % 2
        mirror = (bit_y == 0) & (bit_x == 1)
        moved_x = jnp.where(mirror, level - 1 - coord_x, coord_x)
        moved_y = jnp.where(mirror, level - 1 - coord_y, coord_y)
        turned = bit_y == 0
        coord_x = jnp.where(turned, moved_y, moved_x) + level * bit_x
        coord_y = jnp.where(turned, moved_x, moved_y) + level * bit_y
        remain = remain // 4
        level = level * 2
    return (coord_x, coord_y)


def block_curve(count_x, count_y):
    total = count_x * count_y
    square = count_y * count_y
    position = jnp.arange(total, dtype=jnp.int32)
    half = position // square
    inner_x, inner_y = hilbert_points(count_y)
    along_x = inner_x[position % square] + half * count_y
    along_y = inner_y[position % square]
    device = along_x * count_y + along_y
    return jnp.zeros((total,), jnp.int32).at[device].set(position)


def layer_norm(values):
    centre = values - jnp.mean(values, axis=-1, keepdims=True)
    spread = jnp.mean(centre * centre, axis=-1, keepdims=True)
    return centre * lax.rsqrt(spread + 1e-05)


def attend_patch(rows, qkv_weight, proj_weight, up_weight, down_weight):
    base = rows.astype(jnp.float32)
    normed = layer_norm(base).astype(jnp.bfloat16)
    projected = jnp.dot(normed, qkv_weight, preferred_element_type=jnp.float32).astype(jnp.bfloat16)
    width = rows.shape[1]
    count = rows.shape[0]
    query = projected[:, :width].reshape(count, HEADS, HD)
    keyset = projected[:, width : 2 * width].reshape(count, HEADS, HD)
    valueset = projected[:, 2 * width :].reshape(count, HEADS, HD)
    scores = jnp.einsum("qhd,khd->hqk", query, keyset, preferred_element_type=jnp.float32) * (
        1.0 / math.sqrt(HD)
    )
    largest = jnp.max(scores, axis=-1, keepdims=True)
    expo = jnp.exp(scores - largest)
    weights = (expo / jnp.sum(expo, axis=-1, keepdims=True)).astype(jnp.bfloat16)
    attended = jnp.einsum(
        "hqk,khd->qhd", weights, valueset, preferred_element_type=jnp.float32
    ).astype(jnp.bfloat16)
    middle = base + jnp.dot(
        attended.reshape(count, width), proj_weight, preferred_element_type=jnp.float32
    )
    second = layer_norm(middle).astype(jnp.bfloat16)
    hidden = jax.nn.gelu(
        jnp.dot(second, up_weight, preferred_element_type=jnp.float32), approximate=True
    ).astype(jnp.bfloat16)
    final = middle + jnp.dot(hidden, down_weight, preferred_element_type=jnp.float32)
    return final.astype(jnp.bfloat16)


def onehot_gather_kernel(index_ref, table_ref, out_ref, acc_ref):
    rows = index_ref.shape[0]
    chunk = 512
    wanted = index_ref[...]
    acc_ref[...] = jnp.zeros_like(acc_ref)
    for part in range(table_ref.shape[0] // chunk):
        ids = lax.broadcasted_iota(jnp.int32, (rows, chunk), 1) + part * chunk
        pick = jnp.where(wanted == ids, 1.0, 0.0).astype(jnp.bfloat16)
        acc_ref[...] += jnp.dot(
            pick, table_ref[pl.ds(part * chunk, chunk), :], preferred_element_type=jnp.float32
        )
    out_ref[...] = acc_ref[...].astype(out_ref.dtype)


def onehot_gather(table, index):
    count = index.shape[0]
    width = table.shape[1]
    tile = 256
    return pl.pallas_call(
        onehot_gather_kernel,
        grid=(count // tile,),
        in_specs=[
            pl.BlockSpec((tile, 1), lambda i: (i, 0)),
            pl.BlockSpec(table.shape, lambda i: (0, 0)),
        ],
        out_specs=pl.BlockSpec((tile, width), lambda i: (i, 0)),
        out_shape=jax.ShapeDtypeStruct((count, width), table.dtype),
        scratch_shapes=[pltpu.VMEM((tile, width), jnp.float32)],
    )(index.reshape(count, 1), table)


MESH = pl.DeviceIdType.MESH


def gather_rows(index_ref, table_ref, out_ref, first, last):
    tile = 256
    chunk = 512

    def one_tile(i, carry):
        rows = pl.ds(pl.multiple_of(i * tile, tile), tile)
        wanted = index_ref[rows, :]
        total = jnp.zeros((tile, out_ref.shape[1]), jnp.float32)
        for part in range(table_ref.shape[0] // chunk):
            ids = lax.broadcasted_iota(jnp.int32, (tile, chunk), 1) + part * chunk
            pick = jnp.where(wanted == ids, 1.0, 0.0).astype(jnp.bfloat16)
            total += jnp.dot(
                pick, table_ref[pl.ds(part * chunk, chunk), :], preferred_element_type=jnp.float32
            )
        out_ref[rows, :] = total.astype(out_ref.dtype)
        return carry

    lax.fori_loop(first, last, one_tile, 0)


def count_gather_kernel(nx, ny, index_ref, table_ref, mine_ref, rows_ref, out_ref, row_buf, grid_buf, send1, recv1, send2, recv2, own_sem):
    me_x = lax.axis_index("gx")
    me_y = lax.axis_index("gy")
    barrier = pltpu.get_barrier_semaphore()
    for k in range(1, ny):
        pl.semaphore_signal(
            barrier, inc=1, device_id=(me_x, lax.rem(me_y + k, ny)), device_id_type=MESH
        )
    for k in range(1, nx):
        pl.semaphore_signal(
            barrier, inc=1, device_id=(lax.rem(me_x + k, nx), me_y), device_id_type=MESH
        )
    pl.semaphore_wait(barrier, nx + ny - 2)

    own = pltpu.make_async_copy(mine_ref, row_buf.at[pl.ds(me_y, 1)], own_sem.at[0])
    own.start()
    for k in range(1, ny):
        pltpu.make_async_remote_copy(
            src_ref=mine_ref,
            dst_ref=row_buf.at[pl.ds(me_y, 1)],
            send_sem=send1.at[k],
            recv_sem=recv1.at[k],
            device_id=(me_x, lax.rem(me_y + k, ny)),
            device_id_type=MESH,
        ).start()
    tiles = rows_ref.shape[0] // 256
    gather_rows(index_ref, table_ref, rows_ref, 0, tiles // 2)
    own.wait()
    for k in range(1, ny):
        sender = lax.rem(me_y - k + ny, ny)
        copy = pltpu.make_async_remote_copy(
            src_ref=mine_ref,
            dst_ref=row_buf.at[pl.ds(sender, 1)],
            send_sem=send1.at[k],
            recv_sem=recv1.at[k],
            device_id=(me_x, sender),
            device_id_type=MESH,
        )
        copy.wait_send()
        copy.wait_recv()

    own = pltpu.make_async_copy(row_buf, grid_buf.at[me_x], own_sem.at[1])
    own.start()
    for k in range(1, nx):
        pltpu.make_async_remote_copy(
            src_ref=row_buf,
            dst_ref=grid_buf.at[me_x],
            send_sem=send2.at[k],
            recv_sem=recv2.at[k],
            device_id=(lax.rem(me_x + k, nx), me_y),
            device_id_type=MESH,
        ).start()
    gather_rows(index_ref, table_ref, rows_ref, tiles // 2, tiles)
    own.wait()
    for k in range(1, nx):
        sender = lax.rem(me_x - k + nx, nx)
        copy = pltpu.make_async_remote_copy(
            src_ref=row_buf,
            dst_ref=grid_buf.at[sender],
            send_sem=send2.at[k],
            recv_sem=recv2.at[k],
            device_id=(sender, me_y),
            device_id_type=MESH,
        )
        copy.wait_send()
        copy.wait_recv()
    out_ref[...] = grid_buf[...]


def gather_counts(mine, table, index):
    nx = lax.axis_size("gx")
    ny = lax.axis_size("gy")
    lanes = 128
    listed, grid = pl.pallas_call(
        functools.partial(count_gather_kernel, nx, ny),
        out_shape=(
            jax.ShapeDtypeStruct((index.shape[0], table.shape[1]), table.dtype),
            jax.ShapeDtypeStruct((nx, ny, lanes), jnp.int32),
        ),
        in_specs=[pl.BlockSpec(memory_space=pltpu.VMEM)] * 3,
        out_specs=(pl.BlockSpec(memory_space=pltpu.VMEM), pl.BlockSpec(memory_space=pltpu.VMEM)),
        scratch_shapes=[
            pltpu.VMEM((ny, lanes), jnp.int32),
            pltpu.VMEM((nx, ny, lanes), jnp.int32),
            pltpu.SemaphoreType.DMA((ny,)),
            pltpu.SemaphoreType.DMA((ny,)),
            pltpu.SemaphoreType.DMA((nx,)),
            pltpu.SemaphoreType.DMA((nx,)),
            pltpu.SemaphoreType.DMA((2,)),
        ],
        compiler_params=pltpu.CompilerParams(collective_id=0, has_side_effects=True),
    )(index.reshape(-1, 1), table, jnp.broadcast_to(mine, (1, lanes)))
    return listed, grid[:, :, 0].reshape(nx * ny)


def attention_kernel(q_ref, k_ref, v_ref, base_ref, proj_ref, out_ref):
    query = q_ref[...]
    keyset = k_ref[...]
    valueset = v_ref[...]
    width = query.shape[1]
    head_of = lax.broadcasted_iota(jnp.int32, (1, width), 1) // HD
    attended = jnp.zeros((query.shape[0], width), jnp.float32)
    for head in range(HEADS):
        mine = head_of == head
        scores = lax.dot_general(
            jnp.where(mine, query, jnp.zeros_like(query)),
            keyset,
            (((1,), (1,)), ((), ())),
            preferred_element_type=jnp.float32,
        ) * (1.0 / math.sqrt(HD))
        largest = jnp.max(scores, axis=-1, keepdims=True)
        expo = jnp.exp(scores - largest)
        weights = (expo * (1.0 / jnp.sum(expo, axis=-1, keepdims=True))).astype(jnp.bfloat16)
        mixed = jnp.dot(weights, valueset, preferred_element_type=jnp.float32)
        attended = jnp.where(mine, mixed, attended)
    out_ref[...] = base_ref[...].astype(jnp.float32) + jnp.dot(
        attended.astype(jnp.bfloat16), proj_ref[...], preferred_element_type=jnp.float32
    )


def attention_mid(rows, qkv_weight, proj_weight):
    count, width = rows.shape
    base = rows.astype(jnp.float32)
    normed = layer_norm(base).astype(jnp.bfloat16)
    projected = jnp.dot(normed, qkv_weight, preferred_element_type=jnp.float32).astype(jnp.bfloat16)
    tile = 256
    tiles = PATCH // tile
    grid = (count // PATCH, tiles)
    return pl.pallas_call(
        attention_kernel,
        grid=grid,
        in_specs=[
            pl.BlockSpec((tile, width), lambda p, t: (p * tiles + t, 0)),
            pl.BlockSpec((PATCH, width), lambda p, t: (p, 1)),
            pl.BlockSpec((PATCH, width), lambda p, t: (p, 2)),
            pl.BlockSpec((tile, width), lambda p, t: (p * tiles + t, 0)),
            pl.BlockSpec((width, width), lambda p, t: (0, 0)),
        ],
        out_specs=pl.BlockSpec((tile, width), lambda p, t: (p * tiles + t, 0)),
        out_shape=jax.ShapeDtypeStruct((count, width), jnp.float32),
    )(projected, projected, projected, rows, proj_weight)


def feed_forward(middle, up_weight, down_weight):
    second = layer_norm(middle).astype(jnp.bfloat16)
    hidden = jax.nn.gelu(
        jnp.dot(second, up_weight, preferred_element_type=jnp.float32), approximate=True
    ).astype(jnp.bfloat16)
    final = middle + jnp.dot(hidden, down_weight, preferred_element_type=jnp.float32)
    return final.astype(jnp.bfloat16)


def curve_tables(count_x, count_y):
    square = count_y * count_y
    index = np.arange(square)
    coord_x = np.zeros(square, np.int64)
    coord_y = np.zeros(square, np.int64)
    remain = index.copy()
    level = 1
    while level < count_y:
        bit_x = remain // 2 % 2
        bit_y = np.bitwise_xor(remain, bit_x) % 2
        mirror = (bit_y == 0) & (bit_x == 1)
        moved_x = np.where(mirror, level - 1 - coord_x, coord_x)
        moved_y = np.where(mirror, level - 1 - coord_y, coord_y)
        turned = bit_y == 0
        coord_x = np.where(turned, moved_y, moved_x) + level * bit_x
        coord_y = np.where(turned, moved_x, moved_y) + level * bit_y
        remain = remain // 4
        level = level * 2
    position = np.arange(count_x * count_y)
    along_x = coord_x[position % square] + (position // square) * count_y
    along_y = coord_y[position % square]
    return [int(d) for d in along_x * count_y + along_y]


def shards(
    features,
    occupied,
    voxel_order,
    conv_weight,
    cpe_linear,
    qkv_weight,
    proj_weight,
    up_weight,
    down_weight,
):
    span_x, span_y, width = features.shape
    cells = span_x * span_y
    occ_flat = occupied.reshape(cells)
    mine = jnp.sum(occ_flat, dtype=jnp.int32)
    masked = features * occupied[:, :, None].astype(jnp.bfloat16)
    padded = with_halo(masked, (("gx", 0), ("gy", 1)), 1)
    total = jnp.zeros((cells, width), jnp.float32)
    for offset in range(9):
        step_x = offset // 3
        step_y = offset % 3
        window = padded[step_x : step_x + span_x, step_y : step_y + span_y].reshape(cells, width)
        total = total + jnp.dot(window, conv_weight[offset], preferred_element_type=jnp.float32)
    conv = total.astype(jnp.bfloat16)
    linear = jnp.dot(conv, cpe_linear, preferred_element_type=jnp.float32)
    encoded = (features.reshape(cells, width).astype(jnp.float32) + layer_norm(linear)).astype(
        jnp.bfloat16
    )
    order = voxel_order[0]
    voxel = jnp.arange(cells, dtype=jnp.int32)
    _, rank_of = lax.sort_key_val(order, voxel)
    key = (1 - occ_flat) * cells + rank_of
    _, listed_voxel = lax.sort_key_val(key, voxel)
    capacity = CAP
    list_index = jnp.arange(LIVE + 2 * capacity, dtype=jnp.int32)
    picked = jnp.where(list_index < mine, listed_voxel[: LIVE + 2 * capacity], -1)
    list_rows, counts = gather_counts(mine, encoded, picked)
    devices = counts.shape[0]
    count_x = lax.axis_size("gx")
    count_y = lax.axis_size("gy")
    here_x = lax.axis_index("gx")
    here_y = lax.axis_index("gy")
    ranks = block_curve(count_x, count_y)
    position = ranks[here_x * count_y + here_y]
    by_position = jnp.zeros((devices,), jnp.int32).at[ranks].set(counts)
    starts = jnp.cumsum(by_position, dtype=jnp.int32) - by_position
    start_here = starts[position]
    excess = start_here - position * LIVE
    beyond = start_here + mine - (position + 1) * LIVE
    slot = jnp.arange(capacity, dtype=jnp.int32)
    empty = jnp.zeros((capacity, width), jnp.bfloat16)
    extended = jnp.concatenate([empty, list_rows], axis=0)
    mine_rows = lax.dynamic_slice_in_dim(extended, capacity - excess, LIVE, 0)
    to_prev = jnp.where((slot < -excess)[:, None], list_rows[:capacity], empty)
    to_next = jnp.where(
        (slot < beyond)[:, None], lax.dynamic_slice_in_dim(list_rows, LIVE - excess, capacity, 0), empty
    )
    device_at = curve_tables(count_x, count_y)
    forward = [(device_at[p], device_at[p + 1]) for p in range(devices - 1)]
    backward = [(target, source) for source, target in forward]
    from_prev = lax.ppermute(to_next, ("gx", "gy"), forward)
    from_next = lax.ppermute(to_prev, ("gx", "gy"), backward)
    from_prev = jnp.where((slot < excess)[:, None], from_prev, empty)
    from_next = jnp.where((slot < -beyond)[:, None], from_next, empty)
    leading = jnp.concatenate(
        [from_prev, jnp.zeros((LIVE - capacity, width), jnp.bfloat16)], axis=0
    )
    trailing = lax.dynamic_slice_in_dim(
        jnp.concatenate([jnp.zeros((LIVE, width), jnp.bfloat16), from_next], axis=0),
        -beyond,
        LIVE,
        0,
    )
    owned = mine_rows + leading + trailing
    middle = attention_mid(owned, qkv_weight, proj_weight)
    return feed_forward(middle, up_weight, down_weight)


def solution(mesh):
    return jax.shard_map(
        shards,
        mesh=mesh,
        in_specs=(
            P("gx", "gy", None),
            P("gx", "gy"),
            P(("gx", "gy"), None),
            P(),
            P(),
            P(),
            P(),
            P(),
            P(),
        ),
        out_specs=P(("gx", "gy"), None),
        check_vma=False,
    )
```

```python
import functools
import math

import jax
import numpy as np
import jax.numpy as jnp
from jax import lax
from jax.experimental import pallas as pl
from jax.experimental.pallas import tpu as pltpu
from jax.sharding import PartitionSpec as P

HEADS = 8
PATCH = 1024
LIVE = 2048
CAP = 256
HD = 32


def with_halo(block, sides, width):
    for axis, dim in sides:
        count = lax.axis_size(axis)
        forward = [(i, i + 1) for i in range(count - 1)]
        backward = [(target, source) for source, target in forward]
        low = lax.ppermute(
            lax.slice_in_dim(block, block.shape[dim] - width, None, axis=dim), axis, forward
        )
        high = lax.ppermute(lax.slice_in_dim(block, 0, width, axis=dim), axis, backward)
        block = jnp.concatenate([low, block, high], axis=dim)
    return block


def passed_along(block, axis, distance):
    devices = range(lax.axis_size(axis))
    route = [(i - distance, i) for i in devices if i - distance in devices]
    return lax.ppermute(block, axis, route)


def hilbert_points(side):
    index = jnp.arange(side * side, dtype=jnp.int32)
    coord_x = jnp.zeros((side * side,), jnp.int32)
    coord_y = jnp.zeros((side * side,), jnp.int32)
    remain = index
    level = 1
    while level < side:
        bit_x = remain // 2 % 2
        bit_y = jnp.bitwise_xor(remain, bit_x) % 2
        mirror = (bit_y == 0) & (bit_x == 1)
        moved_x = jnp.where(mirror, level - 1 - coord_x, coord_x)
        moved_y = jnp.where(mirror, level - 1 - coord_y, coord_y)
        turned = bit_y == 0
        coord_x = jnp.where(turned, moved_y, moved_x) + level * bit_x
        coord_y = jnp.where(turned, moved_x, moved_y) + level * bit_y
        remain = remain // 4
        level = level * 2
    return (coord_x, coord_y)


def block_curve(count_x, count_y):
    total = count_x * count_y
    square = count_y * count_y
    position = jnp.arange(total, dtype=jnp.int32)
    half = position // square
    inner_x, inner_y = hilbert_points(count_y)
    along_x = inner_x[position % square] + half * count_y
    along_y = inner_y[position % square]
    device = along_x * count_y + along_y
    return jnp.zeros((total,), jnp.int32).at[device].set(position)


def layer_norm(values):
    centre = values - jnp.mean(values, axis=-1, keepdims=True)
    spread = jnp.mean(centre * centre, axis=-1, keepdims=True)
    return centre * lax.rsqrt(spread + 1e-05)


def attend_patch(rows, qkv_weight, proj_weight, up_weight, down_weight):
    base = rows.astype(jnp.float32)
    normed = layer_norm(base).astype(jnp.bfloat16)
    projected = jnp.dot(normed, qkv_weight, preferred_element_type=jnp.float32).astype(jnp.bfloat16)
    width = rows.shape[1]
    count = rows.shape[0]
    query = projected[:, :width].reshape(count, HEADS, HD)
    keyset = projected[:, width : 2 * width].reshape(count, HEADS, HD)
    valueset = projected[:, 2 * width :].reshape(count, HEADS, HD)
    scores = jnp.einsum("qhd,khd->hqk", query, keyset, preferred_element_type=jnp.float32) * (
        1.0 / math.sqrt(HD)
    )
    largest = jnp.max(scores, axis=-1, keepdims=True)
    expo = jnp.exp(scores - largest)
    weights = (expo / jnp.sum(expo, axis=-1, keepdims=True)).astype(jnp.bfloat16)
    attended = jnp.einsum(
        "hqk,khd->qhd", weights, valueset, preferred_element_type=jnp.float32
    ).astype(jnp.bfloat16)
    middle = base + jnp.dot(
        attended.reshape(count, width), proj_weight, preferred_element_type=jnp.float32
    )
    second = layer_norm(middle).astype(jnp.bfloat16)
    hidden = jax.nn.gelu(
        jnp.dot(second, up_weight, preferred_element_type=jnp.float32), approximate=True
    ).astype(jnp.bfloat16)
    final = middle + jnp.dot(hidden, down_weight, preferred_element_type=jnp.float32)
    return final.astype(jnp.bfloat16)


def onehot_gather_kernel(index_ref, table_ref, out_ref, acc_ref):
    rows = index_ref.shape[0]
    chunk = 512
    wanted = index_ref[...]
    acc_ref[...] = jnp.zeros_like(acc_ref)
    for part in range(table_ref.shape[0] // chunk):
        ids = lax.broadcasted_iota(jnp.int32, (rows, chunk), 1) + part * chunk
        pick = jnp.where(wanted == ids, 1.0, 0.0).astype(jnp.bfloat16)
        acc_ref[...] += jnp.dot(
            pick, table_ref[pl.ds(part * chunk, chunk), :], preferred_element_type=jnp.float32
        )
    out_ref[...] = acc_ref[...].astype(out_ref.dtype)


def onehot_gather(table, index):
    count = index.shape[0]
    width = table.shape[1]
    tile = 256
    return pl.pallas_call(
        onehot_gather_kernel,
        grid=(count // tile,),
        in_specs=[
            pl.BlockSpec((tile, 1), lambda i: (i, 0)),
            pl.BlockSpec(table.shape, lambda i: (0, 0)),
        ],
        out_specs=pl.BlockSpec((tile, width), lambda i: (i, 0)),
        out_shape=jax.ShapeDtypeStruct((count, width), table.dtype),
        scratch_shapes=[pltpu.VMEM((tile, width), jnp.float32)],
    )(index.reshape(count, 1), table)


MESH = pl.DeviceIdType.MESH


def gather_rows(index_ref, table_ref, out_ref, first, last):
    tile = 256
    chunk = 512

    def one_tile(i, carry):
        rows = pl.ds(pl.multiple_of(i * tile, tile), tile)
        wanted = index_ref[rows, :]
        total = jnp.zeros((tile, out_ref.shape[1]), jnp.float32)
        for part in range(table_ref.shape[0] // chunk):
            ids = lax.broadcasted_iota(jnp.int32, (tile, chunk), 1) + part * chunk
            pick = jnp.where(wanted == ids, 1.0, 0.0).astype(jnp.bfloat16)
            total += jnp.dot(
                pick, table_ref[pl.ds(part * chunk, chunk), :], preferred_element_type=jnp.float32
            )
        out_ref[rows, :] = total.astype(out_ref.dtype)
        return carry

    lax.fori_loop(first, last, one_tile, 0)


def count_gather_kernel(nx, ny, index_ref, table_ref, mine_ref, rows_ref, out_ref, row_buf, grid_buf, send1, recv1, send2, recv2, own_sem):
    me_x = lax.axis_index("gx")
    me_y = lax.axis_index("gy")
    barrier = pltpu.get_barrier_semaphore()
    for k in range(1, ny):
        pl.semaphore_signal(
            barrier, inc=1, device_id=(me_x, lax.rem(me_y + k, ny)), device_id_type=MESH
        )
    for k in range(1, nx):
        pl.semaphore_signal(
            barrier, inc=1, device_id=(lax.rem(me_x + k, nx), me_y), device_id_type=MESH
        )
    pl.semaphore_wait(barrier, nx + ny - 2)

    own = pltpu.make_async_copy(mine_ref, row_buf.at[pl.ds(me_y, 1)], own_sem.at[0])
    own.start()
    for k in range(1, ny):
        pltpu.make_async_remote_copy(
            src_ref=mine_ref,
            dst_ref=row_buf.at[pl.ds(me_y, 1)],
            send_sem=send1.at[k],
            recv_sem=recv1.at[k],
            device_id=(me_x, lax.rem(me_y + k, ny)),
            device_id_type=MESH,
        ).start()
    tiles = rows_ref.shape[0] // 256
    gather_rows(index_ref, table_ref, rows_ref, 0, tiles // 2)
    own.wait()
    for k in range(1, ny):
        sender = lax.rem(me_y - k + ny, ny)
        copy = pltpu.make_async_remote_copy(
            src_ref=mine_ref,
            dst_ref=row_buf.at[pl.ds(sender, 1)],
            send_sem=send1.at[k],
            recv_sem=recv1.at[k],
            device_id=(me_x, sender),
            device_id_type=MESH,
        )
        copy.wait_send()
        copy.wait_recv()

    own = pltpu.make_async_copy(row_buf, grid_buf.at[me_x], own_sem.at[1])
    own.start()
    for k in range(1, nx):
        pltpu.make_async_remote_copy(
            src_ref=row_buf,
            dst_ref=grid_buf.at[me_x],
            send_sem=send2.at[k],
            recv_sem=recv2.at[k],
            device_id=(lax.rem(me_x + k, nx), me_y),
            device_id_type=MESH,
        ).start()
    gather_rows(index_ref, table_ref, rows_ref, tiles // 2, tiles)
    own.wait()
    for k in range(1, nx):
        sender = lax.rem(me_x - k + nx, nx)
        copy = pltpu.make_async_remote_copy(
            src_ref=row_buf,
            dst_ref=grid_buf.at[sender],
            send_sem=send2.at[k],
            recv_sem=recv2.at[k],
            device_id=(sender, me_y),
            device_id_type=MESH,
        )
        copy.wait_send()
        copy.wait_recv()
    out_ref[...] = grid_buf[...]


def gather_counts(mine, table, index):
    nx = lax.axis_size("gx")
    ny = lax.axis_size("gy")
    lanes = 128
    listed, grid = pl.pallas_call(
        functools.partial(count_gather_kernel, nx, ny),
        out_shape=(
            jax.ShapeDtypeStruct((index.shape[0], table.shape[1]), table.dtype),
            jax.ShapeDtypeStruct((nx, ny, lanes), jnp.int32),
        ),
        in_specs=[pl.BlockSpec(memory_space=pltpu.VMEM)] * 3,
        out_specs=(pl.BlockSpec(memory_space=pltpu.VMEM), pl.BlockSpec(memory_space=pltpu.VMEM)),
        scratch_shapes=[
            pltpu.VMEM((ny, lanes), jnp.int32),
            pltpu.VMEM((nx, ny, lanes), jnp.int32),
            pltpu.SemaphoreType.DMA((ny,)),
            pltpu.SemaphoreType.DMA((ny,)),
            pltpu.SemaphoreType.DMA((nx,)),
            pltpu.SemaphoreType.DMA((nx,)),
            pltpu.SemaphoreType.DMA((2,)),
        ],
        compiler_params=pltpu.CompilerParams(collective_id=0, has_side_effects=True),
    )(index.reshape(-1, 1), table, jnp.broadcast_to(mine, (1, lanes)))
    return listed, grid[:, :, 0].reshape(nx * ny)


def attention_kernel(q_ref, k_ref, v_ref, base_ref, proj_ref, out_ref):
    query = q_ref[...]
    keyset = k_ref[...]
    valueset = v_ref[...]
    width = query.shape[1]
    head_of = lax.broadcasted_iota(jnp.int32, (1, width), 1) // HD
    attended = jnp.zeros((query.shape[0], width), jnp.float32)
    for head in range(HEADS):
        mine = head_of == head
        scores = lax.dot_general(
            jnp.where(mine, query, jnp.zeros_like(query)),
            keyset,
            (((1,), (1,)), ((), ())),
            preferred_element_type=jnp.float32,
        ) * (1.0 / math.sqrt(HD))
        largest = jnp.max(scores, axis=-1, keepdims=True)
        expo = jnp.exp(scores - largest)
        weights = (expo * (1.0 / jnp.sum(expo, axis=-1, keepdims=True))).astype(jnp.bfloat16)
        mixed = jnp.dot(weights, valueset, preferred_element_type=jnp.float32)
        attended = jnp.where(mine, mixed, attended)
    out_ref[...] = base_ref[...].astype(jnp.float32) + jnp.dot(
        attended.astype(jnp.bfloat16), proj_ref[...], preferred_element_type=jnp.float32
    )


def attention_mid(rows, qkv_weight, proj_weight):
    count, width = rows.shape
    base = rows.astype(jnp.float32)
    normed = layer_norm(base).astype(jnp.bfloat16)
    projected = jnp.dot(normed, qkv_weight, preferred_element_type=jnp.float32).astype(jnp.bfloat16)
    tile = 256
    tiles = PATCH // tile
    grid = (count // PATCH, tiles)
    return pl.pallas_call(
        attention_kernel,
        grid=grid,
        in_specs=[
            pl.BlockSpec((tile, width), lambda p, t: (p * tiles + t, 0)),
            pl.BlockSpec((PATCH, width), lambda p, t: (p, 1)),
            pl.BlockSpec((PATCH, width), lambda p, t: (p, 2)),
            pl.BlockSpec((tile, width), lambda p, t: (p * tiles + t, 0)),
            pl.BlockSpec((width, width), lambda p, t: (0, 0)),
        ],
        out_specs=pl.BlockSpec((tile, width), lambda p, t: (p * tiles + t, 0)),
        out_shape=jax.ShapeDtypeStruct((count, width), jnp.float32),
    )(projected, projected, projected, rows, proj_weight)


def feed_forward(middle, up_weight, down_weight):
    second = layer_norm(middle).astype(jnp.bfloat16)
    hidden = jax.nn.gelu(
        jnp.dot(second, up_weight, preferred_element_type=jnp.float32), approximate=True
    ).astype(jnp.bfloat16)
    final = middle + jnp.dot(hidden, down_weight, preferred_element_type=jnp.float32)
    return final.astype(jnp.bfloat16)


def curve_tables(count_x, count_y):
    square = count_y * count_y
    index = np.arange(square)
    coord_x = np.zeros(square, np.int64)
    coord_y = np.zeros(square, np.int64)
    remain = index.copy()
    level = 1
    while level < count_y:
        bit_x = remain // 2 % 2
        bit_y = np.bitwise_xor(remain, bit_x) % 2
        mirror = (bit_y == 0) & (bit_x == 1)
        moved_x = np.where(mirror, level - 1 - coord_x, coord_x)
        moved_y = np.where(mirror, level - 1 - coord_y, coord_y)
        turned = bit_y == 0
        coord_x = np.where(turned, moved_y, moved_x) + level * bit_x
        coord_y = np.where(turned, moved_x, moved_y) + level * bit_y
        remain = remain // 4
        level = level * 2
    position = np.arange(count_x * count_y)
    along_x = coord_x[position % square] + (position // square) * count_y
    along_y = coord_y[position % square]
    return [int(d) for d in along_x * count_y + along_y]


def conv_kernel(shifted_ref, features_ref, weight_ref, linear_ref, out_ref):
    rows = features_ref.shape[0]
    side = shifted_ref.shape[2]
    width = features_ref.shape[-1]
    first = pl.program_id(0) * rows
    total = jnp.zeros((rows * side, width), jnp.float32)
    for offset in range(9):
        step_x = offset // 3
        step_y = offset % 3
        window = shifted_ref[step_y, pl.ds(first + step_x, rows)].reshape(rows * side, width)
        total += jnp.dot(window, weight_ref[offset], preferred_element_type=jnp.float32)
    linear = jnp.dot(total.astype(jnp.bfloat16), linear_ref[...], preferred_element_type=jnp.float32)
    base = features_ref[...].reshape(rows * side, width).astype(jnp.float32)
    out_ref[...] = (base + layer_norm(linear)).astype(out_ref.dtype)


def encode(padded, features, conv_weight, cpe_linear):
    span_x, span_y, width = features.shape
    shifted = jnp.stack([padded[:, step : step + span_y] for step in range(3)])
    rows = 8
    return pl.pallas_call(
        conv_kernel,
        grid=(span_x // rows,),
        in_specs=[
            pl.BlockSpec(memory_space=pltpu.VMEM),
            pl.BlockSpec((rows, span_y, width), lambda i: (i, 0, 0)),
            pl.BlockSpec(conv_weight.shape, lambda i: (0, 0, 0)),
            pl.BlockSpec(cpe_linear.shape, lambda i: (0, 0)),
        ],
        out_specs=pl.BlockSpec((rows * span_y, width), lambda i: (i, 0)),
        out_shape=jax.ShapeDtypeStruct((span_x * span_y, width), features.dtype),
    )(shifted, features, conv_weight, cpe_linear)


def shards(
    features,
    occupied,
    voxel_order,
    conv_weight,
    cpe_linear,
    qkv_weight,
    proj_weight,
    up_weight,
    down_weight,
):
    span_x, span_y, width = features.shape
    cells = span_x * span_y
    occ_flat = occupied.reshape(cells)
    mine = jnp.sum(occ_flat, dtype=jnp.int32)
    masked = features * occupied[:, :, None].astype(jnp.bfloat16)
    padded = with_halo(masked, (("gx", 0), ("gy", 1)), 1)
    encoded = encode(padded, features, conv_weight, cpe_linear)
    order = voxel_order[0]
    voxel = jnp.arange(cells, dtype=jnp.int32)
    _, rank_of = lax.sort_key_val(order, voxel)
    key = (1 - occ_flat) * cells + rank_of
    _, listed_voxel = lax.sort_key_val(key, voxel)
    capacity = CAP
    list_index = jnp.arange(LIVE + 2 * capacity, dtype=jnp.int32)
    picked = jnp.where(list_index < mine, listed_voxel[: LIVE + 2 * capacity], -1)
    list_rows, counts = gather_counts(mine, encoded, picked)
    devices = counts.shape[0]
    count_x = lax.axis_size("gx")
    count_y = lax.axis_size("gy")
    here_x = lax.axis_index("gx")
    here_y = lax.axis_index("gy")
    ranks = block_curve(count_x, count_y)
    position = ranks[here_x * count_y + here_y]
    by_position = jnp.zeros((devices,), jnp.int32).at[ranks].set(counts)
    starts = jnp.cumsum(by_position, dtype=jnp.int32) - by_position
    start_here = starts[position]
    excess = start_here - position * LIVE
    beyond = start_here + mine - (position + 1) * LIVE
    slot = jnp.arange(capacity, dtype=jnp.int32)
    empty = jnp.zeros((capacity, width), jnp.bfloat16)
    extended = jnp.concatenate([empty, list_rows], axis=0)
    mine_rows = lax.dynamic_slice_in_dim(extended, capacity - excess, LIVE, 0)
    to_prev = jnp.where((slot < -excess)[:, None], list_rows[:capacity], empty)
    to_next = jnp.where(
        (slot < beyond)[:, None], lax.dynamic_slice_in_dim(list_rows, LIVE - excess, capacity, 0), empty
    )
    device_at = curve_tables(count_x, count_y)
    forward = [(device_at[p], device_at[p + 1]) for p in range(devices - 1)]
    backward = [(target, source) for source, target in forward]
    from_prev = lax.ppermute(to_next, ("gx", "gy"), forward)
    from_next = lax.ppermute(to_prev, ("gx", "gy"), backward)
    from_prev = jnp.where((slot < excess)[:, None], from_prev, empty)
    from_next = jnp.where((slot < -beyond)[:, None], from_next, empty)
    leading = jnp.concatenate(
        [from_prev, jnp.zeros((LIVE - capacity, width), jnp.bfloat16)], axis=0
    )
    trailing = lax.dynamic_slice_in_dim(
        jnp.concatenate([jnp.zeros((LIVE, width), jnp.bfloat16), from_next], axis=0),
        -beyond,
        LIVE,
        0,
    )
    owned = mine_rows + leading + trailing
    middle = attention_mid(owned, qkv_weight, proj_weight)
    return feed_forward(middle, up_weight, down_weight)


def solution(mesh):
    return jax.shard_map(
        shards,
        mesh=mesh,
        in_specs=(
            P("gx", "gy", None),
            P("gx", "gy"),
            P(("gx", "gy"), None),
            P(),
            P(),
            P(),
            P(),
            P(),
            P(),
        ),
        out_specs=P(("gx", "gy"), None),
        check_vma=False,
    )
```

```python
import functools
import math

import jax
import numpy as np
import jax.numpy as jnp
from jax import lax
from jax.experimental import pallas as pl
from jax.experimental.pallas import tpu as pltpu
from jax.sharding import PartitionSpec as P

HEADS = 8
PATCH = 1024
LIVE = 2048
CAP = 256
HD = 32


def with_halo(block, sides, width):
    for axis, dim in sides:
        count = lax.axis_size(axis)
        forward = [(i, i + 1) for i in range(count - 1)]
        backward = [(target, source) for source, target in forward]
        low = lax.ppermute(
            lax.slice_in_dim(block, block.shape[dim] - width, None, axis=dim), axis, forward
        )
        high = lax.ppermute(lax.slice_in_dim(block, 0, width, axis=dim), axis, backward)
        block = jnp.concatenate([low, block, high], axis=dim)
    return block


def passed_along(block, axis, distance):
    devices = range(lax.axis_size(axis))
    route = [(i - distance, i) for i in devices if i - distance in devices]
    return lax.ppermute(block, axis, route)


def hilbert_points(side):
    index = jnp.arange(side * side, dtype=jnp.int32)
    coord_x = jnp.zeros((side * side,), jnp.int32)
    coord_y = jnp.zeros((side * side,), jnp.int32)
    remain = index
    level = 1
    while level < side:
        bit_x = remain // 2 % 2
        bit_y = jnp.bitwise_xor(remain, bit_x) % 2
        mirror = (bit_y == 0) & (bit_x == 1)
        moved_x = jnp.where(mirror, level - 1 - coord_x, coord_x)
        moved_y = jnp.where(mirror, level - 1 - coord_y, coord_y)
        turned = bit_y == 0
        coord_x = jnp.where(turned, moved_y, moved_x) + level * bit_x
        coord_y = jnp.where(turned, moved_x, moved_y) + level * bit_y
        remain = remain // 4
        level = level * 2
    return (coord_x, coord_y)


def block_curve(count_x, count_y):
    total = count_x * count_y
    square = count_y * count_y
    position = jnp.arange(total, dtype=jnp.int32)
    half = position // square
    inner_x, inner_y = hilbert_points(count_y)
    along_x = inner_x[position % square] + half * count_y
    along_y = inner_y[position % square]
    device = along_x * count_y + along_y
    return jnp.zeros((total,), jnp.int32).at[device].set(position)


def layer_norm(values):
    centre = values - jnp.mean(values, axis=-1, keepdims=True)
    spread = jnp.mean(centre * centre, axis=-1, keepdims=True)
    return centre * lax.rsqrt(spread + 1e-05)


def attend_patch(rows, qkv_weight, proj_weight, up_weight, down_weight):
    base = rows.astype(jnp.float32)
    normed = layer_norm(base).astype(jnp.bfloat16)
    projected = jnp.dot(normed, qkv_weight, preferred_element_type=jnp.float32).astype(jnp.bfloat16)
    width = rows.shape[1]
    count = rows.shape[0]
    query = projected[:, :width].reshape(count, HEADS, HD)
    keyset = projected[:, width : 2 * width].reshape(count, HEADS, HD)
    valueset = projected[:, 2 * width :].reshape(count, HEADS, HD)
    scores = jnp.einsum("qhd,khd->hqk", query, keyset, preferred_element_type=jnp.float32) * (
        1.0 / math.sqrt(HD)
    )
    largest = jnp.max(scores, axis=-1, keepdims=True)
    expo = jnp.exp(scores - largest)
    weights = (expo / jnp.sum(expo, axis=-1, keepdims=True)).astype(jnp.bfloat16)
    attended = jnp.einsum(
        "hqk,khd->qhd", weights, valueset, preferred_element_type=jnp.float32
    ).astype(jnp.bfloat16)
    middle = base + jnp.dot(
        attended.reshape(count, width), proj_weight, preferred_element_type=jnp.float32
    )
    second = layer_norm(middle).astype(jnp.bfloat16)
    hidden = jax.nn.gelu(
        jnp.dot(second, up_weight, preferred_element_type=jnp.float32), approximate=True
    ).astype(jnp.bfloat16)
    final = middle + jnp.dot(hidden, down_weight, preferred_element_type=jnp.float32)
    return final.astype(jnp.bfloat16)


def onehot_gather_kernel(index_ref, table_ref, out_ref, acc_ref):
    rows = index_ref.shape[0]
    chunk = 512
    wanted = index_ref[...]
    acc_ref[...] = jnp.zeros_like(acc_ref)
    for part in range(table_ref.shape[0] // chunk):
        ids = lax.broadcasted_iota(jnp.int32, (rows, chunk), 1) + part * chunk
        pick = jnp.where(wanted == ids, 1.0, 0.0).astype(jnp.bfloat16)
        acc_ref[...] += jnp.dot(
            pick, table_ref[pl.ds(part * chunk, chunk), :], preferred_element_type=jnp.float32
        )
    out_ref[...] = acc_ref[...].astype(out_ref.dtype)


def onehot_gather(table, index):
    count = index.shape[0]
    width = table.shape[1]
    tile = 256
    return pl.pallas_call(
        onehot_gather_kernel,
        grid=(count // tile,),
        in_specs=[
            pl.BlockSpec((tile, 1), lambda i: (i, 0)),
            pl.BlockSpec(table.shape, lambda i: (0, 0)),
        ],
        out_specs=pl.BlockSpec((tile, width), lambda i: (i, 0)),
        out_shape=jax.ShapeDtypeStruct((count, width), table.dtype),
        scratch_shapes=[pltpu.VMEM((tile, width), jnp.float32)],
    )(index.reshape(count, 1), table)


MESH = pl.DeviceIdType.MESH


def gather_rows(index_ref, table_ref, out_ref, first, last):
    tile = 256
    chunk = 512

    def one_tile(i, carry):
        rows = pl.ds(pl.multiple_of(i * tile, tile), tile)
        wanted = index_ref[rows, :]
        total = jnp.zeros((tile, out_ref.shape[1]), jnp.float32)
        for part in range(table_ref.shape[0] // chunk):
            ids = lax.broadcasted_iota(jnp.int32, (tile, chunk), 1) + part * chunk
            pick = jnp.where(wanted == ids, 1.0, 0.0).astype(jnp.bfloat16)
            total += jnp.dot(
                pick, table_ref[pl.ds(part * chunk, chunk), :], preferred_element_type=jnp.float32
            )
        out_ref[rows, :] = total.astype(out_ref.dtype)
        return carry

    lax.fori_loop(first, last, one_tile, 0)


def count_gather_kernel(nx, ny, index_ref, table_ref, mine_ref, rows_ref, out_ref, row_buf, grid_buf, send1, recv1, send2, recv2, own_sem):
    me_x = lax.axis_index("gx")
    me_y = lax.axis_index("gy")
    barrier = pltpu.get_barrier_semaphore()
    for k in range(1, ny):
        pl.semaphore_signal(
            barrier, inc=1, device_id=(me_x, lax.rem(me_y + k, ny)), device_id_type=MESH
        )
    for k in range(1, nx):
        pl.semaphore_signal(
            barrier, inc=1, device_id=(lax.rem(me_x + k, nx), me_y), device_id_type=MESH
        )
    pl.semaphore_wait(barrier, nx + ny - 2)

    own = pltpu.make_async_copy(mine_ref, row_buf.at[pl.ds(me_y, 1)], own_sem.at[0])
    own.start()
    for k in range(1, ny):
        pltpu.make_async_remote_copy(
            src_ref=mine_ref,
            dst_ref=row_buf.at[pl.ds(me_y, 1)],
            send_sem=send1.at[k],
            recv_sem=recv1.at[k],
            device_id=(me_x, lax.rem(me_y + k, ny)),
            device_id_type=MESH,
        ).start()
    tiles = rows_ref.shape[0] // 256
    gather_rows(index_ref, table_ref, rows_ref, 0, tiles // 2)
    own.wait()
    for k in range(1, ny):
        sender = lax.rem(me_y - k + ny, ny)
        copy = pltpu.make_async_remote_copy(
            src_ref=mine_ref,
            dst_ref=row_buf.at[pl.ds(sender, 1)],
            send_sem=send1.at[k],
            recv_sem=recv1.at[k],
            device_id=(me_x, sender),
            device_id_type=MESH,
        )
        copy.wait_send()
        copy.wait_recv()

    own = pltpu.make_async_copy(row_buf, grid_buf.at[me_x], own_sem.at[1])
    own.start()
    for k in range(1, nx):
        pltpu.make_async_remote_copy(
            src_ref=row_buf,
            dst_ref=grid_buf.at[me_x],
            send_sem=send2.at[k],
            recv_sem=recv2.at[k],
            device_id=(lax.rem(me_x + k, nx), me_y),
            device_id_type=MESH,
        ).start()
    gather_rows(index_ref, table_ref, rows_ref, tiles // 2, tiles)
    own.wait()
    for k in range(1, nx):
        sender = lax.rem(me_x - k + nx, nx)
        copy = pltpu.make_async_remote_copy(
            src_ref=row_buf,
            dst_ref=grid_buf.at[sender],
            send_sem=send2.at[k],
            recv_sem=recv2.at[k],
            device_id=(sender, me_y),
            device_id_type=MESH,
        )
        copy.wait_send()
        copy.wait_recv()
    out_ref[...] = grid_buf[...]


def gather_counts(mine, table, index):
    nx = lax.axis_size("gx")
    ny = lax.axis_size("gy")
    lanes = 128
    listed, grid = pl.pallas_call(
        functools.partial(count_gather_kernel, nx, ny),
        out_shape=(
            jax.ShapeDtypeStruct((index.shape[0], table.shape[1]), table.dtype),
            jax.ShapeDtypeStruct((nx, ny, lanes), jnp.int32),
        ),
        in_specs=[pl.BlockSpec(memory_space=pltpu.VMEM)] * 3,
        out_specs=(pl.BlockSpec(memory_space=pltpu.VMEM), pl.BlockSpec(memory_space=pltpu.VMEM)),
        scratch_shapes=[
            pltpu.VMEM((ny, lanes), jnp.int32),
            pltpu.VMEM((nx, ny, lanes), jnp.int32),
            pltpu.SemaphoreType.DMA((ny,)),
            pltpu.SemaphoreType.DMA((ny,)),
            pltpu.SemaphoreType.DMA((nx,)),
            pltpu.SemaphoreType.DMA((nx,)),
            pltpu.SemaphoreType.DMA((2,)),
        ],
        compiler_params=pltpu.CompilerParams(collective_id=0, has_side_effects=True),
    )(index.reshape(-1, 1), table, jnp.broadcast_to(mine, (1, lanes)))
    return listed, grid[:, :, 0].reshape(nx * ny)


def attention_kernel(q_ref, k_ref, v_ref, base_ref, proj_ref, out_ref):
    query = q_ref[...]
    keyset = k_ref[...]
    valueset = v_ref[...]
    width = query.shape[1]
    head_of = lax.broadcasted_iota(jnp.int32, (1, width), 1) // HD
    attended = jnp.zeros((query.shape[0], width), jnp.float32)
    for head in range(HEADS):
        mine = head_of == head
        scores = jnp.dot(
            jnp.where(mine, query, jnp.zeros_like(query)),
            keyset,
            preferred_element_type=jnp.float32,
        ) * (1.0 / math.sqrt(HD))
        largest = jnp.max(scores, axis=-1, keepdims=True)
        expo = jnp.exp(scores - largest)
        weights = (expo * (1.0 / jnp.sum(expo, axis=-1, keepdims=True))).astype(jnp.bfloat16)
        mixed = jnp.dot(weights, valueset, preferred_element_type=jnp.float32)
        attended = jnp.where(mine, mixed, attended)
    out_ref[...] = base_ref[...].astype(jnp.float32) + jnp.dot(
        attended.astype(jnp.bfloat16), proj_ref[...], preferred_element_type=jnp.float32
    )


def attention_mid(rows, qkv_weight, proj_weight):
    count, width = rows.shape
    base = rows.astype(jnp.float32)
    normed = layer_norm(base).astype(jnp.bfloat16)
    projected = jnp.dot(normed, qkv_weight, preferred_element_type=jnp.float32).astype(jnp.bfloat16)
    tile = 256
    tiles = PATCH // tile
    grid = (count // PATCH, tiles)
    return pl.pallas_call(
        attention_kernel,
        grid=grid,
        in_specs=[
            pl.BlockSpec((tile, width), lambda p, t: (p * tiles + t, 0)),
            pl.BlockSpec((width, PATCH), lambda p, t: (0, p)),
            pl.BlockSpec((PATCH, width), lambda p, t: (p, 2)),
            pl.BlockSpec((tile, width), lambda p, t: (p * tiles + t, 0)),
            pl.BlockSpec((width, width), lambda p, t: (0, 0)),
        ],
        out_specs=pl.BlockSpec((tile, width), lambda p, t: (p * tiles + t, 0)),
        out_shape=jax.ShapeDtypeStruct((count, width), jnp.float32),
    )(projected, projected[:, width : 2 * width].T, projected, rows, proj_weight)


def feed_forward(middle, up_weight, down_weight):
    second = layer_norm(middle).astype(jnp.bfloat16)
    hidden = jax.nn.gelu(
        jnp.dot(second, up_weight, preferred_element_type=jnp.float32), approximate=True
    ).astype(jnp.bfloat16)
    final = middle + jnp.dot(hidden, down_weight, preferred_element_type=jnp.float32)
    return final.astype(jnp.bfloat16)


def curve_tables(count_x, count_y):
    square = count_y * count_y
    index = np.arange(square)
    coord_x = np.zeros(square, np.int64)
    coord_y = np.zeros(square, np.int64)
    remain = index.copy()
    level = 1
    while level < count_y:
        bit_x = remain // 2 % 2
        bit_y = np.bitwise_xor(remain, bit_x) % 2
        mirror = (bit_y == 0) & (bit_x == 1)
        moved_x = np.where(mirror, level - 1 - coord_x, coord_x)
        moved_y = np.where(mirror, level - 1 - coord_y, coord_y)
        turned = bit_y == 0
        coord_x = np.where(turned, moved_y, moved_x) + level * bit_x
        coord_y = np.where(turned, moved_x, moved_y) + level * bit_y
        remain = remain // 4
        level = level * 2
    position = np.arange(count_x * count_y)
    along_x = coord_x[position % square] + (position // square) * count_y
    along_y = coord_y[position % square]
    return [int(d) for d in along_x * count_y + along_y]


def conv_kernel(shifted_ref, features_ref, weight_ref, linear_ref, out_ref):
    rows = features_ref.shape[0]
    side = shifted_ref.shape[2]
    width = features_ref.shape[-1]
    first = pl.program_id(0) * rows
    total = jnp.zeros((rows * side, width), jnp.float32)
    for offset in range(9):
        step_x = offset // 3
        step_y = offset % 3
        window = shifted_ref[step_y, pl.ds(first + step_x, rows)].reshape(rows * side, width)
        total += jnp.dot(window, weight_ref[offset], preferred_element_type=jnp.float32)
    linear = jnp.dot(total.astype(jnp.bfloat16), linear_ref[...], preferred_element_type=jnp.float32)
    base = features_ref[...].reshape(rows * side, width).astype(jnp.float32)
    out_ref[...] = (base + layer_norm(linear)).astype(out_ref.dtype)


def encode(padded, features, conv_weight, cpe_linear):
    span_x, span_y, width = features.shape
    shifted = jnp.stack([padded[:, step : step + span_y] for step in range(3)])
    rows = 8
    return pl.pallas_call(
        conv_kernel,
        grid=(span_x // rows,),
        in_specs=[
            pl.BlockSpec(memory_space=pltpu.VMEM),
            pl.BlockSpec((rows, span_y, width), lambda i: (i, 0, 0)),
            pl.BlockSpec(conv_weight.shape, lambda i: (0, 0, 0)),
            pl.BlockSpec(cpe_linear.shape, lambda i: (0, 0)),
        ],
        out_specs=pl.BlockSpec((rows * span_y, width), lambda i: (i, 0)),
        out_shape=jax.ShapeDtypeStruct((span_x * span_y, width), features.dtype),
    )(shifted, features, conv_weight, cpe_linear)


def shards(
    features,
    occupied,
    voxel_order,
    conv_weight,
    cpe_linear,
    qkv_weight,
    proj_weight,
    up_weight,
    down_weight,
):
    span_x, span_y, width = features.shape
    cells = span_x * span_y
    occ_flat = occupied.reshape(cells)
    mine = jnp.sum(occ_flat, dtype=jnp.int32)
    masked = features * occupied[:, :, None].astype(jnp.bfloat16)
    padded = with_halo(masked, (("gx", 0), ("gy", 1)), 1)
    encoded = encode(padded, features, conv_weight, cpe_linear)
    order = voxel_order[0]
    voxel = jnp.arange(cells, dtype=jnp.int32)
    _, rank_of = lax.sort_key_val(order, voxel)
    key = (1 - occ_flat) * cells + rank_of
    _, listed_voxel = lax.sort_key_val(key, voxel)
    capacity = CAP
    list_index = jnp.arange(LIVE + 2 * capacity, dtype=jnp.int32)
    picked = jnp.where(list_index < mine, listed_voxel[: LIVE + 2 * capacity], -1)
    list_rows, counts = gather_counts(mine, encoded, picked)
    devices = counts.shape[0]
    count_x = lax.axis_size("gx")
    count_y = lax.axis_size("gy")
    here_x = lax.axis_index("gx")
    here_y = lax.axis_index("gy")
    ranks = block_curve(count_x, count_y)
    position = ranks[here_x * count_y + here_y]
    by_position = jnp.zeros((devices,), jnp.int32).at[ranks].set(counts)
    starts = jnp.cumsum(by_position, dtype=jnp.int32) - by_position
    start_here = starts[position]
    excess = start_here - position * LIVE
    beyond = start_here + mine - (position + 1) * LIVE
    slot = jnp.arange(capacity, dtype=jnp.int32)
    empty = jnp.zeros((capacity, width), jnp.bfloat16)
    extended = jnp.concatenate([empty, list_rows], axis=0)
    mine_rows = lax.dynamic_slice_in_dim(extended, capacity - excess, LIVE, 0)
    to_prev = jnp.where((slot < -excess)[:, None], list_rows[:capacity], empty)
    to_next = jnp.where(
        (slot < beyond)[:, None], lax.dynamic_slice_in_dim(list_rows, LIVE - excess, capacity, 0), empty
    )
    device_at = curve_tables(count_x, count_y)
    forward = [(device_at[p], device_at[p + 1]) for p in range(devices - 1)]
    backward = [(target, source) for source, target in forward]
    from_prev = lax.ppermute(to_next, ("gx", "gy"), forward)
    from_next = lax.ppermute(to_prev, ("gx", "gy"), backward)
    from_prev = jnp.where((slot < excess)[:, None], from_prev, empty)
    from_next = jnp.where((slot < -beyond)[:, None], from_next, empty)
    leading = jnp.concatenate(
        [from_prev, jnp.zeros((LIVE - capacity, width), jnp.bfloat16)], axis=0
    )
    trailing = lax.dynamic_slice_in_dim(
        jnp.concatenate([jnp.zeros((LIVE, width), jnp.bfloat16), from_next], axis=0),
        -beyond,
        LIVE,
        0,
    )
    owned = mine_rows + leading + trailing
    middle = attention_mid(owned, qkv_weight, proj_weight)
    return feed_forward(middle, up_weight, down_weight)


def solution(mesh):
    return jax.shard_map(
        shards,
        mesh=mesh,
        in_specs=(
            P("gx", "gy", None),
            P("gx", "gy"),
            P(("gx", "gy"), None),
            P(),
            P(),
            P(),
            P(),
            P(),
            P(),
        ),
        out_specs=P(("gx", "gy"), None),
        check_vma=False,
    )
```

```python
import functools
import math

import jax
import numpy as np
import jax.numpy as jnp
from jax import lax
from jax.experimental import pallas as pl
from jax.experimental.pallas import tpu as pltpu
from jax.sharding import PartitionSpec as P

HEADS = 8
PATCH = 1024
LIVE = 2048
CAP = 256
HD = 32


def with_halo(block, sides, width):
    for axis, dim in sides:
        count = lax.axis_size(axis)
        forward = [(i, i + 1) for i in range(count - 1)]
        backward = [(target, source) for source, target in forward]
        low = lax.ppermute(
            lax.slice_in_dim(block, block.shape[dim] - width, None, axis=dim), axis, forward
        )
        high = lax.ppermute(lax.slice_in_dim(block, 0, width, axis=dim), axis, backward)
        block = jnp.concatenate([low, block, high], axis=dim)
    return block


def passed_along(block, axis, distance):
    devices = range(lax.axis_size(axis))
    route = [(i - distance, i) for i in devices if i - distance in devices]
    return lax.ppermute(block, axis, route)


def hilbert_points(side):
    index = jnp.arange(side * side, dtype=jnp.int32)
    coord_x = jnp.zeros((side * side,), jnp.int32)
    coord_y = jnp.zeros((side * side,), jnp.int32)
    remain = index
    level = 1
    while level < side:
        bit_x = remain // 2 % 2
        bit_y = jnp.bitwise_xor(remain, bit_x) % 2
        mirror = (bit_y == 0) & (bit_x == 1)
        moved_x = jnp.where(mirror, level - 1 - coord_x, coord_x)
        moved_y = jnp.where(mirror, level - 1 - coord_y, coord_y)
        turned = bit_y == 0
        coord_x = jnp.where(turned, moved_y, moved_x) + level * bit_x
        coord_y = jnp.where(turned, moved_x, moved_y) + level * bit_y
        remain = remain // 4
        level = level * 2
    return (coord_x, coord_y)


def block_curve(count_x, count_y):
    total = count_x * count_y
    square = count_y * count_y
    position = jnp.arange(total, dtype=jnp.int32)
    half = position // square
    inner_x, inner_y = hilbert_points(count_y)
    along_x = inner_x[position % square] + half * count_y
    along_y = inner_y[position % square]
    device = along_x * count_y + along_y
    return jnp.zeros((total,), jnp.int32).at[device].set(position)


def layer_norm(values):
    centre = values - jnp.mean(values, axis=-1, keepdims=True)
    spread = jnp.mean(centre * centre, axis=-1, keepdims=True)
    return centre * lax.rsqrt(spread + 1e-05)


def attend_patch(rows, qkv_weight, proj_weight, up_weight, down_weight):
    base = rows.astype(jnp.float32)
    normed = layer_norm(base).astype(jnp.bfloat16)
    projected = jnp.dot(normed, qkv_weight, preferred_element_type=jnp.float32).astype(jnp.bfloat16)
    width = rows.shape[1]
    count = rows.shape[0]
    query = projected[:, :width].reshape(count, HEADS, HD)
    keyset = projected[:, width : 2 * width].reshape(count, HEADS, HD)
    valueset = projected[:, 2 * width :].reshape(count, HEADS, HD)
    scores = jnp.einsum("qhd,khd->hqk", query, keyset, preferred_element_type=jnp.float32) * (
        1.0 / math.sqrt(HD)
    )
    largest = jnp.max(scores, axis=-1, keepdims=True)
    expo = jnp.exp(scores - largest)
    weights = (expo / jnp.sum(expo, axis=-1, keepdims=True)).astype(jnp.bfloat16)
    attended = jnp.einsum(
        "hqk,khd->qhd", weights, valueset, preferred_element_type=jnp.float32
    ).astype(jnp.bfloat16)
    middle = base + jnp.dot(
        attended.reshape(count, width), proj_weight, preferred_element_type=jnp.float32
    )
    second = layer_norm(middle).astype(jnp.bfloat16)
    hidden = jax.nn.gelu(
        jnp.dot(second, up_weight, preferred_element_type=jnp.float32), approximate=True
    ).astype(jnp.bfloat16)
    final = middle + jnp.dot(hidden, down_weight, preferred_element_type=jnp.float32)
    return final.astype(jnp.bfloat16)


def onehot_gather_kernel(index_ref, table_ref, out_ref, acc_ref):
    rows = index_ref.shape[0]
    chunk = 512
    wanted = index_ref[...]
    acc_ref[...] = jnp.zeros_like(acc_ref)
    for part in range(table_ref.shape[0] // chunk):
        ids = lax.broadcasted_iota(jnp.int32, (rows, chunk), 1) + part * chunk
        pick = jnp.where(wanted == ids, 1.0, 0.0).astype(jnp.bfloat16)
        acc_ref[...] += jnp.dot(
            pick, table_ref[pl.ds(part * chunk, chunk), :], preferred_element_type=jnp.float32
        )
    out_ref[...] = acc_ref[...].astype(out_ref.dtype)


def onehot_gather(table, index):
    count = index.shape[0]
    width = table.shape[1]
    tile = 256
    return pl.pallas_call(
        onehot_gather_kernel,
        grid=(count // tile,),
        in_specs=[
            pl.BlockSpec((tile, 1), lambda i: (i, 0)),
            pl.BlockSpec(table.shape, lambda i: (0, 0)),
        ],
        out_specs=pl.BlockSpec((tile, width), lambda i: (i, 0)),
        out_shape=jax.ShapeDtypeStruct((count, width), table.dtype),
        scratch_shapes=[pltpu.VMEM((tile, width), jnp.float32)],
    )(index.reshape(count, 1), table)


MESH = pl.DeviceIdType.MESH


def gather_rows(index_ref, table_ref, out_ref, first, last):
    tile = 256
    chunk = 512

    def one_tile(i, carry):
        rows = pl.ds(pl.multiple_of(i * tile, tile), tile)
        wanted = index_ref[rows, :]
        total = jnp.zeros((tile, out_ref.shape[1]), jnp.float32)
        for part in range(table_ref.shape[0] // chunk):
            ids = lax.broadcasted_iota(jnp.int32, (tile, chunk), 1) + part * chunk
            pick = jnp.where(wanted == ids, 1.0, 0.0).astype(jnp.bfloat16)
            total += jnp.dot(
                pick, table_ref[pl.ds(part * chunk, chunk), :], preferred_element_type=jnp.float32
            )
        out_ref[rows, :] = total.astype(out_ref.dtype)
        return carry

    lax.fori_loop(first, last, one_tile, 0)


def count_gather_kernel(nx, index_ref, table_ref, row_ref, rows_ref, out_ref, grid_buf, send2, recv2, own_sem):
    me_x = lax.axis_index("gx")
    me_y = lax.axis_index("gy")
    barrier = pltpu.get_barrier_semaphore()
    for k in range(1, nx):
        pl.semaphore_signal(
            barrier, inc=1, device_id=(lax.rem(me_x + k, nx), me_y), device_id_type=MESH
        )
    pl.semaphore_wait(barrier, nx - 1)
    own = pltpu.make_async_copy(row_ref, grid_buf.at[me_x], own_sem.at[0])
    own.start()
    for k in range(1, nx):
        pltpu.make_async_remote_copy(
            src_ref=row_ref,
            dst_ref=grid_buf.at[me_x],
            send_sem=send2.at[k],
            recv_sem=recv2.at[k],
            device_id=(lax.rem(me_x + k, nx), me_y),
            device_id_type=MESH,
        ).start()
    gather_rows(index_ref, table_ref, rows_ref, 0, rows_ref.shape[0] // 256)
    own.wait()
    for k in range(1, nx):
        sender = lax.rem(me_x - k + nx, nx)
        copy = pltpu.make_async_remote_copy(
            src_ref=row_ref,
            dst_ref=grid_buf.at[sender],
            send_sem=send2.at[k],
            recv_sem=recv2.at[k],
            device_id=(sender, me_y),
            device_id_type=MESH,
        )
        copy.wait_send()
        copy.wait_recv()
    out_ref[...] = grid_buf[...]


def gather_counts(row, table, index):
    nx = lax.axis_size("gx")
    ny, lanes = row.shape
    listed, grid = pl.pallas_call(
        functools.partial(count_gather_kernel, nx),
        out_shape=(
            jax.ShapeDtypeStruct((index.shape[0], table.shape[1]), table.dtype),
            jax.ShapeDtypeStruct((nx, ny, lanes), jnp.int32),
        ),
        in_specs=[pl.BlockSpec(memory_space=pltpu.VMEM)] * 3,
        out_specs=(pl.BlockSpec(memory_space=pltpu.VMEM), pl.BlockSpec(memory_space=pltpu.VMEM)),
        scratch_shapes=[
            pltpu.VMEM((nx, ny, lanes), jnp.int32),
            pltpu.SemaphoreType.DMA((nx,)),
            pltpu.SemaphoreType.DMA((nx,)),
            pltpu.SemaphoreType.DMA((1,)),
        ],
        compiler_params=pltpu.CompilerParams(collective_id=0, has_side_effects=True),
    )(index.reshape(-1, 1), table, row)
    return listed, grid[:, :, 0].reshape(nx * ny)


def attention_kernel(q_ref, k_ref, v_ref, base_ref, proj_ref, out_ref):
    query = q_ref[...]
    keyset = k_ref[...]
    valueset = v_ref[...]
    width = query.shape[1]
    head_of = lax.broadcasted_iota(jnp.int32, (1, width), 1) // HD
    attended = jnp.zeros((query.shape[0], width), jnp.float32)
    for head in range(HEADS):
        mine = head_of == head
        scores = lax.dot_general(
            jnp.where(mine, query, jnp.zeros_like(query)),
            keyset,
            (((1,), (1,)), ((), ())),
            preferred_element_type=jnp.float32,
        ) * (1.0 / math.sqrt(HD))
        largest = jnp.max(scores, axis=-1, keepdims=True)
        expo = jnp.exp(scores - largest)
        weights = (expo * (1.0 / jnp.sum(expo, axis=-1, keepdims=True))).astype(jnp.bfloat16)
        mixed = jnp.dot(weights, valueset, preferred_element_type=jnp.float32)
        attended = jnp.where(mine, mixed, attended)
    out_ref[...] = base_ref[...].astype(jnp.float32) + jnp.dot(
        attended.astype(jnp.bfloat16), proj_ref[...], preferred_element_type=jnp.float32
    )


def attention_mid(rows, qkv_weight, proj_weight):
    count, width = rows.shape
    base = rows.astype(jnp.float32)
    normed = layer_norm(base).astype(jnp.bfloat16)
    projected = jnp.dot(normed, qkv_weight, preferred_element_type=jnp.float32).astype(jnp.bfloat16)
    tile = 256
    tiles = PATCH // tile
    grid = (count // PATCH, tiles)
    return pl.pallas_call(
        attention_kernel,
        grid=grid,
        in_specs=[
            pl.BlockSpec((tile, width), lambda p, t: (p * tiles + t, 0)),
            pl.BlockSpec((PATCH, width), lambda p, t: (p, 1)),
            pl.BlockSpec((PATCH, width), lambda p, t: (p, 2)),
            pl.BlockSpec((tile, width), lambda p, t: (p * tiles + t, 0)),
            pl.BlockSpec((width, width), lambda p, t: (0, 0)),
        ],
        out_specs=pl.BlockSpec((tile, width), lambda p, t: (p * tiles + t, 0)),
        out_shape=jax.ShapeDtypeStruct((count, width), jnp.float32),
    )(projected, projected, projected, rows, proj_weight)


def feed_forward(middle, up_weight, down_weight):
    second = layer_norm(middle).astype(jnp.bfloat16)
    hidden = jax.nn.gelu(
        jnp.dot(second, up_weight, preferred_element_type=jnp.float32), approximate=True
    ).astype(jnp.bfloat16)
    final = middle + jnp.dot(hidden, down_weight, preferred_element_type=jnp.float32)
    return final.astype(jnp.bfloat16)


def curve_tables(count_x, count_y):
    square = count_y * count_y
    index = np.arange(square)
    coord_x = np.zeros(square, np.int64)
    coord_y = np.zeros(square, np.int64)
    remain = index.copy()
    level = 1
    while level < count_y:
        bit_x = remain // 2 % 2
        bit_y = np.bitwise_xor(remain, bit_x) % 2
        mirror = (bit_y == 0) & (bit_x == 1)
        moved_x = np.where(mirror, level - 1 - coord_x, coord_x)
        moved_y = np.where(mirror, level - 1 - coord_y, coord_y)
        turned = bit_y == 0
        coord_x = np.where(turned, moved_y, moved_x) + level * bit_x
        coord_y = np.where(turned, moved_x, moved_y) + level * bit_y
        remain = remain // 4
        level = level * 2
    position = np.arange(count_x * count_y)
    along_x = coord_x[position % square] + (position // square) * count_y
    along_y = coord_y[position % square]
    return [int(d) for d in along_x * count_y + along_y]


def conv_kernel(ny, shifted_ref, features_ref, weight_ref, linear_ref, mine_ref, out_ref, row_out, row_buf, send1, recv1, own_sem):
    me_x = lax.axis_index("gx")
    me_y = lax.axis_index("gy")
    step = pl.program_id(0)

    @pl.when(step == 0)
    def _():
        barrier = pltpu.get_barrier_semaphore()
        for k in range(1, ny):
            pl.semaphore_signal(
                barrier, inc=1, device_id=(me_x, lax.rem(me_y + k, ny)), device_id_type=MESH
            )
        pl.semaphore_wait(barrier, ny - 1)
        pltpu.make_async_copy(mine_ref, row_buf.at[pl.ds(me_y, 1)], own_sem.at[0]).start()
        for k in range(1, ny):
            pltpu.make_async_remote_copy(
                src_ref=mine_ref,
                dst_ref=row_buf.at[pl.ds(me_y, 1)],
                send_sem=send1.at[k],
                recv_sem=recv1.at[k],
                device_id=(me_x, lax.rem(me_y + k, ny)),
                device_id_type=MESH,
            ).start()

    rows = features_ref.shape[0]
    side = shifted_ref.shape[2]
    width = features_ref.shape[-1]
    first = pl.program_id(0) * rows
    total = jnp.zeros((rows * side, width), jnp.float32)
    for offset in range(9):
        step_x = offset // 3
        step_y = offset % 3
        window = shifted_ref[step_y, pl.ds(first + step_x, rows)].reshape(rows * side, width)
        total += jnp.dot(window, weight_ref[offset], preferred_element_type=jnp.float32)
    linear = jnp.dot(total.astype(jnp.bfloat16), linear_ref[...], preferred_element_type=jnp.float32)
    base = features_ref[...].reshape(rows * side, width).astype(jnp.float32)
    out_ref[...] = (base + layer_norm(linear)).astype(out_ref.dtype)

    @pl.when(step == pl.num_programs(0) - 1)
    def _():
        pltpu.make_async_copy(mine_ref, row_buf.at[pl.ds(me_y, 1)], own_sem.at[0]).wait()
        for k in range(1, ny):
            sender = lax.rem(me_y - k + ny, ny)
            copy = pltpu.make_async_remote_copy(
                src_ref=mine_ref,
                dst_ref=row_buf.at[pl.ds(sender, 1)],
                send_sem=send1.at[k],
                recv_sem=recv1.at[k],
                device_id=(me_x, sender),
                device_id_type=MESH,
            )
            copy.wait_send()
            copy.wait_recv()
        row_out[...] = row_buf[...]


def encode(padded, features, conv_weight, cpe_linear, mine):
    span_x, span_y, width = features.shape
    shifted = jnp.stack([padded[:, step : step + span_y] for step in range(3)])
    rows = 8
    ny = lax.axis_size("gy")
    lanes = 128
    return pl.pallas_call(
        functools.partial(conv_kernel, ny),
        grid=(span_x // rows,),
        in_specs=[
            pl.BlockSpec(memory_space=pltpu.VMEM),
            pl.BlockSpec((rows, span_y, width), lambda i: (i, 0, 0)),
            pl.BlockSpec(conv_weight.shape, lambda i: (0, 0, 0)),
            pl.BlockSpec(cpe_linear.shape, lambda i: (0, 0)),
            pl.BlockSpec((1, lanes), lambda i: (0, 0)),
        ],
        out_specs=(
            pl.BlockSpec((rows * span_y, width), lambda i: (i, 0)),
            pl.BlockSpec((ny, lanes), lambda i: (0, 0)),
        ),
        out_shape=(
            jax.ShapeDtypeStruct((span_x * span_y, width), features.dtype),
            jax.ShapeDtypeStruct((ny, lanes), jnp.int32),
        ),
        scratch_shapes=[
            pltpu.VMEM((ny, lanes), jnp.int32),
            pltpu.SemaphoreType.DMA((ny,)),
            pltpu.SemaphoreType.DMA((ny,)),
            pltpu.SemaphoreType.DMA((1,)),
        ],
        compiler_params=pltpu.CompilerParams(collective_id=1, has_side_effects=True),
    )(shifted, features, conv_weight, cpe_linear, jnp.broadcast_to(mine, (1, lanes)))


def shards(
    features,
    occupied,
    voxel_order,
    conv_weight,
    cpe_linear,
    qkv_weight,
    proj_weight,
    up_weight,
    down_weight,
):
    span_x, span_y, width = features.shape
    cells = span_x * span_y
    occ_flat = occupied.reshape(cells)
    mine = jnp.sum(occ_flat, dtype=jnp.int32)
    masked = features * occupied[:, :, None].astype(jnp.bfloat16)
    padded = with_halo(masked, (("gx", 0), ("gy", 1)), 1)
    encoded, row_counts = encode(padded, features, conv_weight, cpe_linear, mine)
    order = voxel_order[0]
    voxel = jnp.arange(cells, dtype=jnp.int32)
    _, rank_of = lax.sort_key_val(order, voxel)
    key = (1 - occ_flat) * cells + rank_of
    _, listed_voxel = lax.sort_key_val(key, voxel)
    capacity = CAP
    list_index = jnp.arange(LIVE + 2 * capacity, dtype=jnp.int32)
    picked = jnp.where(list_index < mine, listed_voxel[: LIVE + 2 * capacity], -1)
    list_rows, counts = gather_counts(row_counts, encoded, picked)
    devices = counts.shape[0]
    count_x = lax.axis_size("gx")
    count_y = lax.axis_size("gy")
    here_x = lax.axis_index("gx")
    here_y = lax.axis_index("gy")
    ranks = block_curve(count_x, count_y)
    position = ranks[here_x * count_y + here_y]
    by_position = jnp.zeros((devices,), jnp.int32).at[ranks].set(counts)
    starts = jnp.cumsum(by_position, dtype=jnp.int32) - by_position
    start_here = starts[position]
    excess = start_here - position * LIVE
    beyond = start_here + mine - (position + 1) * LIVE
    slot = jnp.arange(capacity, dtype=jnp.int32)
    empty = jnp.zeros((capacity, width), jnp.bfloat16)
    extended = jnp.concatenate([empty, list_rows], axis=0)
    mine_rows = lax.dynamic_slice_in_dim(extended, capacity - excess, LIVE, 0)
    to_prev = jnp.where((slot < -excess)[:, None], list_rows[:capacity], empty)
    to_next = jnp.where(
        (slot < beyond)[:, None], lax.dynamic_slice_in_dim(list_rows, LIVE - excess, capacity, 0), empty
    )
    device_at = curve_tables(count_x, count_y)
    forward = [(device_at[p], device_at[p + 1]) for p in range(devices - 1)]
    backward = [(target, source) for source, target in forward]
    from_prev = lax.ppermute(to_next, ("gx", "gy"), forward)
    from_next = lax.ppermute(to_prev, ("gx", "gy"), backward)
    from_prev = jnp.where((slot < excess)[:, None], from_prev, empty)
    from_next = jnp.where((slot < -beyond)[:, None], from_next, empty)
    leading = jnp.concatenate(
        [from_prev, jnp.zeros((LIVE - capacity, width), jnp.bfloat16)], axis=0
    )
    trailing = lax.dynamic_slice_in_dim(
        jnp.concatenate([jnp.zeros((LIVE, width), jnp.bfloat16), from_next], axis=0),
        -beyond,
        LIVE,
        0,
    )
    owned = mine_rows + leading + trailing
    middle = attention_mid(owned, qkv_weight, proj_weight)
    return feed_forward(middle, up_weight, down_weight)


def solution(mesh):
    return jax.shard_map(
        shards,
        mesh=mesh,
        in_specs=(
            P("gx", "gy", None),
            P("gx", "gy"),
            P(("gx", "gy"), None),
            P(),
            P(),
            P(),
            P(),
            P(),
            P(),
        ),
        out_specs=P(("gx", "gy"), None),
        check_vma=False,
    )
```

```python
import functools
import math

import jax
import numpy as np
import jax.numpy as jnp
from jax import lax
from jax.experimental import pallas as pl
from jax.experimental.pallas import tpu as pltpu
from jax.sharding import PartitionSpec as P

HEADS = 8
PATCH = 1024
LIVE = 2048
CAP = 256
HD = 32


def with_halo(block, sides, width):
    for axis, dim in sides:
        count = lax.axis_size(axis)
        forward = [(i, i + 1) for i in range(count - 1)]
        backward = [(target, source) for source, target in forward]
        low = lax.ppermute(
            lax.slice_in_dim(block, block.shape[dim] - width, None, axis=dim), axis, forward
        )
        high = lax.ppermute(lax.slice_in_dim(block, 0, width, axis=dim), axis, backward)
        block = jnp.concatenate([low, block, high], axis=dim)
    return block


def passed_along(block, axis, distance):
    devices = range(lax.axis_size(axis))
    route = [(i - distance, i) for i in devices if i - distance in devices]
    return lax.ppermute(block, axis, route)


def hilbert_points(side):
    index = jnp.arange(side * side, dtype=jnp.int32)
    coord_x = jnp.zeros((side * side,), jnp.int32)
    coord_y = jnp.zeros((side * side,), jnp.int32)
    remain = index
    level = 1
    while level < side:
        bit_x = remain // 2 % 2
        bit_y = jnp.bitwise_xor(remain, bit_x) % 2
        mirror = (bit_y == 0) & (bit_x == 1)
        moved_x = jnp.where(mirror, level - 1 - coord_x, coord_x)
        moved_y = jnp.where(mirror, level - 1 - coord_y, coord_y)
        turned = bit_y == 0
        coord_x = jnp.where(turned, moved_y, moved_x) + level * bit_x
        coord_y = jnp.where(turned, moved_x, moved_y) + level * bit_y
        remain = remain // 4
        level = level * 2
    return (coord_x, coord_y)


def block_curve(count_x, count_y):
    total = count_x * count_y
    square = count_y * count_y
    position = jnp.arange(total, dtype=jnp.int32)
    half = position // square
    inner_x, inner_y = hilbert_points(count_y)
    along_x = inner_x[position % square] + half * count_y
    along_y = inner_y[position % square]
    device = along_x * count_y + along_y
    return jnp.zeros((total,), jnp.int32).at[device].set(position)


def layer_norm(values):
    centre = values - jnp.mean(values, axis=-1, keepdims=True)
    spread = jnp.mean(centre * centre, axis=-1, keepdims=True)
    return centre * lax.rsqrt(spread + 1e-05)


def attend_patch(rows, qkv_weight, proj_weight, up_weight, down_weight):
    base = rows.astype(jnp.float32)
    normed = layer_norm(base).astype(jnp.bfloat16)
    projected = jnp.dot(normed, qkv_weight, preferred_element_type=jnp.float32).astype(jnp.bfloat16)
    width = rows.shape[1]
    count = rows.shape[0]
    query = projected[:, :width].reshape(count, HEADS, HD)
    keyset = projected[:, width : 2 * width].reshape(count, HEADS, HD)
    valueset = projected[:, 2 * width :].reshape(count, HEADS, HD)
    scores = jnp.einsum("qhd,khd->hqk", query, keyset, preferred_element_type=jnp.float32) * (
        1.0 / math.sqrt(HD)
    )
    largest = jnp.max(scores, axis=-1, keepdims=True)
    expo = jnp.exp(scores - largest)
    weights = (expo / jnp.sum(expo, axis=-1, keepdims=True)).astype(jnp.bfloat16)
    attended = jnp.einsum(
        "hqk,khd->qhd", weights, valueset, preferred_element_type=jnp.float32
    ).astype(jnp.bfloat16)
    middle = base + jnp.dot(
        attended.reshape(count, width), proj_weight, preferred_element_type=jnp.float32
    )
    second = layer_norm(middle).astype(jnp.bfloat16)
    hidden = jax.nn.gelu(
        jnp.dot(second, up_weight, preferred_element_type=jnp.float32), approximate=True
    ).astype(jnp.bfloat16)
    final = middle + jnp.dot(hidden, down_weight, preferred_element_type=jnp.float32)
    return final.astype(jnp.bfloat16)


def onehot_gather_kernel(index_ref, table_ref, out_ref, acc_ref):
    rows = index_ref.shape[0]
    chunk = 512
    wanted = index_ref[...]
    acc_ref[...] = jnp.zeros_like(acc_ref)
    for part in range(table_ref.shape[0] // chunk):
        ids = lax.broadcasted_iota(jnp.int32, (rows, chunk), 1) + part * chunk
        pick = jnp.where(wanted == ids, 1.0, 0.0).astype(jnp.bfloat16)
        acc_ref[...] += jnp.dot(
            pick, table_ref[pl.ds(part * chunk, chunk), :], preferred_element_type=jnp.float32
        )
    out_ref[...] = acc_ref[...].astype(out_ref.dtype)


def onehot_gather(table, index):
    count = index.shape[0]
    width = table.shape[1]
    tile = 256
    return pl.pallas_call(
        onehot_gather_kernel,
        grid=(count // tile,),
        in_specs=[
            pl.BlockSpec((tile, 1), lambda i: (i, 0)),
            pl.BlockSpec(table.shape, lambda i: (0, 0)),
        ],
        out_specs=pl.BlockSpec((tile, width), lambda i: (i, 0)),
        out_shape=jax.ShapeDtypeStruct((count, width), table.dtype),
        scratch_shapes=[pltpu.VMEM((tile, width), jnp.float32)],
    )(index.reshape(count, 1), table)


MESH = pl.DeviceIdType.MESH


def gather_rows(index_ref, table_ref, out_ref, first, last):
    tile = 256
    chunk = 512

    def one_tile(i, carry):
        rows = pl.ds(pl.multiple_of(i * tile, tile), tile)
        wanted = index_ref[rows, :]
        total = jnp.zeros((tile, out_ref.shape[1]), jnp.float32)
        for part in range(table_ref.shape[0] // chunk):
            ids = lax.broadcasted_iota(jnp.int32, (tile, chunk), 1) + part * chunk
            pick = jnp.where(wanted == ids, 1.0, 0.0).astype(jnp.bfloat16)
            total += jnp.dot(
                pick, table_ref[pl.ds(part * chunk, chunk), :], preferred_element_type=jnp.float32
            )
        out_ref[rows, :] = total.astype(out_ref.dtype)
        return carry

    lax.fori_loop(first, last, one_tile, 0)


def count_gather_kernel(nx, ny, index_ref, table_ref, mine_ref, rows_ref, out_ref, row_buf, grid_buf, send1, recv1, send2, recv2, own_sem):
    me_x = lax.axis_index("gx")
    me_y = lax.axis_index("gy")
    barrier = pltpu.get_barrier_semaphore()
    for k in range(1, ny):
        pl.semaphore_signal(
            barrier, inc=1, device_id=(me_x, lax.rem(me_y + k, ny)), device_id_type=MESH
        )
    for k in range(1, nx):
        pl.semaphore_signal(
            barrier, inc=1, device_id=(lax.rem(me_x + k, nx), me_y), device_id_type=MESH
        )
    pl.semaphore_wait(barrier, nx + ny - 2)

    own = pltpu.make_async_copy(mine_ref, row_buf.at[pl.ds(me_y, 1)], own_sem.at[0])
    own.start()
    for k in range(1, ny):
        pltpu.make_async_remote_copy(
            src_ref=mine_ref,
            dst_ref=row_buf.at[pl.ds(me_y, 1)],
            send_sem=send1.at[k],
            recv_sem=recv1.at[k],
            device_id=(me_x, lax.rem(me_y + k, ny)),
            device_id_type=MESH,
        ).start()
    tiles = rows_ref.shape[0] // 256
    gather_rows(index_ref, table_ref, rows_ref, 0, tiles // 2)
    own.wait()
    for k in range(1, ny):
        sender = lax.rem(me_y - k + ny, ny)
        copy = pltpu.make_async_remote_copy(
            src_ref=mine_ref,
            dst_ref=row_buf.at[pl.ds(sender, 1)],
            send_sem=send1.at[k],
            recv_sem=recv1.at[k],
            device_id=(me_x, sender),
            device_id_type=MESH,
        )
        copy.wait_send()
        copy.wait_recv()

    own = pltpu.make_async_copy(row_buf, grid_buf.at[me_x], own_sem.at[1])
    own.start()
    for k in range(1, nx):
        pltpu.make_async_remote_copy(
            src_ref=row_buf,
            dst_ref=grid_buf.at[me_x],
            send_sem=send2.at[k],
            recv_sem=recv2.at[k],
            device_id=(lax.rem(me_x + k, nx), me_y),
            device_id_type=MESH,
        ).start()
    gather_rows(index_ref, table_ref, rows_ref, tiles // 2, tiles)
    own.wait()
    for k in range(1, nx):
        sender = lax.rem(me_x - k + nx, nx)
        copy = pltpu.make_async_remote_copy(
            src_ref=row_buf,
            dst_ref=grid_buf.at[sender],
            send_sem=send2.at[k],
            recv_sem=recv2.at[k],
            device_id=(sender, me_y),
            device_id_type=MESH,
        )
        copy.wait_send()
        copy.wait_recv()
    out_ref[...] = grid_buf[...]


def gather_counts(mine, table, index):
    nx = lax.axis_size("gx")
    ny = lax.axis_size("gy")
    lanes = 128
    listed, grid = pl.pallas_call(
        functools.partial(count_gather_kernel, nx, ny),
        out_shape=(
            jax.ShapeDtypeStruct((index.shape[0], table.shape[1]), table.dtype),
            jax.ShapeDtypeStruct((nx, ny, lanes), jnp.int32),
        ),
        in_specs=[pl.BlockSpec(memory_space=pltpu.VMEM)] * 3,
        out_specs=(pl.BlockSpec(memory_space=pltpu.VMEM), pl.BlockSpec(memory_space=pltpu.VMEM)),
        scratch_shapes=[
            pltpu.VMEM((ny, lanes), jnp.int32),
            pltpu.VMEM((nx, ny, lanes), jnp.int32),
            pltpu.SemaphoreType.DMA((ny,)),
            pltpu.SemaphoreType.DMA((ny,)),
            pltpu.SemaphoreType.DMA((nx,)),
            pltpu.SemaphoreType.DMA((nx,)),
            pltpu.SemaphoreType.DMA((2,)),
        ],
        compiler_params=pltpu.CompilerParams(collective_id=0, has_side_effects=True),
    )(index.reshape(-1, 1), table, jnp.broadcast_to(mine, (1, lanes)))
    return listed, grid[:, :, 0].reshape(nx * ny)


def attention_kernel(q_ref, k_ref, v_ref, base_ref, proj_ref, out_ref):
    query = q_ref[...]
    keyset = k_ref[...]
    valueset = v_ref[...]
    width = query.shape[1]
    head_of = lax.broadcasted_iota(jnp.int32, (1, width), 1) // HD
    attended = jnp.zeros((query.shape[0], width), jnp.float32)
    for head in range(HEADS):
        mine = head_of == head
        scores = lax.dot_general(
            jnp.where(mine, query, jnp.zeros_like(query)),
            keyset,
            (((1,), (1,)), ((), ())),
            preferred_element_type=jnp.float32,
        ) * (1.0 / math.sqrt(HD))
        largest = jnp.max(scores, axis=-1, keepdims=True)
        expo = jnp.exp(scores - largest)
        scale = 1.0 / jnp.sum(expo, axis=-1, keepdims=True)
        mixed = jnp.dot(expo.astype(jnp.bfloat16), valueset, preferred_element_type=jnp.float32)
        attended = jnp.where(mine, mixed * scale, attended)
    out_ref[...] = base_ref[...].astype(jnp.float32) + jnp.dot(
        attended.astype(jnp.bfloat16), proj_ref[...], preferred_element_type=jnp.float32
    )


def attention_mid(rows, qkv_weight, proj_weight):
    count, width = rows.shape
    base = rows.astype(jnp.float32)
    normed = layer_norm(base).astype(jnp.bfloat16)
    projected = jnp.dot(normed, qkv_weight, preferred_element_type=jnp.float32).astype(jnp.bfloat16)
    tile = 256
    tiles = PATCH // tile
    grid = (count // PATCH, tiles)
    return pl.pallas_call(
        attention_kernel,
        grid=grid,
        in_specs=[
            pl.BlockSpec((tile, width), lambda p, t: (p * tiles + t, 0)),
            pl.BlockSpec((PATCH, width), lambda p, t: (p, 1)),
            pl.BlockSpec((PATCH, width), lambda p, t: (p, 2)),
            pl.BlockSpec((tile, width), lambda p, t: (p * tiles + t, 0)),
            pl.BlockSpec((width, width), lambda p, t: (0, 0)),
        ],
        out_specs=pl.BlockSpec((tile, width), lambda p, t: (p * tiles + t, 0)),
        out_shape=jax.ShapeDtypeStruct((count, width), jnp.float32),
    )(projected, projected, projected, rows, proj_weight)


def feed_forward(middle, up_weight, down_weight):
    second = layer_norm(middle).astype(jnp.bfloat16)
    hidden = jax.nn.gelu(
        jnp.dot(second, up_weight, preferred_element_type=jnp.float32), approximate=True
    ).astype(jnp.bfloat16)
    final = middle + jnp.dot(hidden, down_weight, preferred_element_type=jnp.float32)
    return final.astype(jnp.bfloat16)


def curve_tables(count_x, count_y):
    square = count_y * count_y
    index = np.arange(square)
    coord_x = np.zeros(square, np.int64)
    coord_y = np.zeros(square, np.int64)
    remain = index.copy()
    level = 1
    while level < count_y:
        bit_x = remain // 2 % 2
        bit_y = np.bitwise_xor(remain, bit_x) % 2
        mirror = (bit_y == 0) & (bit_x == 1)
        moved_x = np.where(mirror, level - 1 - coord_x, coord_x)
        moved_y = np.where(mirror, level - 1 - coord_y, coord_y)
        turned = bit_y == 0
        coord_x = np.where(turned, moved_y, moved_x) + level * bit_x
        coord_y = np.where(turned, moved_x, moved_y) + level * bit_y
        remain = remain // 4
        level = level * 2
    position = np.arange(count_x * count_y)
    along_x = coord_x[position % square] + (position // square) * count_y
    along_y = coord_y[position % square]
    return [int(d) for d in along_x * count_y + along_y]


def conv_kernel(shifted_ref, features_ref, weight_ref, linear_ref, out_ref):
    rows = features_ref.shape[0]
    side = shifted_ref.shape[2]
    width = features_ref.shape[-1]
    first = pl.program_id(0) * rows
    total = jnp.zeros((rows * side, width), jnp.float32)
    for offset in range(9):
        step_x = offset // 3
        step_y = offset % 3
        window = shifted_ref[step_y, pl.ds(first + step_x, rows)].reshape(rows * side, width)
        total += jnp.dot(window, weight_ref[offset], preferred_element_type=jnp.float32)
    linear = jnp.dot(total.astype(jnp.bfloat16), linear_ref[...], preferred_element_type=jnp.float32)
    base = features_ref[...].reshape(rows * side, width).astype(jnp.float32)
    out_ref[...] = (base + layer_norm(linear)).astype(out_ref.dtype)


def encode(padded, features, conv_weight, cpe_linear):
    span_x, span_y, width = features.shape
    shifted = jnp.stack([padded[:, step : step + span_y] for step in range(3)])
    rows = 8
    return pl.pallas_call(
        conv_kernel,
        grid=(span_x // rows,),
        in_specs=[
            pl.BlockSpec(memory_space=pltpu.VMEM),
            pl.BlockSpec((rows, span_y, width), lambda i: (i, 0, 0)),
            pl.BlockSpec(conv_weight.shape, lambda i: (0, 0, 0)),
            pl.BlockSpec(cpe_linear.shape, lambda i: (0, 0)),
        ],
        out_specs=pl.BlockSpec((rows * span_y, width), lambda i: (i, 0)),
        out_shape=jax.ShapeDtypeStruct((span_x * span_y, width), features.dtype),
    )(shifted, features, conv_weight, cpe_linear)


def shards(
    features,
    occupied,
    voxel_order,
    conv_weight,
    cpe_linear,
    qkv_weight,
    proj_weight,
    up_weight,
    down_weight,
):
    span_x, span_y, width = features.shape
    cells = span_x * span_y
    occ_flat = occupied.reshape(cells)
    mine = jnp.sum(occ_flat, dtype=jnp.int32)
    masked = features * occupied[:, :, None].astype(jnp.bfloat16)
    padded = with_halo(masked, (("gx", 0), ("gy", 1)), 1)
    encoded = encode(padded, features, conv_weight, cpe_linear)
    order = voxel_order[0]
    voxel = jnp.arange(cells, dtype=jnp.int32)
    _, rank_of = lax.sort_key_val(order, voxel)
    key = (1 - occ_flat) * cells + rank_of
    _, listed_voxel = lax.sort_key_val(key, voxel)
    capacity = CAP
    list_index = jnp.arange(LIVE + 2 * capacity, dtype=jnp.int32)
    picked = jnp.where(list_index < mine, listed_voxel[: LIVE + 2 * capacity], -1)
    list_rows, counts = gather_counts(mine, encoded, picked)
    devices = counts.shape[0]
    count_x = lax.axis_size("gx")
    count_y = lax.axis_size("gy")
    here_x = lax.axis_index("gx")
    here_y = lax.axis_index("gy")
    ranks = block_curve(count_x, count_y)
    position = ranks[here_x * count_y + here_y]
    by_position = jnp.zeros((devices,), jnp.int32).at[ranks].set(counts)
    starts = jnp.cumsum(by_position, dtype=jnp.int32) - by_position
    start_here = starts[position]
    excess = start_here - position * LIVE
    beyond = start_here + mine - (position + 1) * LIVE
    slot = jnp.arange(capacity, dtype=jnp.int32)
    empty = jnp.zeros((capacity, width), jnp.bfloat16)
    extended = jnp.concatenate([empty, list_rows], axis=0)
    mine_rows = lax.dynamic_slice_in_dim(extended, capacity - excess, LIVE, 0)
    to_prev = jnp.where((slot < -excess)[:, None], list_rows[:capacity], empty)
    to_next = jnp.where(
        (slot < beyond)[:, None], lax.dynamic_slice_in_dim(list_rows, LIVE - excess, capacity, 0), empty
    )
    device_at = curve_tables(count_x, count_y)
    forward = [(device_at[p], device_at[p + 1]) for p in range(devices - 1)]
    backward = [(target, source) for source, target in forward]
    from_prev = lax.ppermute(to_next, ("gx", "gy"), forward)
    from_next = lax.ppermute(to_prev, ("gx", "gy"), backward)
    from_prev = jnp.where((slot < excess)[:, None], from_prev, empty)
    from_next = jnp.where((slot < -beyond)[:, None], from_next, empty)
    leading = jnp.concatenate(
        [from_prev, jnp.zeros((LIVE - capacity, width), jnp.bfloat16)], axis=0
    )
    trailing = lax.dynamic_slice_in_dim(
        jnp.concatenate([jnp.zeros((LIVE, width), jnp.bfloat16), from_next], axis=0),
        -beyond,
        LIVE,
        0,
    )
    owned = mine_rows + leading + trailing
    middle = attention_mid(owned, qkv_weight, proj_weight)
    return feed_forward(middle, up_weight, down_weight)


def solution(mesh):
    return jax.shard_map(
        shards,
        mesh=mesh,
        in_specs=(
            P("gx", "gy", None),
            P("gx", "gy"),
            P(("gx", "gy"), None),
            P(),
            P(),
            P(),
            P(),
            P(),
            P(),
        ),
        out_specs=P(("gx", "gy"), None),
        check_vma=False,
    )
```

```python
import functools
import math

import jax
import numpy as np
import jax.numpy as jnp
from jax import lax
from jax.experimental import pallas as pl
from jax.experimental.pallas import tpu as pltpu
from jax.sharding import PartitionSpec as P

HEADS = 8
PATCH = 1024
LIVE = 2048
CAP = 256
HD = 32


def with_halo(block, sides, width):
    for axis, dim in sides:
        count = lax.axis_size(axis)
        forward = [(i, i + 1) for i in range(count - 1)]
        backward = [(target, source) for source, target in forward]
        low = lax.ppermute(
            lax.slice_in_dim(block, block.shape[dim] - width, None, axis=dim), axis, forward
        )
        high = lax.ppermute(lax.slice_in_dim(block, 0, width, axis=dim), axis, backward)
        block = jnp.concatenate([low, block, high], axis=dim)
    return block


def passed_along(block, axis, distance):
    devices = range(lax.axis_size(axis))
    route = [(i - distance, i) for i in devices if i - distance in devices]
    return lax.ppermute(block, axis, route)


def hilbert_points(side):
    index = jnp.arange(side * side, dtype=jnp.int32)
    coord_x = jnp.zeros((side * side,), jnp.int32)
    coord_y = jnp.zeros((side * side,), jnp.int32)
    remain = index
    level = 1
    while level < side:
        bit_x = remain // 2 % 2
        bit_y = jnp.bitwise_xor(remain, bit_x) % 2
        mirror = (bit_y == 0) & (bit_x == 1)
        moved_x = jnp.where(mirror, level - 1 - coord_x, coord_x)
        moved_y = jnp.where(mirror, level - 1 - coord_y, coord_y)
        turned = bit_y == 0
        coord_x = jnp.where(turned, moved_y, moved_x) + level * bit_x
        coord_y = jnp.where(turned, moved_x, moved_y) + level * bit_y
        remain = remain // 4
        level = level * 2
    return (coord_x, coord_y)


def block_curve(count_x, count_y):
    total = count_x * count_y
    square = count_y * count_y
    position = jnp.arange(total, dtype=jnp.int32)
    half = position // square
    inner_x, inner_y = hilbert_points(count_y)
    along_x = inner_x[position % square] + half * count_y
    along_y = inner_y[position % square]
    device = along_x * count_y + along_y
    return jnp.zeros((total,), jnp.int32).at[device].set(position)


def layer_norm(values):
    centre = values - jnp.mean(values, axis=-1, keepdims=True)
    spread = jnp.mean(centre * centre, axis=-1, keepdims=True)
    return centre * lax.rsqrt(spread + 1e-05)


def attend_patch(rows, qkv_weight, proj_weight, up_weight, down_weight):
    base = rows.astype(jnp.float32)
    normed = layer_norm(base).astype(jnp.bfloat16)
    projected = jnp.dot(normed, qkv_weight, preferred_element_type=jnp.float32).astype(jnp.bfloat16)
    width = rows.shape[1]
    count = rows.shape[0]
    query = projected[:, :width].reshape(count, HEADS, HD)
    keyset = projected[:, width : 2 * width].reshape(count, HEADS, HD)
    valueset = projected[:, 2 * width :].reshape(count, HEADS, HD)
    scores = jnp.einsum("qhd,khd->hqk", query, keyset, preferred_element_type=jnp.float32) * (
        1.0 / math.sqrt(HD)
    )
    largest = jnp.max(scores, axis=-1, keepdims=True)
    expo = jnp.exp(scores - largest)
    weights = (expo / jnp.sum(expo, axis=-1, keepdims=True)).astype(jnp.bfloat16)
    attended = jnp.einsum(
        "hqk,khd->qhd", weights, valueset, preferred_element_type=jnp.float32
    ).astype(jnp.bfloat16)
    middle = base + jnp.dot(
        attended.reshape(count, width), proj_weight, preferred_element_type=jnp.float32
    )
    second = layer_norm(middle).astype(jnp.bfloat16)
    hidden = jax.nn.gelu(
        jnp.dot(second, up_weight, preferred_element_type=jnp.float32), approximate=True
    ).astype(jnp.bfloat16)
    final = middle + jnp.dot(hidden, down_weight, preferred_element_type=jnp.float32)
    return final.astype(jnp.bfloat16)


def onehot_gather_kernel(index_ref, table_ref, out_ref, acc_ref):
    rows = index_ref.shape[0]
    chunk = 512
    wanted = index_ref[...]
    acc_ref[...] = jnp.zeros_like(acc_ref)
    for part in range(table_ref.shape[0] // chunk):
        ids = lax.broadcasted_iota(jnp.int32, (rows, chunk), 1) + part * chunk
        pick = jnp.where(wanted == ids, 1.0, 0.0).astype(jnp.bfloat16)
        acc_ref[...] += jnp.dot(
            pick, table_ref[pl.ds(part * chunk, chunk), :], preferred_element_type=jnp.float32
        )
    out_ref[...] = acc_ref[...].astype(out_ref.dtype)


def onehot_gather(table, index):
    count = index.shape[0]
    width = table.shape[1]
    tile = 256
    return pl.pallas_call(
        onehot_gather_kernel,
        grid=(count // tile,),
        in_specs=[
            pl.BlockSpec((tile, 1), lambda i: (i, 0)),
            pl.BlockSpec(table.shape, lambda i: (0, 0)),
        ],
        out_specs=pl.BlockSpec((tile, width), lambda i: (i, 0)),
        out_shape=jax.ShapeDtypeStruct((count, width), table.dtype),
        scratch_shapes=[pltpu.VMEM((tile, width), jnp.float32)],
    )(index.reshape(count, 1), table)


MESH = pl.DeviceIdType.MESH


def gather_rows(index_ref, table_ref, out_ref, first, last):
    tile = 256
    chunk = 512

    def one_tile(i, carry):
        rows = pl.ds(pl.multiple_of(i * tile, tile), tile)
        wanted = index_ref[rows, :]
        total = jnp.zeros((tile, out_ref.shape[1]), jnp.float32)
        for part in range(table_ref.shape[0] // chunk):
            ids = lax.broadcasted_iota(jnp.int32, (tile, chunk), 1) + part * chunk
            pick = jnp.where(wanted == ids, 1.0, 0.0).astype(jnp.bfloat16)
            total += jnp.dot(
                pick, table_ref[pl.ds(part * chunk, chunk), :], preferred_element_type=jnp.float32
            )
        out_ref[rows, :] = total.astype(out_ref.dtype)
        return carry

    lax.fori_loop(first, last, one_tile, 0)


def count_gather_kernel(nx, ny, index_ref, table_ref, mine_ref, rows_ref, out_ref, row_buf, grid_buf, send1, recv1, send2, recv2, own_sem):
    me_x = lax.axis_index("gx")
    me_y = lax.axis_index("gy")
    barrier = pltpu.get_barrier_semaphore()
    for k in range(1, ny):
        pl.semaphore_signal(
            barrier, inc=1, device_id=(me_x, lax.rem(me_y + k, ny)), device_id_type=MESH
        )
    for k in range(1, nx):
        pl.semaphore_signal(
            barrier, inc=1, device_id=(lax.rem(me_x + k, nx), me_y), device_id_type=MESH
        )
    pl.semaphore_wait(barrier, nx + ny - 2)

    own = pltpu.make_async_copy(mine_ref, row_buf.at[pl.ds(me_y, 1)], own_sem.at[0])
    own.start()
    for k in range(1, ny):
        pltpu.make_async_remote_copy(
            src_ref=mine_ref,
            dst_ref=row_buf.at[pl.ds(me_y, 1)],
            send_sem=send1.at[k],
            recv_sem=recv1.at[k],
            device_id=(me_x, lax.rem(me_y + k, ny)),
            device_id_type=MESH,
        ).start()
    tiles = rows_ref.shape[0] // 256
    gather_rows(index_ref, table_ref, rows_ref, 0, tiles // 2)
    own.wait()
    for k in range(1, ny):
        sender = lax.rem(me_y - k + ny, ny)
        copy = pltpu.make_async_remote_copy(
            src_ref=mine_ref,
            dst_ref=row_buf.at[pl.ds(sender, 1)],
            send_sem=send1.at[k],
            recv_sem=recv1.at[k],
            device_id=(me_x, sender),
            device_id_type=MESH,
        )
        copy.wait_send()
        copy.wait_recv()

    own = pltpu.make_async_copy(row_buf, grid_buf.at[me_x], own_sem.at[1])
    own.start()
    for k in range(1, nx):
        pltpu.make_async_remote_copy(
            src_ref=row_buf,
            dst_ref=grid_buf.at[me_x],
            send_sem=send2.at[k],
            recv_sem=recv2.at[k],
            device_id=(lax.rem(me_x + k, nx), me_y),
            device_id_type=MESH,
        ).start()
    gather_rows(index_ref, table_ref, rows_ref, tiles // 2, tiles)
    own.wait()
    for k in range(1, nx):
        sender = lax.rem(me_x - k + nx, nx)
        copy = pltpu.make_async_remote_copy(
            src_ref=row_buf,
            dst_ref=grid_buf.at[sender],
            send_sem=send2.at[k],
            recv_sem=recv2.at[k],
            device_id=(sender, me_y),
            device_id_type=MESH,
        )
        copy.wait_send()
        copy.wait_recv()
    out_ref[...] = grid_buf[...]


def gather_counts(mine, table, index):
    nx = lax.axis_size("gx")
    ny = lax.axis_size("gy")
    lanes = 128
    listed, grid = pl.pallas_call(
        functools.partial(count_gather_kernel, nx, ny),
        out_shape=(
            jax.ShapeDtypeStruct((index.shape[0], table.shape[1]), table.dtype),
            jax.ShapeDtypeStruct((nx, ny, lanes), jnp.int32),
        ),
        in_specs=[pl.BlockSpec(memory_space=pltpu.VMEM)] * 3,
        out_specs=(pl.BlockSpec(memory_space=pltpu.VMEM), pl.BlockSpec(memory_space=pltpu.VMEM)),
        scratch_shapes=[
            pltpu.VMEM((ny, lanes), jnp.int32),
            pltpu.VMEM((nx, ny, lanes), jnp.int32),
            pltpu.SemaphoreType.DMA((ny,)),
            pltpu.SemaphoreType.DMA((ny,)),
            pltpu.SemaphoreType.DMA((nx,)),
            pltpu.SemaphoreType.DMA((nx,)),
            pltpu.SemaphoreType.DMA((2,)),
        ],
        compiler_params=pltpu.CompilerParams(collective_id=0, has_side_effects=True),
    )(index.reshape(-1, 1), table, jnp.broadcast_to(mine, (1, lanes)))
    return listed, grid[:, :, 0].reshape(nx * ny)


def attention_kernel(q_ref, k_ref, v_ref, base_ref, proj_ref, out_ref):
    query = q_ref[...]
    keyset = k_ref[...]
    valueset = v_ref[...]
    width = query.shape[1]
    head_of = lax.broadcasted_iota(jnp.int32, (1, width), 1) // HD
    attended = jnp.zeros((query.shape[0], width), jnp.float32)
    for head in range(HEADS):
        mine = head_of == head
        scores = lax.dot_general(
            jnp.where(mine, query, jnp.zeros_like(query)),
            keyset,
            (((1,), (1,)), ((), ())),
            preferred_element_type=jnp.float32,
        ) * (1.0 / math.sqrt(HD))
        largest = jnp.max(scores, axis=-1, keepdims=True)
        expo = jnp.exp(scores - largest)
        scale = 1.0 / jnp.sum(expo, axis=-1, keepdims=True)
        mixed = jnp.dot(expo.astype(jnp.bfloat16), valueset, preferred_element_type=jnp.float32)
        attended = jnp.where(mine, mixed * scale, attended)
    out_ref[...] = base_ref[...].astype(jnp.float32) + jnp.dot(
        attended.astype(jnp.bfloat16), proj_ref[...], preferred_element_type=jnp.float32
    )


def attention_mid(rows, qkv_weight, proj_weight):
    count, width = rows.shape
    base = rows.astype(jnp.float32)
    normed = layer_norm(base).astype(jnp.bfloat16)
    projected = jnp.dot(normed, qkv_weight, preferred_element_type=jnp.float32).astype(jnp.bfloat16)
    tile = 512
    tiles = PATCH // tile
    grid = (count // PATCH, tiles)
    return pl.pallas_call(
        attention_kernel,
        grid=grid,
        in_specs=[
            pl.BlockSpec((tile, width), lambda p, t: (p * tiles + t, 0)),
            pl.BlockSpec((PATCH, width), lambda p, t: (p, 1)),
            pl.BlockSpec((PATCH, width), lambda p, t: (p, 2)),
            pl.BlockSpec((tile, width), lambda p, t: (p * tiles + t, 0)),
            pl.BlockSpec((width, width), lambda p, t: (0, 0)),
        ],
        out_specs=pl.BlockSpec((tile, width), lambda p, t: (p * tiles + t, 0)),
        out_shape=jax.ShapeDtypeStruct((count, width), jnp.float32),
    )(projected, projected, projected, rows, proj_weight)


def feed_forward(middle, up_weight, down_weight):
    second = layer_norm(middle).astype(jnp.bfloat16)
    hidden = jax.nn.gelu(
        jnp.dot(second, up_weight, preferred_element_type=jnp.float32), approximate=True
    ).astype(jnp.bfloat16)
    final = middle + jnp.dot(hidden, down_weight, preferred_element_type=jnp.float32)
    return final.astype(jnp.bfloat16)


def curve_tables(count_x, count_y):
    square = count_y * count_y
    index = np.arange(square)
    coord_x = np.zeros(square, np.int64)
    coord_y = np.zeros(square, np.int64)
    remain = index.copy()
    level = 1
    while level < count_y:
        bit_x = remain // 2 % 2
        bit_y = np.bitwise_xor(remain, bit_x) % 2
        mirror = (bit_y == 0) & (bit_x == 1)
        moved_x = np.where(mirror, level - 1 - coord_x, coord_x)
        moved_y = np.where(mirror, level - 1 - coord_y, coord_y)
        turned = bit_y == 0
        coord_x = np.where(turned, moved_y, moved_x) + level * bit_x
        coord_y = np.where(turned, moved_x, moved_y) + level * bit_y
        remain = remain // 4
        level = level * 2
    position = np.arange(count_x * count_y)
    along_x = coord_x[position % square] + (position // square) * count_y
    along_y = coord_y[position % square]
    return [int(d) for d in along_x * count_y + along_y]


def conv_kernel(shifted_ref, features_ref, weight_ref, linear_ref, out_ref):
    rows = features_ref.shape[0]
    side = shifted_ref.shape[2]
    width = features_ref.shape[-1]
    first = pl.program_id(0) * rows
    total = jnp.zeros((rows * side, width), jnp.float32)
    for offset in range(9):
        step_x = offset // 3
        step_y = offset % 3
        window = shifted_ref[step_y, pl.ds(first + step_x, rows)].reshape(rows * side, width)
        total += jnp.dot(window, weight_ref[offset], preferred_element_type=jnp.float32)
    linear = jnp.dot(total.astype(jnp.bfloat16), linear_ref[...], preferred_element_type=jnp.float32)
    base = features_ref[...].reshape(rows * side, width).astype(jnp.float32)
    out_ref[...] = (base + layer_norm(linear)).astype(out_ref.dtype)


def encode(padded, features, conv_weight, cpe_linear):
    span_x, span_y, width = features.shape
    shifted = jnp.stack([padded[:, step : step + span_y] for step in range(3)])
    rows = 8
    return pl.pallas_call(
        conv_kernel,
        grid=(span_x // rows,),
        in_specs=[
            pl.BlockSpec(memory_space=pltpu.VMEM),
            pl.BlockSpec((rows, span_y, width), lambda i: (i, 0, 0)),
            pl.BlockSpec(conv_weight.shape, lambda i: (0, 0, 0)),
            pl.BlockSpec(cpe_linear.shape, lambda i: (0, 0)),
        ],
        out_specs=pl.BlockSpec((rows * span_y, width), lambda i: (i, 0)),
        out_shape=jax.ShapeDtypeStruct((span_x * span_y, width), features.dtype),
    )(shifted, features, conv_weight, cpe_linear)


def shards(
    features,
    occupied,
    voxel_order,
    conv_weight,
    cpe_linear,
    qkv_weight,
    proj_weight,
    up_weight,
    down_weight,
):
    span_x, span_y, width = features.shape
    cells = span_x * span_y
    occ_flat = occupied.reshape(cells)
    mine = jnp.sum(occ_flat, dtype=jnp.int32)
    masked = features * occupied[:, :, None].astype(jnp.bfloat16)
    padded = with_halo(masked, (("gx", 0), ("gy", 1)), 1)
    encoded = encode(padded, features, conv_weight, cpe_linear)
    order = voxel_order[0]
    voxel = jnp.arange(cells, dtype=jnp.int32)
    _, rank_of = lax.sort_key_val(order, voxel)
    key = (1 - occ_flat) * cells + rank_of
    _, listed_voxel = lax.sort_key_val(key, voxel)
    capacity = CAP
    list_index = jnp.arange(LIVE + 2 * capacity, dtype=jnp.int32)
    picked = jnp.where(list_index < mine, listed_voxel[: LIVE + 2 * capacity], -1)
    list_rows, counts = gather_counts(mine, encoded, picked)
    devices = counts.shape[0]
    count_x = lax.axis_size("gx")
    count_y = lax.axis_size("gy")
    here_x = lax.axis_index("gx")
    here_y = lax.axis_index("gy")
    ranks = block_curve(count_x, count_y)
    position = ranks[here_x * count_y + here_y]
    by_position = jnp.zeros((devices,), jnp.int32).at[ranks].set(counts)
    starts = jnp.cumsum(by_position, dtype=jnp.int32) - by_position
    start_here = starts[position]
    excess = start_here - position * LIVE
    beyond = start_here + mine - (position + 1) * LIVE
    slot = jnp.arange(capacity, dtype=jnp.int32)
    empty = jnp.zeros((capacity, width), jnp.bfloat16)
    extended = jnp.concatenate([empty, list_rows], axis=0)
    mine_rows = lax.dynamic_slice_in_dim(extended, capacity - excess, LIVE, 0)
    to_prev = jnp.where((slot < -excess)[:, None], list_rows[:capacity], empty)
    to_next = jnp.where(
        (slot < beyond)[:, None], lax.dynamic_slice_in_dim(list_rows, LIVE - excess, capacity, 0), empty
    )
    device_at = curve_tables(count_x, count_y)
    forward = [(device_at[p], device_at[p + 1]) for p in range(devices - 1)]
    backward = [(target, source) for source, target in forward]
    from_prev = lax.ppermute(to_next, ("gx", "gy"), forward)
    from_next = lax.ppermute(to_prev, ("gx", "gy"), backward)
    from_prev = jnp.where((slot < excess)[:, None], from_prev, empty)
    from_next = jnp.where((slot < -beyond)[:, None], from_next, empty)
    leading = jnp.concatenate(
        [from_prev, jnp.zeros((LIVE - capacity, width), jnp.bfloat16)], axis=0
    )
    trailing = lax.dynamic_slice_in_dim(
        jnp.concatenate([jnp.zeros((LIVE, width), jnp.bfloat16), from_next], axis=0),
        -beyond,
        LIVE,
        0,
    )
    owned = mine_rows + leading + trailing
    middle = attention_mid(owned, qkv_weight, proj_weight)
    return feed_forward(middle, up_weight, down_weight)


def solution(mesh):
    return jax.shard_map(
        shards,
        mesh=mesh,
        in_specs=(
            P("gx", "gy", None),
            P("gx", "gy"),
            P(("gx", "gy"), None),
            P(),
            P(),
            P(),
            P(),
            P(),
            P(),
        ),
        out_specs=P(("gx", "gy"), None),
        check_vma=False,
    )
```

```python
import functools
import math

import jax
import numpy as np
import jax.numpy as jnp
from jax import lax
from jax.experimental import pallas as pl
from jax.experimental.pallas import tpu as pltpu
from jax.sharding import PartitionSpec as P

HEADS = 8
PATCH = 1024
LIVE = 2048
CAP = 256
HD = 32


def with_halo(block, sides, width):
    for axis, dim in sides:
        count = lax.axis_size(axis)
        forward = [(i, i + 1) for i in range(count - 1)]
        backward = [(target, source) for source, target in forward]
        low = lax.ppermute(
            lax.slice_in_dim(block, block.shape[dim] - width, None, axis=dim), axis, forward
        )
        high = lax.ppermute(lax.slice_in_dim(block, 0, width, axis=dim), axis, backward)
        block = jnp.concatenate([low, block, high], axis=dim)
    return block


def passed_along(block, axis, distance):
    devices = range(lax.axis_size(axis))
    route = [(i - distance, i) for i in devices if i - distance in devices]
    return lax.ppermute(block, axis, route)


def hilbert_points(side):
    index = jnp.arange(side * side, dtype=jnp.int32)
    coord_x = jnp.zeros((side * side,), jnp.int32)
    coord_y = jnp.zeros((side * side,), jnp.int32)
    remain = index
    level = 1
    while level < side:
        bit_x = remain // 2 % 2
        bit_y = jnp.bitwise_xor(remain, bit_x) % 2
        mirror = (bit_y == 0) & (bit_x == 1)
        moved_x = jnp.where(mirror, level - 1 - coord_x, coord_x)
        moved_y = jnp.where(mirror, level - 1 - coord_y, coord_y)
        turned = bit_y == 0
        coord_x = jnp.where(turned, moved_y, moved_x) + level * bit_x
        coord_y = jnp.where(turned, moved_x, moved_y) + level * bit_y
        remain = remain // 4
        level = level * 2
    return (coord_x, coord_y)


def block_curve(count_x, count_y):
    total = count_x * count_y
    square = count_y * count_y
    position = jnp.arange(total, dtype=jnp.int32)
    half = position // square
    inner_x, inner_y = hilbert_points(count_y)
    along_x = inner_x[position % square] + half * count_y
    along_y = inner_y[position % square]
    device = along_x * count_y + along_y
    return jnp.zeros((total,), jnp.int32).at[device].set(position)


def layer_norm(values):
    centre = values - jnp.mean(values, axis=-1, keepdims=True)
    spread = jnp.mean(centre * centre, axis=-1, keepdims=True)
    return centre * lax.rsqrt(spread + 1e-05)


def attend_patch(rows, qkv_weight, proj_weight, up_weight, down_weight):
    base = rows.astype(jnp.float32)
    normed = layer_norm(base).astype(jnp.bfloat16)
    projected = jnp.dot(normed, qkv_weight, preferred_element_type=jnp.float32).astype(jnp.bfloat16)
    width = rows.shape[1]
    count = rows.shape[0]
    query = projected[:, :width].reshape(count, HEADS, HD)
    keyset = projected[:, width : 2 * width].reshape(count, HEADS, HD)
    valueset = projected[:, 2 * width :].reshape(count, HEADS, HD)
    scores = jnp.einsum("qhd,khd->hqk", query, keyset, preferred_element_type=jnp.float32) * (
        1.0 / math.sqrt(HD)
    )
    largest = jnp.max(scores, axis=-1, keepdims=True)
    expo = jnp.exp(scores - largest)
    weights = (expo / jnp.sum(expo, axis=-1, keepdims=True)).astype(jnp.bfloat16)
    attended = jnp.einsum(
        "hqk,khd->qhd", weights, valueset, preferred_element_type=jnp.float32
    ).astype(jnp.bfloat16)
    middle = base + jnp.dot(
        attended.reshape(count, width), proj_weight, preferred_element_type=jnp.float32
    )
    second = layer_norm(middle).astype(jnp.bfloat16)
    hidden = jax.nn.gelu(
        jnp.dot(second, up_weight, preferred_element_type=jnp.float32), approximate=True
    ).astype(jnp.bfloat16)
    final = middle + jnp.dot(hidden, down_weight, preferred_element_type=jnp.float32)
    return final.astype(jnp.bfloat16)


def onehot_gather_kernel(index_ref, table_ref, out_ref, acc_ref):
    rows = index_ref.shape[0]
    chunk = 512
    wanted = index_ref[...]
    acc_ref[...] = jnp.zeros_like(acc_ref)
    for part in range(table_ref.shape[0] // chunk):
        ids = lax.broadcasted_iota(jnp.int32, (rows, chunk), 1) + part * chunk
        pick = jnp.where(wanted == ids, 1.0, 0.0).astype(jnp.bfloat16)
        acc_ref[...] += jnp.dot(
            pick, table_ref[pl.ds(part * chunk, chunk), :], preferred_element_type=jnp.float32
        )
    out_ref[...] = acc_ref[...].astype(out_ref.dtype)


def onehot_gather(table, index):
    count = index.shape[0]
    width = table.shape[1]
    tile = 256
    return pl.pallas_call(
        onehot_gather_kernel,
        grid=(count // tile,),
        in_specs=[
            pl.BlockSpec((tile, 1), lambda i: (i, 0)),
            pl.BlockSpec(table.shape, lambda i: (0, 0)),
        ],
        out_specs=pl.BlockSpec((tile, width), lambda i: (i, 0)),
        out_shape=jax.ShapeDtypeStruct((count, width), table.dtype),
        scratch_shapes=[pltpu.VMEM((tile, width), jnp.float32)],
    )(index.reshape(count, 1), table)


MESH = pl.DeviceIdType.MESH


def gather_rows(index_ref, table_ref, out_ref, first, last):
    tile = 256
    chunk = 512

    def one_tile(i, carry):
        rows = pl.ds(pl.multiple_of(i * tile, tile), tile)
        wanted = index_ref[rows, :]
        total = jnp.zeros((tile, out_ref.shape[1]), jnp.float32)
        for part in range(table_ref.shape[0] // chunk):
            ids = lax.broadcasted_iota(jnp.int32, (tile, chunk), 1) + part * chunk
            pick = jnp.where(wanted == ids, 1.0, 0.0).astype(jnp.bfloat16)
            total += jnp.dot(
                pick, table_ref[pl.ds(part * chunk, chunk), :], preferred_element_type=jnp.float32
            )
        out_ref[rows, :] = total.astype(out_ref.dtype)
        return carry

    lax.fori_loop(first, last, one_tile, 0)


def count_gather_kernel(nx, ny, index_ref, table_ref, mine_ref, rows_ref, out_ref, row_buf, grid_buf, send1, recv1, send2, recv2, own_sem):
    me_x = lax.axis_index("gx")
    me_y = lax.axis_index("gy")
    barrier = pltpu.get_barrier_semaphore()
    for k in range(1, ny):
        pl.semaphore_signal(
            barrier, inc=1, device_id=(me_x, lax.rem(me_y + k, ny)), device_id_type=MESH
        )
    for k in range(1, nx):
        pl.semaphore_signal(
            barrier, inc=1, device_id=(lax.rem(me_x + k, nx), me_y), device_id_type=MESH
        )
    pl.semaphore_wait(barrier, nx + ny - 2)

    own = pltpu.make_async_copy(mine_ref, row_buf.at[pl.ds(me_y, 1)], own_sem.at[0])
    own.start()
    for k in range(1, ny):
        pltpu.make_async_remote_copy(
            src_ref=mine_ref,
            dst_ref=row_buf.at[pl.ds(me_y, 1)],
            send_sem=send1.at[k],
            recv_sem=recv1.at[k],
            device_id=(me_x, lax.rem(me_y + k, ny)),
            device_id_type=MESH,
        ).start()
    tiles = rows_ref.shape[0] // 256
    gather_rows(index_ref, table_ref, rows_ref, 0, tiles // 2)
    own.wait()
    for k in range(1, ny):
        sender = lax.rem(me_y - k + ny, ny)
        copy = pltpu.make_async_remote_copy(
            src_ref=mine_ref,
            dst_ref=row_buf.at[pl.ds(sender, 1)],
            send_sem=send1.at[k],
            recv_sem=recv1.at[k],
            device_id=(me_x, sender),
            device_id_type=MESH,
        )
        copy.wait_send()
        copy.wait_recv()

    own = pltpu.make_async_copy(row_buf, grid_buf.at[me_x], own_sem.at[1])
    own.start()
    for k in range(1, nx):
        pltpu.make_async_remote_copy(
            src_ref=row_buf,
            dst_ref=grid_buf.at[me_x],
            send_sem=send2.at[k],
            recv_sem=recv2.at[k],
            device_id=(lax.rem(me_x + k, nx), me_y),
            device_id_type=MESH,
        ).start()
    gather_rows(index_ref, table_ref, rows_ref, tiles // 2, tiles)
    own.wait()
    for k in range(1, nx):
        sender = lax.rem(me_x - k + nx, nx)
        copy = pltpu.make_async_remote_copy(
            src_ref=row_buf,
            dst_ref=grid_buf.at[sender],
            send_sem=send2.at[k],
            recv_sem=recv2.at[k],
            device_id=(sender, me_y),
            device_id_type=MESH,
        )
        copy.wait_send()
        copy.wait_recv()
    out_ref[...] = grid_buf[...]


def gather_counts(mine, table, index):
    nx = lax.axis_size("gx")
    ny = lax.axis_size("gy")
    lanes = 128
    listed, grid = pl.pallas_call(
        functools.partial(count_gather_kernel, nx, ny),
        out_shape=(
            jax.ShapeDtypeStruct((index.shape[0], table.shape[1]), table.dtype),
            jax.ShapeDtypeStruct((nx, ny, lanes), jnp.int32),
        ),
        in_specs=[pl.BlockSpec(memory_space=pltpu.VMEM)] * 3,
        out_specs=(pl.BlockSpec(memory_space=pltpu.VMEM), pl.BlockSpec(memory_space=pltpu.VMEM)),
        scratch_shapes=[
            pltpu.VMEM((ny, lanes), jnp.int32),
            pltpu.VMEM((nx, ny, lanes), jnp.int32),
            pltpu.SemaphoreType.DMA((ny,)),
            pltpu.SemaphoreType.DMA((ny,)),
            pltpu.SemaphoreType.DMA((nx,)),
            pltpu.SemaphoreType.DMA((nx,)),
            pltpu.SemaphoreType.DMA((2,)),
        ],
        compiler_params=pltpu.CompilerParams(collective_id=0, has_side_effects=True),
    )(index.reshape(-1, 1), table, jnp.broadcast_to(mine, (1, lanes)))
    return listed, grid[:, :, 0].reshape(nx * ny)


def attention_kernel(q_ref, k_ref, v_ref, base_ref, proj_ref, out_ref):
    query = q_ref[...]
    keyset = k_ref[...]
    valueset = v_ref[...]
    width = query.shape[1]
    head_of = lax.broadcasted_iota(jnp.int32, (1, width), 1) // HD
    attended = jnp.zeros((query.shape[0], width), jnp.float32)
    for head in range(HEADS):
        mine = head_of == head
        scores = lax.dot_general(
            jnp.where(mine, query, jnp.zeros_like(query)),
            keyset,
            (((1,), (1,)), ((), ())),
            preferred_element_type=jnp.float32,
        ) * (1.0 / math.sqrt(HD))
        largest = jnp.max(scores, axis=-1, keepdims=True)
        expo = jnp.exp(scores - largest)
        scale = 1.0 / jnp.sum(expo, axis=-1, keepdims=True)
        mixed = jnp.dot(expo.astype(jnp.bfloat16), valueset, preferred_element_type=jnp.float32)
        attended = jnp.where(mine, mixed * scale, attended)
    out_ref[...] = base_ref[...].astype(jnp.float32) + jnp.dot(
        attended.astype(jnp.bfloat16), proj_ref[...], preferred_element_type=jnp.float32
    )


def attention_mid(rows, qkv_weight, proj_weight):
    count, width = rows.shape
    base = rows.astype(jnp.float32)
    normed = layer_norm(base).astype(jnp.bfloat16)
    projected = jnp.dot(normed, qkv_weight, preferred_element_type=jnp.float32).astype(jnp.bfloat16)
    tile = 1024
    tiles = PATCH // tile
    grid = (count // PATCH, tiles)
    return pl.pallas_call(
        attention_kernel,
        grid=grid,
        in_specs=[
            pl.BlockSpec((tile, width), lambda p, t: (p * tiles + t, 0)),
            pl.BlockSpec((PATCH, width), lambda p, t: (p, 1)),
            pl.BlockSpec((PATCH, width), lambda p, t: (p, 2)),
            pl.BlockSpec((tile, width), lambda p, t: (p * tiles + t, 0)),
            pl.BlockSpec((width, width), lambda p, t: (0, 0)),
        ],
        out_specs=pl.BlockSpec((tile, width), lambda p, t: (p * tiles + t, 0)),
        out_shape=jax.ShapeDtypeStruct((count, width), jnp.float32),
    )(projected, projected, projected, rows, proj_weight)


def feed_forward(middle, up_weight, down_weight):
    second = layer_norm(middle).astype(jnp.bfloat16)
    hidden = jax.nn.gelu(
        jnp.dot(second, up_weight, preferred_element_type=jnp.float32), approximate=True
    ).astype(jnp.bfloat16)
    final = middle + jnp.dot(hidden, down_weight, preferred_element_type=jnp.float32)
    return final.astype(jnp.bfloat16)


def curve_tables(count_x, count_y):
    square = count_y * count_y
    index = np.arange(square)
    coord_x = np.zeros(square, np.int64)
    coord_y = np.zeros(square, np.int64)
    remain = index.copy()
    level = 1
    while level < count_y:
        bit_x = remain // 2 % 2
        bit_y = np.bitwise_xor(remain, bit_x) % 2
        mirror = (bit_y == 0) & (bit_x == 1)
        moved_x = np.where(mirror, level - 1 - coord_x, coord_x)
        moved_y = np.where(mirror, level - 1 - coord_y, coord_y)
        turned = bit_y == 0
        coord_x = np.where(turned, moved_y, moved_x) + level * bit_x
        coord_y = np.where(turned, moved_x, moved_y) + level * bit_y
        remain = remain // 4
        level = level * 2
    position = np.arange(count_x * count_y)
    along_x = coord_x[position % square] + (position // square) * count_y
    along_y = coord_y[position % square]
    return [int(d) for d in along_x * count_y + along_y]


def conv_kernel(shifted_ref, features_ref, weight_ref, linear_ref, out_ref):
    rows = features_ref.shape[0]
    side = shifted_ref.shape[2]
    width = features_ref.shape[-1]
    first = pl.program_id(0) * rows
    total = jnp.zeros((rows * side, width), jnp.float32)
    for offset in range(9):
        step_x = offset // 3
        step_y = offset % 3
        window = shifted_ref[step_y, pl.ds(first + step_x, rows)].reshape(rows * side, width)
        total += jnp.dot(window, weight_ref[offset], preferred_element_type=jnp.float32)
    linear = jnp.dot(total.astype(jnp.bfloat16), linear_ref[...], preferred_element_type=jnp.float32)
    base = features_ref[...].reshape(rows * side, width).astype(jnp.float32)
    out_ref[...] = (base + layer_norm(linear)).astype(out_ref.dtype)


def encode(padded, features, conv_weight, cpe_linear):
    span_x, span_y, width = features.shape
    shifted = jnp.stack([padded[:, step : step + span_y] for step in range(3)])
    rows = 8
    return pl.pallas_call(
        conv_kernel,
        grid=(span_x // rows,),
        in_specs=[
            pl.BlockSpec(memory_space=pltpu.VMEM),
            pl.BlockSpec((rows, span_y, width), lambda i: (i, 0, 0)),
            pl.BlockSpec(conv_weight.shape, lambda i: (0, 0, 0)),
            pl.BlockSpec(cpe_linear.shape, lambda i: (0, 0)),
        ],
        out_specs=pl.BlockSpec((rows * span_y, width), lambda i: (i, 0)),
        out_shape=jax.ShapeDtypeStruct((span_x * span_y, width), features.dtype),
    )(shifted, features, conv_weight, cpe_linear)


def shards(
    features,
    occupied,
    voxel_order,
    conv_weight,
    cpe_linear,
    qkv_weight,
    proj_weight,
    up_weight,
    down_weight,
):
    span_x, span_y, width = features.shape
    cells = span_x * span_y
    occ_flat = occupied.reshape(cells)
    mine = jnp.sum(occ_flat, dtype=jnp.int32)
    masked = features * occupied[:, :, None].astype(jnp.bfloat16)
    padded = with_halo(masked, (("gx", 0), ("gy", 1)), 1)
    encoded = encode(padded, features, conv_weight, cpe_linear)
    order = voxel_order[0]
    voxel = jnp.arange(cells, dtype=jnp.int32)
    _, rank_of = lax.sort_key_val(order, voxel)
    key = (1 - occ_flat) * cells + rank_of
    _, listed_voxel = lax.sort_key_val(key, voxel)
    capacity = CAP
    list_index = jnp.arange(LIVE + 2 * capacity, dtype=jnp.int32)
    picked = jnp.where(list_index < mine, listed_voxel[: LIVE + 2 * capacity], -1)
    list_rows, counts = gather_counts(mine, encoded, picked)
    devices = counts.shape[0]
    count_x = lax.axis_size("gx")
    count_y = lax.axis_size("gy")
    here_x = lax.axis_index("gx")
    here_y = lax.axis_index("gy")
    ranks = block_curve(count_x, count_y)
    position = ranks[here_x * count_y + here_y]
    by_position = jnp.zeros((devices,), jnp.int32).at[ranks].set(counts)
    starts = jnp.cumsum(by_position, dtype=jnp.int32) - by_position
    start_here = starts[position]
    excess = start_here - position * LIVE
    beyond = start_here + mine - (position + 1) * LIVE
    slot = jnp.arange(capacity, dtype=jnp.int32)
    empty = jnp.zeros((capacity, width), jnp.bfloat16)
    extended = jnp.concatenate([empty, list_rows], axis=0)
    mine_rows = lax.dynamic_slice_in_dim(extended, capacity - excess, LIVE, 0)
    to_prev = jnp.where((slot < -excess)[:, None], list_rows[:capacity], empty)
    to_next = jnp.where(
        (slot < beyond)[:, None], lax.dynamic_slice_in_dim(list_rows, LIVE - excess, capacity, 0), empty
    )
    device_at = curve_tables(count_x, count_y)
    forward = [(device_at[p], device_at[p + 1]) for p in range(devices - 1)]
    backward = [(target, source) for source, target in forward]
    from_prev = lax.ppermute(to_next, ("gx", "gy"), forward)
    from_next = lax.ppermute(to_prev, ("gx", "gy"), backward)
    from_prev = jnp.where((slot < excess)[:, None], from_prev, empty)
    from_next = jnp.where((slot < -beyond)[:, None], from_next, empty)
    leading = jnp.concatenate(
        [from_prev, jnp.zeros((LIVE - capacity, width), jnp.bfloat16)], axis=0
    )
    trailing = lax.dynamic_slice_in_dim(
        jnp.concatenate([jnp.zeros((LIVE, width), jnp.bfloat16), from_next], axis=0),
        -beyond,
        LIVE,
        0,
    )
    owned = mine_rows + leading + trailing
    middle = attention_mid(owned, qkv_weight, proj_weight)
    return feed_forward(middle, up_weight, down_weight)


def solution(mesh):
    return jax.shard_map(
        shards,
        mesh=mesh,
        in_specs=(
            P("gx", "gy", None),
            P("gx", "gy"),
            P(("gx", "gy"), None),
            P(),
            P(),
            P(),
            P(),
            P(),
            P(),
        ),
        out_specs=P(("gx", "gy"), None),
        check_vma=False,
    )
```

```python
import functools
import math

import jax
import numpy as np
import jax.numpy as jnp
from jax import lax
from jax.experimental import pallas as pl
from jax.experimental.pallas import tpu as pltpu
from jax.sharding import PartitionSpec as P

HEADS = 8
PATCH = 1024
LIVE = 2048
CAP = 256
HD = 32


def with_halo(block, sides, width):
    for axis, dim in sides:
        count = lax.axis_size(axis)
        forward = [(i, i + 1) for i in range(count - 1)]
        backward = [(target, source) for source, target in forward]
        low = lax.ppermute(
            lax.slice_in_dim(block, block.shape[dim] - width, None, axis=dim), axis, forward
        )
        high = lax.ppermute(lax.slice_in_dim(block, 0, width, axis=dim), axis, backward)
        block = jnp.concatenate([low, block, high], axis=dim)
    return block


def passed_along(block, axis, distance):
    devices = range(lax.axis_size(axis))
    route = [(i - distance, i) for i in devices if i - distance in devices]
    return lax.ppermute(block, axis, route)


def hilbert_points(side):
    index = jnp.arange(side * side, dtype=jnp.int32)
    coord_x = jnp.zeros((side * side,), jnp.int32)
    coord_y = jnp.zeros((side * side,), jnp.int32)
    remain = index
    level = 1
    while level < side:
        bit_x = remain // 2 % 2
        bit_y = jnp.bitwise_xor(remain, bit_x) % 2
        mirror = (bit_y == 0) & (bit_x == 1)
        moved_x = jnp.where(mirror, level - 1 - coord_x, coord_x)
        moved_y = jnp.where(mirror, level - 1 - coord_y, coord_y)
        turned = bit_y == 0
        coord_x = jnp.where(turned, moved_y, moved_x) + level * bit_x
        coord_y = jnp.where(turned, moved_x, moved_y) + level * bit_y
        remain = remain // 4
        level = level * 2
    return (coord_x, coord_y)


def block_curve(count_x, count_y):
    total = count_x * count_y
    square = count_y * count_y
    position = jnp.arange(total, dtype=jnp.int32)
    half = position // square
    inner_x, inner_y = hilbert_points(count_y)
    along_x = inner_x[position % square] + half * count_y
    along_y = inner_y[position % square]
    device = along_x * count_y + along_y
    return jnp.zeros((total,), jnp.int32).at[device].set(position)


def layer_norm(values):
    centre = values - jnp.mean(values, axis=-1, keepdims=True)
    spread = jnp.mean(centre * centre, axis=-1, keepdims=True)
    return centre * lax.rsqrt(spread + 1e-05)


def attend_patch(rows, qkv_weight, proj_weight, up_weight, down_weight):
    base = rows.astype(jnp.float32)
    normed = layer_norm(base).astype(jnp.bfloat16)
    projected = jnp.dot(normed, qkv_weight, preferred_element_type=jnp.float32).astype(jnp.bfloat16)
    width = rows.shape[1]
    count = rows.shape[0]
    query = projected[:, :width].reshape(count, HEADS, HD)
    keyset = projected[:, width : 2 * width].reshape(count, HEADS, HD)
    valueset = projected[:, 2 * width :].reshape(count, HEADS, HD)
    scores = jnp.einsum("qhd,khd->hqk", query, keyset, preferred_element_type=jnp.float32) * (
        1.0 / math.sqrt(HD)
    )
    largest = jnp.max(scores, axis=-1, keepdims=True)
    expo = jnp.exp(scores - largest)
    weights = (expo / jnp.sum(expo, axis=-1, keepdims=True)).astype(jnp.bfloat16)
    attended = jnp.einsum(
        "hqk,khd->qhd", weights, valueset, preferred_element_type=jnp.float32
    ).astype(jnp.bfloat16)
    middle = base + jnp.dot(
        attended.reshape(count, width), proj_weight, preferred_element_type=jnp.float32
    )
    second = layer_norm(middle).astype(jnp.bfloat16)
    hidden = jax.nn.gelu(
        jnp.dot(second, up_weight, preferred_element_type=jnp.float32), approximate=True
    ).astype(jnp.bfloat16)
    final = middle + jnp.dot(hidden, down_weight, preferred_element_type=jnp.float32)
    return final.astype(jnp.bfloat16)


def onehot_gather_kernel(index_ref, table_ref, out_ref, acc_ref):
    rows = index_ref.shape[0]
    chunk = 512
    wanted = index_ref[...]
    acc_ref[...] = jnp.zeros_like(acc_ref)
    for part in range(table_ref.shape[0] // chunk):
        ids = lax.broadcasted_iota(jnp.int32, (rows, chunk), 1) + part * chunk
        pick = jnp.where(wanted == ids, 1.0, 0.0).astype(jnp.bfloat16)
        acc_ref[...] += jnp.dot(
            pick, table_ref[pl.ds(part * chunk, chunk), :], preferred_element_type=jnp.float32
        )
    out_ref[...] = acc_ref[...].astype(out_ref.dtype)


def onehot_gather(table, index):
    count = index.shape[0]
    width = table.shape[1]
    tile = 256
    return pl.pallas_call(
        onehot_gather_kernel,
        grid=(count // tile,),
        in_specs=[
            pl.BlockSpec((tile, 1), lambda i: (i, 0)),
            pl.BlockSpec(table.shape, lambda i: (0, 0)),
        ],
        out_specs=pl.BlockSpec((tile, width), lambda i: (i, 0)),
        out_shape=jax.ShapeDtypeStruct((count, width), table.dtype),
        scratch_shapes=[pltpu.VMEM((tile, width), jnp.float32)],
    )(index.reshape(count, 1), table)


MESH = pl.DeviceIdType.MESH


def gather_rows(index_ref, table_ref, out_ref, first, last):
    tile = 256
    chunk = 512

    def one_tile(i, carry):
        rows = pl.ds(pl.multiple_of(i * tile, tile), tile)
        wanted = index_ref[rows, :]
        total = jnp.zeros((tile, out_ref.shape[1]), jnp.float32)
        for part in range(table_ref.shape[0] // chunk):
            ids = lax.broadcasted_iota(jnp.int32, (tile, chunk), 1) + part * chunk
            pick = jnp.where(wanted == ids, 1.0, 0.0).astype(jnp.bfloat16)
            total += jnp.dot(
                pick, table_ref[pl.ds(part * chunk, chunk), :], preferred_element_type=jnp.float32
            )
        out_ref[rows, :] = total.astype(out_ref.dtype)
        return carry

    lax.fori_loop(first, last, one_tile, 0)


def count_gather_kernel(nx, ny, index_ref, table_ref, mine_ref, rows_ref, out_ref, row_buf, grid_buf, send1, recv1, send2, recv2, own_sem):
    me_x = lax.axis_index("gx")
    me_y = lax.axis_index("gy")
    barrier = pltpu.get_barrier_semaphore()
    for k in range(1, ny):
        pl.semaphore_signal(
            barrier, inc=1, device_id=(me_x, lax.rem(me_y + k, ny)), device_id_type=MESH
        )
    for k in range(1, nx):
        pl.semaphore_signal(
            barrier, inc=1, device_id=(lax.rem(me_x + k, nx), me_y), device_id_type=MESH
        )
    pl.semaphore_wait(barrier, nx + ny - 2)

    own = pltpu.make_async_copy(mine_ref, row_buf.at[pl.ds(me_y, 1)], own_sem.at[0])
    own.start()
    for k in range(1, ny):
        pltpu.make_async_remote_copy(
            src_ref=mine_ref,
            dst_ref=row_buf.at[pl.ds(me_y, 1)],
            send_sem=send1.at[k],
            recv_sem=recv1.at[k],
            device_id=(me_x, lax.rem(me_y + k, ny)),
            device_id_type=MESH,
        ).start()
    tiles = rows_ref.shape[0] // 256
    gather_rows(index_ref, table_ref, rows_ref, 0, tiles // 2)
    own.wait()
    for k in range(1, ny):
        sender = lax.rem(me_y - k + ny, ny)
        copy = pltpu.make_async_remote_copy(
            src_ref=mine_ref,
            dst_ref=row_buf.at[pl.ds(sender, 1)],
            send_sem=send1.at[k],
            recv_sem=recv1.at[k],
            device_id=(me_x, sender),
            device_id_type=MESH,
        )
        copy.wait_send()
        copy.wait_recv()

    own = pltpu.make_async_copy(row_buf, grid_buf.at[me_x], own_sem.at[1])
    own.start()
    for k in range(1, nx):
        pltpu.make_async_remote_copy(
            src_ref=row_buf,
            dst_ref=grid_buf.at[me_x],
            send_sem=send2.at[k],
            recv_sem=recv2.at[k],
            device_id=(lax.rem(me_x + k, nx), me_y),
            device_id_type=MESH,
        ).start()
    gather_rows(index_ref, table_ref, rows_ref, tiles // 2, tiles)
    own.wait()
    for k in range(1, nx):
        sender = lax.rem(me_x - k + nx, nx)
        copy = pltpu.make_async_remote_copy(
            src_ref=row_buf,
            dst_ref=grid_buf.at[sender],
            send_sem=send2.at[k],
            recv_sem=recv2.at[k],
            device_id=(sender, me_y),
            device_id_type=MESH,
        )
        copy.wait_send()
        copy.wait_recv()
    out_ref[...] = grid_buf[...]


def gather_counts(mine, table, index):
    nx = lax.axis_size("gx")
    ny = lax.axis_size("gy")
    lanes = 128
    listed, grid = pl.pallas_call(
        functools.partial(count_gather_kernel, nx, ny),
        out_shape=(
            jax.ShapeDtypeStruct((index.shape[0], table.shape[1]), table.dtype),
            jax.ShapeDtypeStruct((nx, ny, lanes), jnp.int32),
        ),
        in_specs=[pl.BlockSpec(memory_space=pltpu.VMEM)] * 3,
        out_specs=(pl.BlockSpec(memory_space=pltpu.VMEM), pl.BlockSpec(memory_space=pltpu.VMEM)),
        scratch_shapes=[
            pltpu.VMEM((ny, lanes), jnp.int32),
            pltpu.VMEM((nx, ny, lanes), jnp.int32),
            pltpu.SemaphoreType.DMA((ny,)),
            pltpu.SemaphoreType.DMA((ny,)),
            pltpu.SemaphoreType.DMA((nx,)),
            pltpu.SemaphoreType.DMA((nx,)),
            pltpu.SemaphoreType.DMA((2,)),
        ],
        compiler_params=pltpu.CompilerParams(collective_id=0, has_side_effects=True),
    )(index.reshape(-1, 1), table, jnp.broadcast_to(mine, (1, lanes)))
    return listed, grid[:, :, 0].reshape(nx * ny)


def attention_kernel(q_ref, k_ref, v_ref, base_ref, proj_ref, up_ref, down_ref, out_ref):
    query = q_ref[...]
    keyset = k_ref[...]
    valueset = v_ref[...]
    width = query.shape[1]
    head_of = lax.broadcasted_iota(jnp.int32, (1, width), 1) // HD
    attended = jnp.zeros((query.shape[0], width), jnp.float32)
    for head in range(HEADS):
        mine = head_of == head
        scores = lax.dot_general(
            jnp.where(mine, query, jnp.zeros_like(query)),
            keyset,
            (((1,), (1,)), ((), ())),
            preferred_element_type=jnp.float32,
        ) * (1.0 / math.sqrt(HD))
        largest = jnp.max(scores, axis=-1, keepdims=True)
        expo = jnp.exp(scores - largest)
        scale = 1.0 / jnp.sum(expo, axis=-1, keepdims=True)
        mixed = jnp.dot(expo.astype(jnp.bfloat16), valueset, preferred_element_type=jnp.float32)
        attended = jnp.where(mine, mixed * scale, attended)
    middle = base_ref[...].astype(jnp.float32) + jnp.dot(
        attended.astype(jnp.bfloat16), proj_ref[...], preferred_element_type=jnp.float32
    )
    second = layer_norm(middle).astype(jnp.bfloat16)
    hidden = jax.nn.gelu(
        jnp.dot(second, up_ref[...], preferred_element_type=jnp.float32), approximate=True
    ).astype(jnp.bfloat16)
    final = middle + jnp.dot(hidden, down_ref[...], preferred_element_type=jnp.float32)
    out_ref[...] = final.astype(out_ref.dtype)


def attention_block(rows, qkv_weight, proj_weight, up_weight, down_weight):
    count, width = rows.shape
    base = rows.astype(jnp.float32)
    normed = layer_norm(base).astype(jnp.bfloat16)
    projected = jnp.dot(normed, qkv_weight, preferred_element_type=jnp.float32).astype(jnp.bfloat16)
    tile = 512
    tiles = PATCH // tile
    grid = (count // PATCH, tiles)
    return pl.pallas_call(
        attention_kernel,
        grid=grid,
        in_specs=[
            pl.BlockSpec((tile, width), lambda p, t: (p * tiles + t, 0)),
            pl.BlockSpec((PATCH, width), lambda p, t: (p, 1)),
            pl.BlockSpec((PATCH, width), lambda p, t: (p, 2)),
            pl.BlockSpec((tile, width), lambda p, t: (p * tiles + t, 0)),
            pl.BlockSpec((width, width), lambda p, t: (0, 0)),
            pl.BlockSpec(up_weight.shape, lambda p, t: (0, 0)),
            pl.BlockSpec(down_weight.shape, lambda p, t: (0, 0)),
        ],
        out_specs=pl.BlockSpec((tile, width), lambda p, t: (p * tiles + t, 0)),
        out_shape=jax.ShapeDtypeStruct((count, width), rows.dtype),
    )(projected, projected, projected, rows, proj_weight, up_weight, down_weight)


def feed_forward(middle, up_weight, down_weight):
    second = layer_norm(middle).astype(jnp.bfloat16)
    hidden = jax.nn.gelu(
        jnp.dot(second, up_weight, preferred_element_type=jnp.float32), approximate=True
    ).astype(jnp.bfloat16)
    final = middle + jnp.dot(hidden, down_weight, preferred_element_type=jnp.float32)
    return final.astype(jnp.bfloat16)


def curve_tables(count_x, count_y):
    square = count_y * count_y
    index = np.arange(square)
    coord_x = np.zeros(square, np.int64)
    coord_y = np.zeros(square, np.int64)
    remain = index.copy()
    level = 1
    while level < count_y:
        bit_x = remain // 2 % 2
        bit_y = np.bitwise_xor(remain, bit_x) % 2
        mirror = (bit_y == 0) & (bit_x == 1)
        moved_x = np.where(mirror, level - 1 - coord_x, coord_x)
        moved_y = np.where(mirror, level - 1 - coord_y, coord_y)
        turned = bit_y == 0
        coord_x = np.where(turned, moved_y, moved_x) + level * bit_x
        coord_y = np.where(turned, moved_x, moved_y) + level * bit_y
        remain = remain // 4
        level = level * 2
    position = np.arange(count_x * count_y)
    along_x = coord_x[position % square] + (position // square) * count_y
    along_y = coord_y[position % square]
    return [int(d) for d in along_x * count_y + along_y]


def conv_kernel(shifted_ref, features_ref, weight_ref, linear_ref, out_ref):
    rows = features_ref.shape[0]
    side = shifted_ref.shape[2]
    width = features_ref.shape[-1]
    first = pl.program_id(0) * rows
    total = jnp.zeros((rows * side, width), jnp.float32)
    for offset in range(9):
        step_x = offset // 3
        step_y = offset % 3
        window = shifted_ref[step_y, pl.ds(first + step_x, rows)].reshape(rows * side, width)
        total += jnp.dot(window, weight_ref[offset], preferred_element_type=jnp.float32)
    linear = jnp.dot(total.astype(jnp.bfloat16), linear_ref[...], preferred_element_type=jnp.float32)
    base = features_ref[...].reshape(rows * side, width).astype(jnp.float32)
    out_ref[...] = (base + layer_norm(linear)).astype(out_ref.dtype)


def encode(padded, features, conv_weight, cpe_linear):
    span_x, span_y, width = features.shape
    shifted = jnp.stack([padded[:, step : step + span_y] for step in range(3)])
    rows = 8
    return pl.pallas_call(
        conv_kernel,
        grid=(span_x // rows,),
        in_specs=[
            pl.BlockSpec(memory_space=pltpu.VMEM),
            pl.BlockSpec((rows, span_y, width), lambda i: (i, 0, 0)),
            pl.BlockSpec(conv_weight.shape, lambda i: (0, 0, 0)),
            pl.BlockSpec(cpe_linear.shape, lambda i: (0, 0)),
        ],
        out_specs=pl.BlockSpec((rows * span_y, width), lambda i: (i, 0)),
        out_shape=jax.ShapeDtypeStruct((span_x * span_y, width), features.dtype),
    )(shifted, features, conv_weight, cpe_linear)


def shards(
    features,
    occupied,
    voxel_order,
    conv_weight,
    cpe_linear,
    qkv_weight,
    proj_weight,
    up_weight,
    down_weight,
):
    span_x, span_y, width = features.shape
    cells = span_x * span_y
    occ_flat = occupied.reshape(cells)
    mine = jnp.sum(occ_flat, dtype=jnp.int32)
    masked = features * occupied[:, :, None].astype(jnp.bfloat16)
    padded = with_halo(masked, (("gx", 0), ("gy", 1)), 1)
    encoded = encode(padded, features, conv_weight, cpe_linear)
    order = voxel_order[0]
    voxel = jnp.arange(cells, dtype=jnp.int32)
    _, rank_of = lax.sort_key_val(order, voxel)
    key = (1 - occ_flat) * cells + rank_of
    _, listed_voxel = lax.sort_key_val(key, voxel)
    capacity = CAP
    list_index = jnp.arange(LIVE + 2 * capacity, dtype=jnp.int32)
    picked = jnp.where(list_index < mine, listed_voxel[: LIVE + 2 * capacity], -1)
    list_rows, counts = gather_counts(mine, encoded, picked)
    devices = counts.shape[0]
    count_x = lax.axis_size("gx")
    count_y = lax.axis_size("gy")
    here_x = lax.axis_index("gx")
    here_y = lax.axis_index("gy")
    ranks = block_curve(count_x, count_y)
    position = ranks[here_x * count_y + here_y]
    by_position = jnp.zeros((devices,), jnp.int32).at[ranks].set(counts)
    starts = jnp.cumsum(by_position, dtype=jnp.int32) - by_position
    start_here = starts[position]
    excess = start_here - position * LIVE
    beyond = start_here + mine - (position + 1) * LIVE
    slot = jnp.arange(capacity, dtype=jnp.int32)
    empty = jnp.zeros((capacity, width), jnp.bfloat16)
    extended = jnp.concatenate([empty, list_rows], axis=0)
    mine_rows = lax.dynamic_slice_in_dim(extended, capacity - excess, LIVE, 0)
    to_prev = jnp.where((slot < -excess)[:, None], list_rows[:capacity], empty)
    to_next = jnp.where(
        (slot < beyond)[:, None], lax.dynamic_slice_in_dim(list_rows, LIVE - excess, capacity, 0), empty
    )
    device_at = curve_tables(count_x, count_y)
    forward = [(device_at[p], device_at[p + 1]) for p in range(devices - 1)]
    backward = [(target, source) for source, target in forward]
    from_prev = lax.ppermute(to_next, ("gx", "gy"), forward)
    from_next = lax.ppermute(to_prev, ("gx", "gy"), backward)
    from_prev = jnp.where((slot < excess)[:, None], from_prev, empty)
    from_next = jnp.where((slot < -beyond)[:, None], from_next, empty)
    leading = jnp.concatenate(
        [from_prev, jnp.zeros((LIVE - capacity, width), jnp.bfloat16)], axis=0
    )
    trailing = lax.dynamic_slice_in_dim(
        jnp.concatenate([jnp.zeros((LIVE, width), jnp.bfloat16), from_next], axis=0),
        -beyond,
        LIVE,
        0,
    )
    owned = mine_rows + leading + trailing
    return attention_block(owned, qkv_weight, proj_weight, up_weight, down_weight)


def solution(mesh):
    return jax.shard_map(
        shards,
        mesh=mesh,
        in_specs=(
            P("gx", "gy", None),
            P("gx", "gy"),
            P(("gx", "gy"), None),
            P(),
            P(),
            P(),
            P(),
            P(),
            P(),
        ),
        out_specs=P(("gx", "gy"), None),
        check_vma=False,
    )
```

```python
import functools
import math

import jax
import numpy as np
import jax.numpy as jnp
from jax import lax
from jax.experimental import pallas as pl
from jax.experimental.pallas import tpu as pltpu
from jax.sharding import PartitionSpec as P

HEADS = 8
PATCH = 1024
LIVE = 2048
CAP = 256
HD = 32


def with_halo(block, sides, width):
    for axis, dim in sides:
        count = lax.axis_size(axis)
        forward = [(i, i + 1) for i in range(count - 1)]
        backward = [(target, source) for source, target in forward]
        low = lax.ppermute(
            lax.slice_in_dim(block, block.shape[dim] - width, None, axis=dim), axis, forward
        )
        high = lax.ppermute(lax.slice_in_dim(block, 0, width, axis=dim), axis, backward)
        block = jnp.concatenate([low, block, high], axis=dim)
    return block


def passed_along(block, axis, distance):
    devices = range(lax.axis_size(axis))
    route = [(i - distance, i) for i in devices if i - distance in devices]
    return lax.ppermute(block, axis, route)


def hilbert_points(side):
    index = jnp.arange(side * side, dtype=jnp.int32)
    coord_x = jnp.zeros((side * side,), jnp.int32)
    coord_y = jnp.zeros((side * side,), jnp.int32)
    remain = index
    level = 1
    while level < side:
        bit_x = remain // 2 % 2
        bit_y = jnp.bitwise_xor(remain, bit_x) % 2
        mirror = (bit_y == 0) & (bit_x == 1)
        moved_x = jnp.where(mirror, level - 1 - coord_x, coord_x)
        moved_y = jnp.where(mirror, level - 1 - coord_y, coord_y)
        turned = bit_y == 0
        coord_x = jnp.where(turned, moved_y, moved_x) + level * bit_x
        coord_y = jnp.where(turned, moved_x, moved_y) + level * bit_y
        remain = remain // 4
        level = level * 2
    return (coord_x, coord_y)


def block_curve(count_x, count_y):
    total = count_x * count_y
    square = count_y * count_y
    position = jnp.arange(total, dtype=jnp.int32)
    half = position // square
    inner_x, inner_y = hilbert_points(count_y)
    along_x = inner_x[position % square] + half * count_y
    along_y = inner_y[position % square]
    device = along_x * count_y + along_y
    return jnp.zeros((total,), jnp.int32).at[device].set(position)


def layer_norm(values):
    centre = values - jnp.mean(values, axis=-1, keepdims=True)
    spread = jnp.mean(centre * centre, axis=-1, keepdims=True)
    return centre * lax.rsqrt(spread + 1e-05)


def attend_patch(rows, qkv_weight, proj_weight, up_weight, down_weight):
    base = rows.astype(jnp.float32)
    normed = layer_norm(base).astype(jnp.bfloat16)
    projected = jnp.dot(normed, qkv_weight, preferred_element_type=jnp.float32).astype(jnp.bfloat16)
    width = rows.shape[1]
    count = rows.shape[0]
    query = projected[:, :width].reshape(count, HEADS, HD)
    keyset = projected[:, width : 2 * width].reshape(count, HEADS, HD)
    valueset = projected[:, 2 * width :].reshape(count, HEADS, HD)
    scores = jnp.einsum("qhd,khd->hqk", query, keyset, preferred_element_type=jnp.float32) * (
        1.0 / math.sqrt(HD)
    )
    largest = jnp.max(scores, axis=-1, keepdims=True)
    expo = jnp.exp(scores - largest)
    weights = (expo / jnp.sum(expo, axis=-1, keepdims=True)).astype(jnp.bfloat16)
    attended = jnp.einsum(
        "hqk,khd->qhd", weights, valueset, preferred_element_type=jnp.float32
    ).astype(jnp.bfloat16)
    middle = base + jnp.dot(
        attended.reshape(count, width), proj_weight, preferred_element_type=jnp.float32
    )
    second = layer_norm(middle).astype(jnp.bfloat16)
    hidden = jax.nn.gelu(
        jnp.dot(second, up_weight, preferred_element_type=jnp.float32), approximate=True
    ).astype(jnp.bfloat16)
    final = middle + jnp.dot(hidden, down_weight, preferred_element_type=jnp.float32)
    return final.astype(jnp.bfloat16)


def onehot_gather_kernel(index_ref, table_ref, out_ref, acc_ref):
    rows = index_ref.shape[0]
    chunk = 512
    wanted = index_ref[...]
    acc_ref[...] = jnp.zeros_like(acc_ref)
    for part in range(table_ref.shape[0] // chunk):
        ids = lax.broadcasted_iota(jnp.int32, (rows, chunk), 1) + part * chunk
        pick = jnp.where(wanted == ids, 1.0, 0.0).astype(jnp.bfloat16)
        acc_ref[...] += jnp.dot(
            pick, table_ref[pl.ds(part * chunk, chunk), :], preferred_element_type=jnp.float32
        )
    out_ref[...] = acc_ref[...].astype(out_ref.dtype)


def onehot_gather(table, index):
    count = index.shape[0]
    width = table.shape[1]
    tile = 256
    return pl.pallas_call(
        onehot_gather_kernel,
        grid=(count // tile,),
        in_specs=[
            pl.BlockSpec((tile, 1), lambda i: (i, 0)),
            pl.BlockSpec(table.shape, lambda i: (0, 0)),
        ],
        out_specs=pl.BlockSpec((tile, width), lambda i: (i, 0)),
        out_shape=jax.ShapeDtypeStruct((count, width), table.dtype),
        scratch_shapes=[pltpu.VMEM((tile, width), jnp.float32)],
    )(index.reshape(count, 1), table)


MESH = pl.DeviceIdType.MESH


def gather_rows(index_ref, table_ref, out_ref, first, last):
    tile = 256
    chunk = 512

    def one_tile(i, carry):
        rows = pl.ds(pl.multiple_of(i * tile, tile), tile)
        wanted = index_ref[rows, :]
        total = jnp.zeros((tile, out_ref.shape[1]), jnp.float32)
        for part in range(table_ref.shape[0] // chunk):
            ids = lax.broadcasted_iota(jnp.int32, (tile, chunk), 1) + part * chunk
            pick = jnp.where(wanted == ids, 1.0, 0.0).astype(jnp.bfloat16)
            total += jnp.dot(
                pick, table_ref[pl.ds(part * chunk, chunk), :], preferred_element_type=jnp.float32
            )
        out_ref[rows, :] = total.astype(out_ref.dtype)
        return carry

    lax.fori_loop(first, last, one_tile, 0)


def count_gather_kernel(nx, ny, index_ref, table_ref, mine_ref, rows_ref, out_ref, row_buf, grid_buf, send1, recv1, send2, recv2, own_sem):
    me_x = lax.axis_index("gx")
    me_y = lax.axis_index("gy")
    barrier = pltpu.get_barrier_semaphore()
    for k in range(1, ny):
        pl.semaphore_signal(
            barrier, inc=1, device_id=(me_x, lax.rem(me_y + k, ny)), device_id_type=MESH
        )
    for k in range(1, nx):
        pl.semaphore_signal(
            barrier, inc=1, device_id=(lax.rem(me_x + k, nx), me_y), device_id_type=MESH
        )
    pl.semaphore_wait(barrier, nx + ny - 2)

    own = pltpu.make_async_copy(mine_ref, row_buf.at[pl.ds(me_y, 1)], own_sem.at[0])
    own.start()
    for k in range(1, ny):
        pltpu.make_async_remote_copy(
            src_ref=mine_ref,
            dst_ref=row_buf.at[pl.ds(me_y, 1)],
            send_sem=send1.at[k],
            recv_sem=recv1.at[k],
            device_id=(me_x, lax.rem(me_y + k, ny)),
            device_id_type=MESH,
        ).start()
    tiles = rows_ref.shape[0] // 256
    gather_rows(index_ref, table_ref, rows_ref, 0, tiles // 2)
    own.wait()
    for k in range(1, ny):
        sender = lax.rem(me_y - k + ny, ny)
        copy = pltpu.make_async_remote_copy(
            src_ref=mine_ref,
            dst_ref=row_buf.at[pl.ds(sender, 1)],
            send_sem=send1.at[k],
            recv_sem=recv1.at[k],
            device_id=(me_x, sender),
            device_id_type=MESH,
        )
        copy.wait_send()
        copy.wait_recv()

    own = pltpu.make_async_copy(row_buf, grid_buf.at[me_x], own_sem.at[1])
    own.start()
    for k in range(1, nx):
        pltpu.make_async_remote_copy(
            src_ref=row_buf,
            dst_ref=grid_buf.at[me_x],
            send_sem=send2.at[k],
            recv_sem=recv2.at[k],
            device_id=(lax.rem(me_x + k, nx), me_y),
            device_id_type=MESH,
        ).start()
    gather_rows(index_ref, table_ref, rows_ref, tiles // 2, tiles)
    own.wait()
    for k in range(1, nx):
        sender = lax.rem(me_x - k + nx, nx)
        copy = pltpu.make_async_remote_copy(
            src_ref=row_buf,
            dst_ref=grid_buf.at[sender],
            send_sem=send2.at[k],
            recv_sem=recv2.at[k],
            device_id=(sender, me_y),
            device_id_type=MESH,
        )
        copy.wait_send()
        copy.wait_recv()
    out_ref[...] = grid_buf[...]


def gather_counts(mine, table, index):
    nx = lax.axis_size("gx")
    ny = lax.axis_size("gy")
    lanes = 128
    listed, grid = pl.pallas_call(
        functools.partial(count_gather_kernel, nx, ny),
        out_shape=(
            jax.ShapeDtypeStruct((index.shape[0], table.shape[1]), table.dtype),
            jax.ShapeDtypeStruct((nx, ny, lanes), jnp.int32),
        ),
        in_specs=[pl.BlockSpec(memory_space=pltpu.VMEM)] * 3,
        out_specs=(pl.BlockSpec(memory_space=pltpu.VMEM), pl.BlockSpec(memory_space=pltpu.VMEM)),
        scratch_shapes=[
            pltpu.VMEM((ny, lanes), jnp.int32),
            pltpu.VMEM((nx, ny, lanes), jnp.int32),
            pltpu.SemaphoreType.DMA((ny,)),
            pltpu.SemaphoreType.DMA((ny,)),
            pltpu.SemaphoreType.DMA((nx,)),
            pltpu.SemaphoreType.DMA((nx,)),
            pltpu.SemaphoreType.DMA((2,)),
        ],
        compiler_params=pltpu.CompilerParams(collective_id=0, has_side_effects=True),
    )(index.reshape(-1, 1), table, jnp.broadcast_to(mine, (1, lanes)))
    return listed, grid[:, :, 0].reshape(nx * ny)


def attention_kernel(q_ref, k_ref, v_ref, base_ref, proj_ref, up_ref, down_ref, out_ref):
    query = q_ref[...]
    keyset = k_ref[...]
    valueset = v_ref[...]
    width = query.shape[1]
    head_of = lax.broadcasted_iota(jnp.int32, (1, width), 1) // HD
    attended = jnp.zeros((query.shape[0], width), jnp.float32)
    for head in range(HEADS):
        mine = head_of == head
        scores = lax.dot_general(
            jnp.where(mine, query, jnp.zeros_like(query)),
            keyset,
            (((1,), (1,)), ((), ())),
            preferred_element_type=jnp.float32,
        ) * (1.0 / math.sqrt(HD))
        largest = jnp.max(scores, axis=-1, keepdims=True)
        expo = jnp.exp(scores - largest)
        scale = 1.0 / jnp.sum(expo, axis=-1, keepdims=True)
        mixed = jnp.dot(expo.astype(jnp.bfloat16), valueset, preferred_element_type=jnp.float32)
        attended = jnp.where(mine, mixed * scale, attended)
    middle = base_ref[...].astype(jnp.float32) + jnp.dot(
        attended.astype(jnp.bfloat16), proj_ref[...], preferred_element_type=jnp.float32
    )
    second = layer_norm(middle).astype(jnp.bfloat16)
    hidden = jax.nn.gelu(
        jnp.dot(second, up_ref[...], preferred_element_type=jnp.float32), approximate=True
    ).astype(jnp.bfloat16)
    final = middle + jnp.dot(hidden, down_ref[...], preferred_element_type=jnp.float32)
    out_ref[...] = final.astype(out_ref.dtype)


def attention_block(rows, qkv_weight, proj_weight, up_weight, down_weight):
    count, width = rows.shape
    base = rows.astype(jnp.float32)
    normed = layer_norm(base).astype(jnp.bfloat16)
    projected = jnp.dot(normed, qkv_weight, preferred_element_type=jnp.float32).astype(jnp.bfloat16)
    tile = 512
    tiles = PATCH // tile
    grid = (count // PATCH, tiles)
    return pl.pallas_call(
        attention_kernel,
        grid=grid,
        in_specs=[
            pl.BlockSpec((tile, width), lambda p, t: (p * tiles + t, 0)),
            pl.BlockSpec((PATCH, width), lambda p, t: (p, 1)),
            pl.BlockSpec((PATCH, width), lambda p, t: (p, 2)),
            pl.BlockSpec((tile, width), lambda p, t: (p * tiles + t, 0)),
            pl.BlockSpec((width, width), lambda p, t: (0, 0)),
            pl.BlockSpec(up_weight.shape, lambda p, t: (0, 0)),
            pl.BlockSpec(down_weight.shape, lambda p, t: (0, 0)),
        ],
        out_specs=pl.BlockSpec((tile, width), lambda p, t: (p * tiles + t, 0)),
        out_shape=jax.ShapeDtypeStruct((count, width), rows.dtype),
    )(projected, projected, projected, rows, proj_weight, up_weight, down_weight)


def feed_forward(middle, up_weight, down_weight):
    second = layer_norm(middle).astype(jnp.bfloat16)
    hidden = jax.nn.gelu(
        jnp.dot(second, up_weight, preferred_element_type=jnp.float32), approximate=True
    ).astype(jnp.bfloat16)
    final = middle + jnp.dot(hidden, down_weight, preferred_element_type=jnp.float32)
    return final.astype(jnp.bfloat16)


def curve_tables(count_x, count_y):
    square = count_y * count_y
    index = np.arange(square)
    coord_x = np.zeros(square, np.int64)
    coord_y = np.zeros(square, np.int64)
    remain = index.copy()
    level = 1
    while level < count_y:
        bit_x = remain // 2 % 2
        bit_y = np.bitwise_xor(remain, bit_x) % 2
        mirror = (bit_y == 0) & (bit_x == 1)
        moved_x = np.where(mirror, level - 1 - coord_x, coord_x)
        moved_y = np.where(mirror, level - 1 - coord_y, coord_y)
        turned = bit_y == 0
        coord_x = np.where(turned, moved_y, moved_x) + level * bit_x
        coord_y = np.where(turned, moved_x, moved_y) + level * bit_y
        remain = remain // 4
        level = level * 2
    position = np.arange(count_x * count_y)
    along_x = coord_x[position % square] + (position // square) * count_y
    along_y = coord_y[position % square]
    return [int(d) for d in along_x * count_y + along_y]


def conv_kernel(shifted_ref, features_ref, weight_ref, linear_ref, out_ref):
    rows = features_ref.shape[0]
    side = features_ref.shape[1]
    width = features_ref.shape[-1]
    first = pl.program_id(0) * rows
    total = jnp.zeros((rows * side, width), jnp.float32)
    for offset in range(9):
        step_x = offset // 3
        step_y = offset % 3
        window = shifted_ref[pl.ds(first + step_x, rows), pl.ds(step_y, side)].reshape(rows * side, width)
        total += jnp.dot(window, weight_ref[offset], preferred_element_type=jnp.float32)
    linear = jnp.dot(total.astype(jnp.bfloat16), linear_ref[...], preferred_element_type=jnp.float32)
    base = features_ref[...].reshape(rows * side, width).astype(jnp.float32)
    out_ref[...] = (base + layer_norm(linear)).astype(out_ref.dtype)


def encode(padded, features, conv_weight, cpe_linear):
    span_x, span_y, width = features.shape
    shifted = padded
    rows = 8
    return pl.pallas_call(
        conv_kernel,
        grid=(span_x // rows,),
        in_specs=[
            pl.BlockSpec(memory_space=pltpu.VMEM),
            pl.BlockSpec((rows, span_y, width), lambda i: (i, 0, 0)),
            pl.BlockSpec(conv_weight.shape, lambda i: (0, 0, 0)),
            pl.BlockSpec(cpe_linear.shape, lambda i: (0, 0)),
        ],
        out_specs=pl.BlockSpec((rows * span_y, width), lambda i: (i, 0)),
        out_shape=jax.ShapeDtypeStruct((span_x * span_y, width), features.dtype),
    )(shifted, features, conv_weight, cpe_linear)


def shards(
    features,
    occupied,
    voxel_order,
    conv_weight,
    cpe_linear,
    qkv_weight,
    proj_weight,
    up_weight,
    down_weight,
):
    span_x, span_y, width = features.shape
    cells = span_x * span_y
    occ_flat = occupied.reshape(cells)
    mine = jnp.sum(occ_flat, dtype=jnp.int32)
    masked = features * occupied[:, :, None].astype(jnp.bfloat16)
    padded = with_halo(masked, (("gx", 0), ("gy", 1)), 1)
    encoded = encode(padded, features, conv_weight, cpe_linear)
    order = voxel_order[0]
    voxel = jnp.arange(cells, dtype=jnp.int32)
    _, rank_of = lax.sort_key_val(order, voxel)
    key = (1 - occ_flat) * cells + rank_of
    _, listed_voxel = lax.sort_key_val(key, voxel)
    capacity = CAP
    list_index = jnp.arange(LIVE + 2 * capacity, dtype=jnp.int32)
    picked = jnp.where(list_index < mine, listed_voxel[: LIVE + 2 * capacity], -1)
    list_rows, counts = gather_counts(mine, encoded, picked)
    devices = counts.shape[0]
    count_x = lax.axis_size("gx")
    count_y = lax.axis_size("gy")
    here_x = lax.axis_index("gx")
    here_y = lax.axis_index("gy")
    ranks = block_curve(count_x, count_y)
    position = ranks[here_x * count_y + here_y]
    by_position = jnp.zeros((devices,), jnp.int32).at[ranks].set(counts)
    starts = jnp.cumsum(by_position, dtype=jnp.int32) - by_position
    start_here = starts[position]
    excess = start_here - position * LIVE
    beyond = start_here + mine - (position + 1) * LIVE
    slot = jnp.arange(capacity, dtype=jnp.int32)
    empty = jnp.zeros((capacity, width), jnp.bfloat16)
    extended = jnp.concatenate([empty, list_rows], axis=0)
    mine_rows = lax.dynamic_slice_in_dim(extended, capacity - excess, LIVE, 0)
    to_prev = jnp.where((slot < -excess)[:, None], list_rows[:capacity], empty)
    to_next = jnp.where(
        (slot < beyond)[:, None], lax.dynamic_slice_in_dim(list_rows, LIVE - excess, capacity, 0), empty
    )
    device_at = curve_tables(count_x, count_y)
    forward = [(device_at[p], device_at[p + 1]) for p in range(devices - 1)]
    backward = [(target, source) for source, target in forward]
    from_prev = lax.ppermute(to_next, ("gx", "gy"), forward)
    from_next = lax.ppermute(to_prev, ("gx", "gy"), backward)
    from_prev = jnp.where((slot < excess)[:, None], from_prev, empty)
    from_next = jnp.where((slot < -beyond)[:, None], from_next, empty)
    leading = jnp.concatenate(
        [from_prev, jnp.zeros((LIVE - capacity, width), jnp.bfloat16)], axis=0
    )
    trailing = lax.dynamic_slice_in_dim(
        jnp.concatenate([jnp.zeros((LIVE, width), jnp.bfloat16), from_next], axis=0),
        -beyond,
        LIVE,
        0,
    )
    owned = mine_rows + leading + trailing
    return attention_block(owned, qkv_weight, proj_weight, up_weight, down_weight)


def solution(mesh):
    return jax.shard_map(
        shards,
        mesh=mesh,
        in_specs=(
            P("gx", "gy", None),
            P("gx", "gy"),
            P(("gx", "gy"), None),
            P(),
            P(),
            P(),
            P(),
            P(),
            P(),
        ),
        out_specs=P(("gx", "gy"), None),
        check_vma=False,
    )
```

```python
import functools
import math

import jax
import numpy as np
import jax.numpy as jnp
from jax import lax
from jax.experimental import pallas as pl
from jax.experimental.pallas import tpu as pltpu
from jax.sharding import PartitionSpec as P

HEADS = 8
PATCH = 1024
LIVE = 2048
CAP = 256
HD = 32


def with_halo(block, sides, width):
    for axis, dim in sides:
        count = lax.axis_size(axis)
        forward = [(i, i + 1) for i in range(count - 1)]
        backward = [(target, source) for source, target in forward]
        low = lax.ppermute(
            lax.slice_in_dim(block, block.shape[dim] - width, None, axis=dim), axis, forward
        )
        high = lax.ppermute(lax.slice_in_dim(block, 0, width, axis=dim), axis, backward)
        block = jnp.concatenate([low, block, high], axis=dim)
    return block


def passed_along(block, axis, distance):
    devices = range(lax.axis_size(axis))
    route = [(i - distance, i) for i in devices if i - distance in devices]
    return lax.ppermute(block, axis, route)


def hilbert_points(side):
    index = jnp.arange(side * side, dtype=jnp.int32)
    coord_x = jnp.zeros((side * side,), jnp.int32)
    coord_y = jnp.zeros((side * side,), jnp.int32)
    remain = index
    level = 1
    while level < side:
        bit_x = remain // 2 % 2
        bit_y = jnp.bitwise_xor(remain, bit_x) % 2
        mirror = (bit_y == 0) & (bit_x == 1)
        moved_x = jnp.where(mirror, level - 1 - coord_x, coord_x)
        moved_y = jnp.where(mirror, level - 1 - coord_y, coord_y)
        turned = bit_y == 0
        coord_x = jnp.where(turned, moved_y, moved_x) + level * bit_x
        coord_y = jnp.where(turned, moved_x, moved_y) + level * bit_y
        remain = remain // 4
        level = level * 2
    return (coord_x, coord_y)


def block_curve(count_x, count_y):
    total = count_x * count_y
    square = count_y * count_y
    position = jnp.arange(total, dtype=jnp.int32)
    half = position // square
    inner_x, inner_y = hilbert_points(count_y)
    along_x = inner_x[position % square] + half * count_y
    along_y = inner_y[position % square]
    device = along_x * count_y + along_y
    return jnp.zeros((total,), jnp.int32).at[device].set(position)


def layer_norm(values):
    centre = values - jnp.mean(values, axis=-1, keepdims=True)
    spread = jnp.mean(centre * centre, axis=-1, keepdims=True)
    return centre * lax.rsqrt(spread + 1e-05)


def attend_patch(rows, qkv_weight, proj_weight, up_weight, down_weight):
    base = rows.astype(jnp.float32)
    normed = layer_norm(base).astype(jnp.bfloat16)
    projected = jnp.dot(normed, qkv_weight, preferred_element_type=jnp.float32).astype(jnp.bfloat16)
    width = rows.shape[1]
    count = rows.shape[0]
    query = projected[:, :width].reshape(count, HEADS, HD)
    keyset = projected[:, width : 2 * width].reshape(count, HEADS, HD)
    valueset = projected[:, 2 * width :].reshape(count, HEADS, HD)
    scores = jnp.einsum("qhd,khd->hqk", query, keyset, preferred_element_type=jnp.float32) * (
        1.0 / math.sqrt(HD)
    )
    largest = jnp.max(scores, axis=-1, keepdims=True)
    expo = jnp.exp(scores - largest)
    weights = (expo / jnp.sum(expo, axis=-1, keepdims=True)).astype(jnp.bfloat16)
    attended = jnp.einsum(
        "hqk,khd->qhd", weights, valueset, preferred_element_type=jnp.float32
    ).astype(jnp.bfloat16)
    middle = base + jnp.dot(
        attended.reshape(count, width), proj_weight, preferred_element_type=jnp.float32
    )
    second = layer_norm(middle).astype(jnp.bfloat16)
    hidden = jax.nn.gelu(
        jnp.dot(second, up_weight, preferred_element_type=jnp.float32), approximate=True
    ).astype(jnp.bfloat16)
    final = middle + jnp.dot(hidden, down_weight, preferred_element_type=jnp.float32)
    return final.astype(jnp.bfloat16)


def onehot_gather_kernel(index_ref, table_ref, out_ref, acc_ref):
    rows = index_ref.shape[0]
    chunk = 512
    wanted = index_ref[...]
    acc_ref[...] = jnp.zeros_like(acc_ref)
    for part in range(table_ref.shape[0] // chunk):
        ids = lax.broadcasted_iota(jnp.int32, (rows, chunk), 1) + part * chunk
        pick = jnp.where(wanted == ids, 1.0, 0.0).astype(jnp.bfloat16)
        acc_ref[...] += jnp.dot(
            pick, table_ref[pl.ds(part * chunk, chunk), :], preferred_element_type=jnp.float32
        )
    out_ref[...] = acc_ref[...].astype(out_ref.dtype)


def onehot_gather(table, index):
    count = index.shape[0]
    width = table.shape[1]
    tile = 256
    return pl.pallas_call(
        onehot_gather_kernel,
        grid=(count // tile,),
        in_specs=[
            pl.BlockSpec((tile, 1), lambda i: (i, 0)),
            pl.BlockSpec(table.shape, lambda i: (0, 0)),
        ],
        out_specs=pl.BlockSpec((tile, width), lambda i: (i, 0)),
        out_shape=jax.ShapeDtypeStruct((count, width), table.dtype),
        scratch_shapes=[pltpu.VMEM((tile, width), jnp.float32)],
    )(index.reshape(count, 1), table)


MESH = pl.DeviceIdType.MESH


def gather_rows(index_ref, table_ref, out_ref, first, last):
    tile = 256
    chunk = 512

    def one_tile(i, carry):
        rows = pl.ds(pl.multiple_of(i * tile, tile), tile)
        wanted = index_ref[:, rows]
        total = jnp.zeros((tile, out_ref.shape[1]), jnp.float32)
        for part in range(table_ref.shape[0] // chunk):
            ids = lax.broadcasted_iota(jnp.int32, (chunk, tile), 0) + part * chunk
            pick = jnp.where(wanted == ids, 1.0, 0.0).astype(jnp.bfloat16)
            total += lax.dot_general(
                pick,
                table_ref[pl.ds(part * chunk, chunk), :],
                (((0,), (0,)), ((), ())),
                preferred_element_type=jnp.float32,
            )
        out_ref[rows, :] = total.astype(out_ref.dtype)
        return carry

    lax.fori_loop(first, last, one_tile, 0)


def count_gather_kernel(nx, ny, index_ref, table_ref, mine_ref, rows_ref, out_ref, row_buf, grid_buf, send1, recv1, send2, recv2, own_sem):
    me_x = lax.axis_index("gx")
    me_y = lax.axis_index("gy")
    barrier = pltpu.get_barrier_semaphore()
    for k in range(1, ny):
        pl.semaphore_signal(
            barrier, inc=1, device_id=(me_x, lax.rem(me_y + k, ny)), device_id_type=MESH
        )
    for k in range(1, nx):
        pl.semaphore_signal(
            barrier, inc=1, device_id=(lax.rem(me_x + k, nx), me_y), device_id_type=MESH
        )
    pl.semaphore_wait(barrier, nx + ny - 2)

    own = pltpu.make_async_copy(mine_ref, row_buf.at[pl.ds(me_y, 1)], own_sem.at[0])
    own.start()
    for k in range(1, ny):
        pltpu.make_async_remote_copy(
            src_ref=mine_ref,
            dst_ref=row_buf.at[pl.ds(me_y, 1)],
            send_sem=send1.at[k],
            recv_sem=recv1.at[k],
            device_id=(me_x, lax.rem(me_y + k, ny)),
            device_id_type=MESH,
        ).start()
    tiles = rows_ref.shape[0] // 256
    gather_rows(index_ref, table_ref, rows_ref, 0, tiles // 2)
    own.wait()
    for k in range(1, ny):
        sender = lax.rem(me_y - k + ny, ny)
        copy = pltpu.make_async_remote_copy(
            src_ref=mine_ref,
            dst_ref=row_buf.at[pl.ds(sender, 1)],
            send_sem=send1.at[k],
            recv_sem=recv1.at[k],
            device_id=(me_x, sender),
            device_id_type=MESH,
        )
        copy.wait_send()
        copy.wait_recv()

    own = pltpu.make_async_copy(row_buf, grid_buf.at[me_x], own_sem.at[1])
    own.start()
    for k in range(1, nx):
        pltpu.make_async_remote_copy(
            src_ref=row_buf,
            dst_ref=grid_buf.at[me_x],
            send_sem=send2.at[k],
            recv_sem=recv2.at[k],
            device_id=(lax.rem(me_x + k, nx), me_y),
            device_id_type=MESH,
        ).start()
    gather_rows(index_ref, table_ref, rows_ref, tiles // 2, tiles)
    own.wait()
    for k in range(1, nx):
        sender = lax.rem(me_x - k + nx, nx)
        copy = pltpu.make_async_remote_copy(
            src_ref=row_buf,
            dst_ref=grid_buf.at[sender],
            send_sem=send2.at[k],
            recv_sem=recv2.at[k],
            device_id=(sender, me_y),
            device_id_type=MESH,
        )
        copy.wait_send()
        copy.wait_recv()
    out_ref[...] = grid_buf[...]


def gather_counts(mine, table, index):
    nx = lax.axis_size("gx")
    ny = lax.axis_size("gy")
    lanes = 128
    listed, grid = pl.pallas_call(
        functools.partial(count_gather_kernel, nx, ny),
        out_shape=(
            jax.ShapeDtypeStruct((index.shape[0], table.shape[1]), table.dtype),
            jax.ShapeDtypeStruct((nx, ny, lanes), jnp.int32),
        ),
        in_specs=[pl.BlockSpec(memory_space=pltpu.VMEM)] * 3,
        out_specs=(pl.BlockSpec(memory_space=pltpu.VMEM), pl.BlockSpec(memory_space=pltpu.VMEM)),
        scratch_shapes=[
            pltpu.VMEM((ny, lanes), jnp.int32),
            pltpu.VMEM((nx, ny, lanes), jnp.int32),
            pltpu.SemaphoreType.DMA((ny,)),
            pltpu.SemaphoreType.DMA((ny,)),
            pltpu.SemaphoreType.DMA((nx,)),
            pltpu.SemaphoreType.DMA((nx,)),
            pltpu.SemaphoreType.DMA((2,)),
        ],
        compiler_params=pltpu.CompilerParams(collective_id=0, has_side_effects=True),
    )(index.reshape(1, -1), table, jnp.broadcast_to(mine, (1, lanes)))
    return listed, grid[:, :, 0].reshape(nx * ny)


def attention_kernel(q_ref, k_ref, v_ref, base_ref, proj_ref, up_ref, down_ref, out_ref):
    query = q_ref[...]
    keyset = k_ref[...]
    valueset = v_ref[...]
    width = query.shape[1]
    head_of = lax.broadcasted_iota(jnp.int32, (1, width), 1) // HD
    attended = jnp.zeros((query.shape[0], width), jnp.float32)
    for head in range(HEADS):
        mine = head_of == head
        scores = lax.dot_general(
            jnp.where(mine, query, jnp.zeros_like(query)),
            keyset,
            (((1,), (1,)), ((), ())),
            preferred_element_type=jnp.float32,
        ) * (1.0 / math.sqrt(HD))
        largest = jnp.max(scores, axis=-1, keepdims=True)
        expo = jnp.exp(scores - largest)
        scale = 1.0 / jnp.sum(expo, axis=-1, keepdims=True)
        mixed = jnp.dot(expo.astype(jnp.bfloat16), valueset, preferred_element_type=jnp.float32)
        attended = jnp.where(mine, mixed * scale, attended)
    middle = base_ref[...].astype(jnp.float32) + jnp.dot(
        attended.astype(jnp.bfloat16), proj_ref[...], preferred_element_type=jnp.float32
    )
    second = layer_norm(middle).astype(jnp.bfloat16)
    hidden = jax.nn.gelu(
        jnp.dot(second, up_ref[...], preferred_element_type=jnp.float32), approximate=True
    ).astype(jnp.bfloat16)
    final = middle + jnp.dot(hidden, down_ref[...], preferred_element_type=jnp.float32)
    out_ref[...] = final.astype(out_ref.dtype)


def attention_block(rows, qkv_weight, proj_weight, up_weight, down_weight):
    count, width = rows.shape
    base = rows.astype(jnp.float32)
    normed = layer_norm(base).astype(jnp.bfloat16)
    projected = jnp.dot(normed, qkv_weight, preferred_element_type=jnp.float32).astype(jnp.bfloat16)
    tile = 512
    tiles = PATCH // tile
    grid = (count // PATCH, tiles)
    return pl.pallas_call(
        attention_kernel,
        grid=grid,
        in_specs=[
            pl.BlockSpec((tile, width), lambda p, t: (p * tiles + t, 0)),
            pl.BlockSpec((PATCH, width), lambda p, t: (p, 1)),
            pl.BlockSpec((PATCH, width), lambda p, t: (p, 2)),
            pl.BlockSpec((tile, width), lambda p, t: (p * tiles + t, 0)),
            pl.BlockSpec((width, width), lambda p, t: (0, 0)),
            pl.BlockSpec(up_weight.shape, lambda p, t: (0, 0)),
            pl.BlockSpec(down_weight.shape, lambda p, t: (0, 0)),
        ],
        out_specs=pl.BlockSpec((tile, width), lambda p, t: (p * tiles + t, 0)),
        out_shape=jax.ShapeDtypeStruct((count, width), rows.dtype),
    )(projected, projected, projected, rows, proj_weight, up_weight, down_weight)


def feed_forward(middle, up_weight, down_weight):
    second = layer_norm(middle).astype(jnp.bfloat16)
    hidden = jax.nn.gelu(
        jnp.dot(second, up_weight, preferred_element_type=jnp.float32), approximate=True
    ).astype(jnp.bfloat16)
    final = middle + jnp.dot(hidden, down_weight, preferred_element_type=jnp.float32)
    return final.astype(jnp.bfloat16)


def curve_tables(count_x, count_y):
    square = count_y * count_y
    index = np.arange(square)
    coord_x = np.zeros(square, np.int64)
    coord_y = np.zeros(square, np.int64)
    remain = index.copy()
    level = 1
    while level < count_y:
        bit_x = remain // 2 % 2
        bit_y = np.bitwise_xor(remain, bit_x) % 2
        mirror = (bit_y == 0) & (bit_x == 1)
        moved_x = np.where(mirror, level - 1 - coord_x, coord_x)
        moved_y = np.where(mirror, level - 1 - coord_y, coord_y)
        turned = bit_y == 0
        coord_x = np.where(turned, moved_y, moved_x) + level * bit_x
        coord_y = np.where(turned, moved_x, moved_y) + level * bit_y
        remain = remain // 4
        level = level * 2
    position = np.arange(count_x * count_y)
    along_x = coord_x[position % square] + (position // square) * count_y
    along_y = coord_y[position % square]
    return [int(d) for d in along_x * count_y + along_y]


def conv_kernel(shifted_ref, features_ref, weight_ref, linear_ref, out_ref):
    rows = features_ref.shape[0]
    side = features_ref.shape[1]
    width = features_ref.shape[-1]
    first = pl.program_id(0) * rows
    total = jnp.zeros((rows * side, width), jnp.float32)
    for offset in range(9):
        step_x = offset // 3
        step_y = offset % 3
        window = shifted_ref[pl.ds(first + step_x, rows), pl.ds(step_y, side)].reshape(rows * side, width)
        total += jnp.dot(window, weight_ref[offset], preferred_element_type=jnp.float32)
    linear = jnp.dot(total.astype(jnp.bfloat16), linear_ref[...], preferred_element_type=jnp.float32)
    base = features_ref[...].reshape(rows * side, width).astype(jnp.float32)
    out_ref[...] = (base + layer_norm(linear)).astype(out_ref.dtype)


def encode(padded, features, conv_weight, cpe_linear):
    span_x, span_y, width = features.shape
    shifted = padded
    rows = 8
    return pl.pallas_call(
        conv_kernel,
        grid=(span_x // rows,),
        in_specs=[
            pl.BlockSpec(memory_space=pltpu.VMEM),
            pl.BlockSpec((rows, span_y, width), lambda i: (i, 0, 0)),
            pl.BlockSpec(conv_weight.shape, lambda i: (0, 0, 0)),
            pl.BlockSpec(cpe_linear.shape, lambda i: (0, 0)),
        ],
        out_specs=pl.BlockSpec((rows * span_y, width), lambda i: (i, 0)),
        out_shape=jax.ShapeDtypeStruct((span_x * span_y, width), features.dtype),
    )(shifted, features, conv_weight, cpe_linear)


def shards(
    features,
    occupied,
    voxel_order,
    conv_weight,
    cpe_linear,
    qkv_weight,
    proj_weight,
    up_weight,
    down_weight,
):
    span_x, span_y, width = features.shape
    cells = span_x * span_y
    occ_flat = occupied.reshape(cells)
    mine = jnp.sum(occ_flat, dtype=jnp.int32)
    masked = features * occupied[:, :, None].astype(jnp.bfloat16)
    padded = with_halo(masked, (("gx", 0), ("gy", 1)), 1)
    encoded = encode(padded, features, conv_weight, cpe_linear)
    order = voxel_order[0]
    voxel = jnp.arange(cells, dtype=jnp.int32)
    _, rank_of = lax.sort_key_val(order, voxel)
    key = (1 - occ_flat) * cells + rank_of
    _, listed_voxel = lax.sort_key_val(key, voxel)
    capacity = CAP
    list_index = jnp.arange(LIVE + 2 * capacity, dtype=jnp.int32)
    picked = jnp.where(list_index < mine, listed_voxel[: LIVE + 2 * capacity], -1)
    list_rows, counts = gather_counts(mine, encoded, picked)
    devices = counts.shape[0]
    count_x = lax.axis_size("gx")
    count_y = lax.axis_size("gy")
    here_x = lax.axis_index("gx")
    here_y = lax.axis_index("gy")
    ranks = block_curve(count_x, count_y)
    position = ranks[here_x * count_y + here_y]
    by_position = jnp.zeros((devices,), jnp.int32).at[ranks].set(counts)
    starts = jnp.cumsum(by_position, dtype=jnp.int32) - by_position
    start_here = starts[position]
    excess = start_here - position * LIVE
    beyond = start_here + mine - (position + 1) * LIVE
    slot = jnp.arange(capacity, dtype=jnp.int32)
    empty = jnp.zeros((capacity, width), jnp.bfloat16)
    extended = jnp.concatenate([empty, list_rows], axis=0)
    mine_rows = lax.dynamic_slice_in_dim(extended, capacity - excess, LIVE, 0)
    to_prev = jnp.where((slot < -excess)[:, None], list_rows[:capacity], empty)
    to_next = jnp.where(
        (slot < beyond)[:, None], lax.dynamic_slice_in_dim(list_rows, LIVE - excess, capacity, 0), empty
    )
    device_at = curve_tables(count_x, count_y)
    forward = [(device_at[p], device_at[p + 1]) for p in range(devices - 1)]
    backward = [(target, source) for source, target in forward]
    from_prev = lax.ppermute(to_next, ("gx", "gy"), forward)
    from_next = lax.ppermute(to_prev, ("gx", "gy"), backward)
    from_prev = jnp.where((slot < excess)[:, None], from_prev, empty)
    from_next = jnp.where((slot < -beyond)[:, None], from_next, empty)
    leading = jnp.concatenate(
        [from_prev, jnp.zeros((LIVE - capacity, width), jnp.bfloat16)], axis=0
    )
    trailing = lax.dynamic_slice_in_dim(
        jnp.concatenate([jnp.zeros((LIVE, width), jnp.bfloat16), from_next], axis=0),
        -beyond,
        LIVE,
        0,
    )
    owned = mine_rows + leading + trailing
    return attention_block(owned, qkv_weight, proj_weight, up_weight, down_weight)


def solution(mesh):
    return jax.shard_map(
        shards,
        mesh=mesh,
        in_specs=(
            P("gx", "gy", None),
            P("gx", "gy"),
            P(("gx", "gy"), None),
            P(),
            P(),
            P(),
            P(),
            P(),
            P(),
        ),
        out_specs=P(("gx", "gy"), None),
        check_vma=False,
    )
```

```python
import functools
import math

import jax
import numpy as np
import jax.numpy as jnp
from jax import lax
from jax.experimental import pallas as pl
from jax.experimental.pallas import tpu as pltpu
from jax.sharding import PartitionSpec as P

HEADS = 8
PATCH = 1024
LIVE = 2048
CAP = 256
HD = 32


def with_halo(block, sides, width):
    for axis, dim in sides:
        count = lax.axis_size(axis)
        forward = [(i, i + 1) for i in range(count - 1)]
        backward = [(target, source) for source, target in forward]
        low = lax.ppermute(
            lax.slice_in_dim(block, block.shape[dim] - width, None, axis=dim), axis, forward
        )
        high = lax.ppermute(lax.slice_in_dim(block, 0, width, axis=dim), axis, backward)
        block = jnp.concatenate([low, block, high], axis=dim)
    return block


def passed_along(block, axis, distance):
    devices = range(lax.axis_size(axis))
    route = [(i - distance, i) for i in devices if i - distance in devices]
    return lax.ppermute(block, axis, route)


def hilbert_points(side):
    index = jnp.arange(side * side, dtype=jnp.int32)
    coord_x = jnp.zeros((side * side,), jnp.int32)
    coord_y = jnp.zeros((side * side,), jnp.int32)
    remain = index
    level = 1
    while level < side:
        bit_x = remain // 2 % 2
        bit_y = jnp.bitwise_xor(remain, bit_x) % 2
        mirror = (bit_y == 0) & (bit_x == 1)
        moved_x = jnp.where(mirror, level - 1 - coord_x, coord_x)
        moved_y = jnp.where(mirror, level - 1 - coord_y, coord_y)
        turned = bit_y == 0
        coord_x = jnp.where(turned, moved_y, moved_x) + level * bit_x
        coord_y = jnp.where(turned, moved_x, moved_y) + level * bit_y
        remain = remain // 4
        level = level * 2
    return (coord_x, coord_y)


def block_curve(count_x, count_y):
    total = count_x * count_y
    square = count_y * count_y
    position = jnp.arange(total, dtype=jnp.int32)
    half = position // square
    inner_x, inner_y = hilbert_points(count_y)
    along_x = inner_x[position % square] + half * count_y
    along_y = inner_y[position % square]
    device = along_x * count_y + along_y
    return jnp.zeros((total,), jnp.int32).at[device].set(position)


def layer_norm(values):
    centre = values - jnp.mean(values, axis=-1, keepdims=True)
    spread = jnp.mean(centre * centre, axis=-1, keepdims=True)
    return centre * lax.rsqrt(spread + 1e-05)


def attend_patch(rows, qkv_weight, proj_weight, up_weight, down_weight):
    base = rows.astype(jnp.float32)
    normed = layer_norm(base).astype(jnp.bfloat16)
    projected = jnp.dot(normed, qkv_weight, preferred_element_type=jnp.float32).astype(jnp.bfloat16)
    width = rows.shape[1]
    count = rows.shape[0]
    query = projected[:, :width].reshape(count, HEADS, HD)
    keyset = projected[:, width : 2 * width].reshape(count, HEADS, HD)
    valueset = projected[:, 2 * width :].reshape(count, HEADS, HD)
    scores = jnp.einsum("qhd,khd->hqk", query, keyset, preferred_element_type=jnp.float32) * (
        1.0 / math.sqrt(HD)
    )
    largest = jnp.max(scores, axis=-1, keepdims=True)
    expo = jnp.exp(scores - largest)
    weights = (expo / jnp.sum(expo, axis=-1, keepdims=True)).astype(jnp.bfloat16)
    attended = jnp.einsum(
        "hqk,khd->qhd", weights, valueset, preferred_element_type=jnp.float32
    ).astype(jnp.bfloat16)
    middle = base + jnp.dot(
        attended.reshape(count, width), proj_weight, preferred_element_type=jnp.float32
    )
    second = layer_norm(middle).astype(jnp.bfloat16)
    hidden = jax.nn.gelu(
        jnp.dot(second, up_weight, preferred_element_type=jnp.float32), approximate=True
    ).astype(jnp.bfloat16)
    final = middle + jnp.dot(hidden, down_weight, preferred_element_type=jnp.float32)
    return final.astype(jnp.bfloat16)


def onehot_gather_kernel(index_ref, table_ref, out_ref, acc_ref):
    rows = index_ref.shape[0]
    chunk = 512
    wanted = index_ref[...]
    acc_ref[...] = jnp.zeros_like(acc_ref)
    for part in range(table_ref.shape[0] // chunk):
        ids = lax.broadcasted_iota(jnp.int32, (rows, chunk), 1) + part * chunk
        pick = jnp.where(wanted == ids, 1.0, 0.0).astype(jnp.bfloat16)
        acc_ref[...] += jnp.dot(
            pick, table_ref[pl.ds(part * chunk, chunk), :], preferred_element_type=jnp.float32
        )
    out_ref[...] = acc_ref[...].astype(out_ref.dtype)


def onehot_gather(table, index):
    count = index.shape[0]
    width = table.shape[1]
    tile = 256
    return pl.pallas_call(
        onehot_gather_kernel,
        grid=(count // tile,),
        in_specs=[
            pl.BlockSpec((tile, 1), lambda i: (i, 0)),
            pl.BlockSpec(table.shape, lambda i: (0, 0)),
        ],
        out_specs=pl.BlockSpec((tile, width), lambda i: (i, 0)),
        out_shape=jax.ShapeDtypeStruct((count, width), table.dtype),
        scratch_shapes=[pltpu.VMEM((tile, width), jnp.float32)],
    )(index.reshape(count, 1), table)


MESH = pl.DeviceIdType.MESH


def gather_rows(index_ref, table_ref, out_ref, first, last):
    tile = 256
    chunk = 512

    def one_tile(i, carry):
        rows = pl.ds(pl.multiple_of(i * tile, tile), tile)
        wanted = index_ref[:, rows]
        total = jnp.zeros((tile, out_ref.shape[1]), jnp.float32)
        for part in range(table_ref.shape[0] // chunk):
            ids = lax.broadcasted_iota(jnp.int32, (chunk, tile), 0) + part * chunk
            pick = jnp.where(wanted == ids, 1.0, 0.0).astype(jnp.bfloat16)
            total += lax.dot_general(
                pick,
                table_ref[pl.ds(part * chunk, chunk), :],
                (((0,), (0,)), ((), ())),
                preferred_element_type=jnp.float32,
            )
        out_ref[rows, :] = total.astype(out_ref.dtype)
        return carry

    lax.fori_loop(first, last, one_tile, 0)


def count_gather_kernel(nx, ny, index_ref, table_ref, mine_ref, rows_ref, out_ref, row_buf, grid_buf, send1, recv1, send2, recv2, own_sem):
    me_x = lax.axis_index("gx")
    me_y = lax.axis_index("gy")
    barrier = pltpu.get_barrier_semaphore()
    for k in range(1, ny):
        pl.semaphore_signal(
            barrier, inc=1, device_id=(me_x, lax.rem(me_y + k, ny)), device_id_type=MESH
        )
    for k in range(1, nx):
        pl.semaphore_signal(
            barrier, inc=1, device_id=(lax.rem(me_x + k, nx), me_y), device_id_type=MESH
        )
    pl.semaphore_wait(barrier, nx + ny - 2)

    own = pltpu.make_async_copy(mine_ref, row_buf.at[pl.ds(me_y, 1)], own_sem.at[0])
    own.start()
    for k in range(1, ny):
        pltpu.make_async_remote_copy(
            src_ref=mine_ref,
            dst_ref=row_buf.at[pl.ds(me_y, 1)],
            send_sem=send1.at[k],
            recv_sem=recv1.at[k],
            device_id=(me_x, lax.rem(me_y + k, ny)),
            device_id_type=MESH,
        ).start()
    tiles = rows_ref.shape[0] // 256
    gather_rows(index_ref, table_ref, rows_ref, 0, tiles // 2)
    own.wait()
    for k in range(1, ny):
        sender = lax.rem(me_y - k + ny, ny)
        copy = pltpu.make_async_remote_copy(
            src_ref=mine_ref,
            dst_ref=row_buf.at[pl.ds(sender, 1)],
            send_sem=send1.at[k],
            recv_sem=recv1.at[k],
            device_id=(me_x, sender),
            device_id_type=MESH,
        )
        copy.wait_send()
        copy.wait_recv()

    own = pltpu.make_async_copy(row_buf, grid_buf.at[me_x], own_sem.at[1])
    own.start()
    for k in range(1, nx):
        pltpu.make_async_remote_copy(
            src_ref=row_buf,
            dst_ref=grid_buf.at[me_x],
            send_sem=send2.at[k],
            recv_sem=recv2.at[k],
            device_id=(lax.rem(me_x + k, nx), me_y),
            device_id_type=MESH,
        ).start()
    gather_rows(index_ref, table_ref, rows_ref, tiles // 2, tiles)
    own.wait()
    for k in range(1, nx):
        sender = lax.rem(me_x - k + nx, nx)
        copy = pltpu.make_async_remote_copy(
            src_ref=row_buf,
            dst_ref=grid_buf.at[sender],
            send_sem=send2.at[k],
            recv_sem=recv2.at[k],
            device_id=(sender, me_y),
            device_id_type=MESH,
        )
        copy.wait_send()
        copy.wait_recv()
    out_ref[...] = grid_buf[...]


def gather_counts(mine, table, index):
    nx = lax.axis_size("gx")
    ny = lax.axis_size("gy")
    lanes = 128
    listed, grid = pl.pallas_call(
        functools.partial(count_gather_kernel, nx, ny),
        out_shape=(
            jax.ShapeDtypeStruct((index.shape[0], table.shape[1]), table.dtype),
            jax.ShapeDtypeStruct((nx, ny, lanes), jnp.int32),
        ),
        in_specs=[pl.BlockSpec(memory_space=pltpu.VMEM)] * 3,
        out_specs=(pl.BlockSpec(memory_space=pltpu.VMEM), pl.BlockSpec(memory_space=pltpu.VMEM)),
        scratch_shapes=[
            pltpu.VMEM((ny, lanes), jnp.int32),
            pltpu.VMEM((nx, ny, lanes), jnp.int32),
            pltpu.SemaphoreType.DMA((ny,)),
            pltpu.SemaphoreType.DMA((ny,)),
            pltpu.SemaphoreType.DMA((nx,)),
            pltpu.SemaphoreType.DMA((nx,)),
            pltpu.SemaphoreType.DMA((2,)),
        ],
        compiler_params=pltpu.CompilerParams(collective_id=0, has_side_effects=True),
    )(index.reshape(1, -1), table, jnp.broadcast_to(mine, (1, lanes)))
    return listed, grid[:, :, 0].reshape(nx * ny)


def attention_kernel(q_ref, k_ref, v_ref, base_ref, proj_ref, up_ref, down_ref, out_ref):
    query = q_ref[...]
    keyset = k_ref[...]
    valueset = v_ref[...]
    width = query.shape[1]
    head_of = lax.broadcasted_iota(jnp.int32, (1, width), 1) // HD
    attended = jnp.zeros((query.shape[0], width), jnp.float32)
    for head in range(HEADS):
        mine = head_of == head
        scores = lax.dot_general(
            jnp.where(mine, query, jnp.zeros_like(query)),
            keyset,
            (((1,), (1,)), ((), ())),
            preferred_element_type=jnp.float32,
        ) * (1.0 / math.sqrt(HD))
        largest = jnp.max(scores, axis=-1, keepdims=True)
        expo = jnp.exp(scores - largest)
        scale = 1.0 / jnp.sum(expo, axis=-1, keepdims=True)
        mixed = jnp.dot(expo.astype(jnp.bfloat16), valueset, preferred_element_type=jnp.float32)
        attended = jnp.where(mine, mixed * scale, attended)
    middle = base_ref[...].astype(jnp.float32) + jnp.dot(
        attended.astype(jnp.bfloat16), proj_ref[...], preferred_element_type=jnp.float32
    )
    second = layer_norm(middle).astype(jnp.bfloat16)
    hidden = jax.nn.gelu(
        jnp.dot(second, up_ref[...], preferred_element_type=jnp.float32), approximate=True
    ).astype(jnp.bfloat16)
    final = middle + jnp.dot(hidden, down_ref[...], preferred_element_type=jnp.float32)
    out_ref[...] = final.astype(out_ref.dtype)


def attention_block(rows, qkv_weight, proj_weight, up_weight, down_weight):
    count, width = rows.shape
    base = rows.astype(jnp.float32)
    normed = layer_norm(base).astype(jnp.bfloat16)
    projected = jnp.dot(normed, qkv_weight, preferred_element_type=jnp.float32).astype(jnp.bfloat16)
    tile = 512
    tiles = PATCH // tile
    grid = (count // PATCH, tiles)
    return pl.pallas_call(
        attention_kernel,
        grid=grid,
        in_specs=[
            pl.BlockSpec((tile, width), lambda p, t: (p * tiles + t, 0)),
            pl.BlockSpec((PATCH, width), lambda p, t: (p, 1)),
            pl.BlockSpec((PATCH, width), lambda p, t: (p, 2)),
            pl.BlockSpec((tile, width), lambda p, t: (p * tiles + t, 0)),
            pl.BlockSpec((width, width), lambda p, t: (0, 0)),
            pl.BlockSpec(up_weight.shape, lambda p, t: (0, 0)),
            pl.BlockSpec(down_weight.shape, lambda p, t: (0, 0)),
        ],
        out_specs=pl.BlockSpec((tile, width), lambda p, t: (p * tiles + t, 0)),
        out_shape=jax.ShapeDtypeStruct((count, width), rows.dtype),
    )(projected, projected, projected, rows, proj_weight, up_weight, down_weight)


def feed_forward(middle, up_weight, down_weight):
    second = layer_norm(middle).astype(jnp.bfloat16)
    hidden = jax.nn.gelu(
        jnp.dot(second, up_weight, preferred_element_type=jnp.float32), approximate=True
    ).astype(jnp.bfloat16)
    final = middle + jnp.dot(hidden, down_weight, preferred_element_type=jnp.float32)
    return final.astype(jnp.bfloat16)


def curve_tables(count_x, count_y):
    square = count_y * count_y
    index = np.arange(square)
    coord_x = np.zeros(square, np.int64)
    coord_y = np.zeros(square, np.int64)
    remain = index.copy()
    level = 1
    while level < count_y:
        bit_x = remain // 2 % 2
        bit_y = np.bitwise_xor(remain, bit_x) % 2
        mirror = (bit_y == 0) & (bit_x == 1)
        moved_x = np.where(mirror, level - 1 - coord_x, coord_x)
        moved_y = np.where(mirror, level - 1 - coord_y, coord_y)
        turned = bit_y == 0
        coord_x = np.where(turned, moved_y, moved_x) + level * bit_x
        coord_y = np.where(turned, moved_x, moved_y) + level * bit_y
        remain = remain // 4
        level = level * 2
    position = np.arange(count_x * count_y)
    along_x = coord_x[position % square] + (position // square) * count_y
    along_y = coord_y[position % square]
    return [int(d) for d in along_x * count_y + along_y]


def conv_kernel(shifted_ref, features_ref, weight_ref, linear_ref, out_ref):
    rows = features_ref.shape[0]
    side = features_ref.shape[1]
    width = features_ref.shape[-1]
    first = pl.program_id(0) * rows
    total = jnp.zeros((rows * side, width), jnp.float32)
    for offset in range(9):
        step_x = offset // 3
        step_y = offset % 3
        window = shifted_ref[pl.ds(first + step_x, rows), pl.ds(step_y, side)].reshape(rows * side, width)
        total += jnp.dot(window, weight_ref[offset], preferred_element_type=jnp.float32)
    linear = jnp.dot(total.astype(jnp.bfloat16), linear_ref[...], preferred_element_type=jnp.float32)
    base = features_ref[...].reshape(rows * side, width).astype(jnp.float32)
    out_ref[...] = (base + layer_norm(linear)).astype(out_ref.dtype)


def encode(padded, features, conv_weight, cpe_linear):
    span_x, span_y, width = features.shape
    shifted = padded
    rows = 8
    return pl.pallas_call(
        conv_kernel,
        grid=(span_x // rows,),
        in_specs=[
            pl.BlockSpec(memory_space=pltpu.VMEM),
            pl.BlockSpec((rows, span_y, width), lambda i: (i, 0, 0)),
            pl.BlockSpec(conv_weight.shape, lambda i: (0, 0, 0)),
            pl.BlockSpec(cpe_linear.shape, lambda i: (0, 0)),
        ],
        out_specs=pl.BlockSpec((rows * span_y, width), lambda i: (i, 0)),
        out_shape=jax.ShapeDtypeStruct((span_x * span_y, width), features.dtype),
    )(shifted, features, conv_weight, cpe_linear)


def shards(
    features,
    occupied,
    voxel_order,
    conv_weight,
    cpe_linear,
    qkv_weight,
    proj_weight,
    up_weight,
    down_weight,
):
    span_x, span_y, width = features.shape
    cells = span_x * span_y
    occ_flat = occupied.reshape(cells)
    mine = jnp.sum(occ_flat, dtype=jnp.int32)
    masked = features * occupied[:, :, None].astype(jnp.bfloat16)
    padded = with_halo(masked, (("gx", 0), ("gy", 1)), 1)
    encoded = encode(padded, features, conv_weight, cpe_linear)
    order = voxel_order[0]
    voxel = jnp.arange(cells, dtype=jnp.int32)
    _, rank_of = lax.sort_key_val(order, voxel, is_stable=False)
    key = (1 - occ_flat) * cells + rank_of
    _, listed_voxel = lax.sort_key_val(key, voxel, is_stable=False)
    capacity = CAP
    list_index = jnp.arange(LIVE + 2 * capacity, dtype=jnp.int32)
    picked = jnp.where(list_index < mine, listed_voxel[: LIVE + 2 * capacity], -1)
    list_rows, counts = gather_counts(mine, encoded, picked)
    devices = counts.shape[0]
    count_x = lax.axis_size("gx")
    count_y = lax.axis_size("gy")
    here_x = lax.axis_index("gx")
    here_y = lax.axis_index("gy")
    ranks = block_curve(count_x, count_y)
    position = ranks[here_x * count_y + here_y]
    by_position = jnp.zeros((devices,), jnp.int32).at[ranks].set(counts)
    starts = jnp.cumsum(by_position, dtype=jnp.int32) - by_position
    start_here = starts[position]
    excess = start_here - position * LIVE
    beyond = start_here + mine - (position + 1) * LIVE
    slot = jnp.arange(capacity, dtype=jnp.int32)
    empty = jnp.zeros((capacity, width), jnp.bfloat16)
    extended = jnp.concatenate([empty, list_rows], axis=0)
    mine_rows = lax.dynamic_slice_in_dim(extended, capacity - excess, LIVE, 0)
    to_prev = jnp.where((slot < -excess)[:, None], list_rows[:capacity], empty)
    to_next = jnp.where(
        (slot < beyond)[:, None], lax.dynamic_slice_in_dim(list_rows, LIVE - excess, capacity, 0), empty
    )
    device_at = curve_tables(count_x, count_y)
    forward = [(device_at[p], device_at[p + 1]) for p in range(devices - 1)]
    backward = [(target, source) for source, target in forward]
    from_prev = lax.ppermute(to_next, ("gx", "gy"), forward)
    from_next = lax.ppermute(to_prev, ("gx", "gy"), backward)
    from_prev = jnp.where((slot < excess)[:, None], from_prev, empty)
    from_next = jnp.where((slot < -beyond)[:, None], from_next, empty)
    leading = jnp.concatenate(
        [from_prev, jnp.zeros((LIVE - capacity, width), jnp.bfloat16)], axis=0
    )
    trailing = lax.dynamic_slice_in_dim(
        jnp.concatenate([jnp.zeros((LIVE, width), jnp.bfloat16), from_next], axis=0),
        -beyond,
        LIVE,
        0,
    )
    owned = mine_rows + leading + trailing
    return attention_block(owned, qkv_weight, proj_weight, up_weight, down_weight)


def solution(mesh):
    return jax.shard_map(
        shards,
        mesh=mesh,
        in_specs=(
            P("gx", "gy", None),
            P("gx", "gy"),
            P(("gx", "gy"), None),
            P(),
            P(),
            P(),
            P(),
            P(),
            P(),
        ),
        out_specs=P(("gx", "gy"), None),
        check_vma=False,
    )
```

```python
import functools
import math

import jax
import numpy as np
import jax.numpy as jnp
from jax import lax
from jax.experimental import pallas as pl
from jax.experimental.pallas import tpu as pltpu
from jax.sharding import PartitionSpec as P

HEADS = 8
PATCH = 1024
LIVE = 2048
CAP = 256
HD = 32


def with_halo(block, sides, width):
    for axis, dim in sides:
        count = lax.axis_size(axis)
        forward = [(i, i + 1) for i in range(count - 1)]
        backward = [(target, source) for source, target in forward]
        low = lax.ppermute(
            lax.slice_in_dim(block, block.shape[dim] - width, None, axis=dim), axis, forward
        )
        high = lax.ppermute(lax.slice_in_dim(block, 0, width, axis=dim), axis, backward)
        block = jnp.concatenate([low, block, high], axis=dim)
    return block


def passed_along(block, axis, distance):
    devices = range(lax.axis_size(axis))
    route = [(i - distance, i) for i in devices if i - distance in devices]
    return lax.ppermute(block, axis, route)


def hilbert_points(side):
    index = jnp.arange(side * side, dtype=jnp.int32)
    coord_x = jnp.zeros((side * side,), jnp.int32)
    coord_y = jnp.zeros((side * side,), jnp.int32)
    remain = index
    level = 1
    while level < side:
        bit_x = remain // 2 % 2
        bit_y = jnp.bitwise_xor(remain, bit_x) % 2
        mirror = (bit_y == 0) & (bit_x == 1)
        moved_x = jnp.where(mirror, level - 1 - coord_x, coord_x)
        moved_y = jnp.where(mirror, level - 1 - coord_y, coord_y)
        turned = bit_y == 0
        coord_x = jnp.where(turned, moved_y, moved_x) + level * bit_x
        coord_y = jnp.where(turned, moved_x, moved_y) + level * bit_y
        remain = remain // 4
        level = level * 2
    return (coord_x, coord_y)


def block_curve(count_x, count_y):
    total = count_x * count_y
    square = count_y * count_y
    position = jnp.arange(total, dtype=jnp.int32)
    half = position // square
    inner_x, inner_y = hilbert_points(count_y)
    along_x = inner_x[position % square] + half * count_y
    along_y = inner_y[position % square]
    device = along_x * count_y + along_y
    return jnp.zeros((total,), jnp.int32).at[device].set(position)


def layer_norm(values):
    centre = values - jnp.mean(values, axis=-1, keepdims=True)
    spread = jnp.mean(centre * centre, axis=-1, keepdims=True)
    return centre * lax.rsqrt(spread + 1e-05)


def attend_patch(rows, qkv_weight, proj_weight, up_weight, down_weight):
    base = rows.astype(jnp.float32)
    normed = layer_norm(base).astype(jnp.bfloat16)
    projected = jnp.dot(normed, qkv_weight, preferred_element_type=jnp.float32).astype(jnp.bfloat16)
    width = rows.shape[1]
    count = rows.shape[0]
    query = projected[:, :width].reshape(count, HEADS, HD)
    keyset = projected[:, width : 2 * width].reshape(count, HEADS, HD)
    valueset = projected[:, 2 * width :].reshape(count, HEADS, HD)
    scores = jnp.einsum("qhd,khd->hqk", query, keyset, preferred_element_type=jnp.float32) * (
        1.0 / math.sqrt(HD)
    )
    largest = jnp.max(scores, axis=-1, keepdims=True)
    expo = jnp.exp(scores - largest)
    weights = (expo / jnp.sum(expo, axis=-1, keepdims=True)).astype(jnp.bfloat16)
    attended = jnp.einsum(
        "hqk,khd->qhd", weights, valueset, preferred_element_type=jnp.float32
    ).astype(jnp.bfloat16)
    middle = base + jnp.dot(
        attended.reshape(count, width), proj_weight, preferred_element_type=jnp.float32
    )
    second = layer_norm(middle).astype(jnp.bfloat16)
    hidden = jax.nn.gelu(
        jnp.dot(second, up_weight, preferred_element_type=jnp.float32), approximate=True
    ).astype(jnp.bfloat16)
    final = middle + jnp.dot(hidden, down_weight, preferred_element_type=jnp.float32)
    return final.astype(jnp.bfloat16)


def onehot_gather_kernel(index_ref, table_ref, out_ref, acc_ref):
    rows = index_ref.shape[0]
    chunk = 512
    wanted = index_ref[...]
    acc_ref[...] = jnp.zeros_like(acc_ref)
    for part in range(table_ref.shape[0] // chunk):
        ids = lax.broadcasted_iota(jnp.int32, (rows, chunk), 1) + part * chunk
        pick = jnp.where(wanted == ids, 1.0, 0.0).astype(jnp.bfloat16)
        acc_ref[...] += jnp.dot(
            pick, table_ref[pl.ds(part * chunk, chunk), :], preferred_element_type=jnp.float32
        )
    out_ref[...] = acc_ref[...].astype(out_ref.dtype)


def onehot_gather(table, index):
    count = index.shape[0]
    width = table.shape[1]
    tile = 256
    return pl.pallas_call(
        onehot_gather_kernel,
        grid=(count // tile,),
        in_specs=[
            pl.BlockSpec((tile, 1), lambda i: (i, 0)),
            pl.BlockSpec(table.shape, lambda i: (0, 0)),
        ],
        out_specs=pl.BlockSpec((tile, width), lambda i: (i, 0)),
        out_shape=jax.ShapeDtypeStruct((count, width), table.dtype),
        scratch_shapes=[pltpu.VMEM((tile, width), jnp.float32)],
    )(index.reshape(count, 1), table)


MESH = pl.DeviceIdType.MESH


def gather_rows(index_ref, table_ref, out_ref, first, last):
    tile = 256
    chunk = 512

    def one_tile(i, carry):
        rows = pl.ds(pl.multiple_of(i * tile, tile), tile)
        wanted = index_ref[:, rows]
        total = jnp.zeros((tile, out_ref.shape[1]), jnp.float32)
        for part in range(table_ref.shape[0] // chunk):
            ids = lax.broadcasted_iota(jnp.int32, (chunk, tile), 0) + part * chunk
            pick = jnp.where(wanted == ids, 1.0, 0.0).astype(jnp.bfloat16)
            total += lax.dot_general(
                pick,
                table_ref[pl.ds(part * chunk, chunk), :],
                (((0,), (0,)), ((), ())),
                preferred_element_type=jnp.float32,
            )
        out_ref[rows, :] = total.astype(out_ref.dtype)
        return carry

    lax.fori_loop(first, last, one_tile, 0)


def count_gather_kernel(nx, ny, index_ref, table_ref, mine_ref, rows_ref, out_ref, row_buf, grid_buf, send1, recv1, send2, recv2, own_sem):
    me_x = lax.axis_index("gx")
    me_y = lax.axis_index("gy")
    barrier = pltpu.get_barrier_semaphore()
    for k in range(1, ny):
        pl.semaphore_signal(
            barrier, inc=1, device_id=(me_x, lax.rem(me_y + k, ny)), device_id_type=MESH
        )
    for k in range(1, nx):
        pl.semaphore_signal(
            barrier, inc=1, device_id=(lax.rem(me_x + k, nx), me_y), device_id_type=MESH
        )
    pl.semaphore_wait(barrier, nx + ny - 2)

    own = pltpu.make_async_copy(mine_ref, row_buf.at[pl.ds(me_y, 1)], own_sem.at[0])
    own.start()
    for k in range(1, ny):
        pltpu.make_async_remote_copy(
            src_ref=mine_ref,
            dst_ref=row_buf.at[pl.ds(me_y, 1)],
            send_sem=send1.at[k],
            recv_sem=recv1.at[k],
            device_id=(me_x, lax.rem(me_y + k, ny)),
            device_id_type=MESH,
        ).start()
    tiles = rows_ref.shape[0] // 256
    gather_rows(index_ref, table_ref, rows_ref, 0, tiles // 2)
    own.wait()
    for k in range(1, ny):
        sender = lax.rem(me_y - k + ny, ny)
        copy = pltpu.make_async_remote_copy(
            src_ref=mine_ref,
            dst_ref=row_buf.at[pl.ds(sender, 1)],
            send_sem=send1.at[k],
            recv_sem=recv1.at[k],
            device_id=(me_x, sender),
            device_id_type=MESH,
        )
        copy.wait_send()
        copy.wait_recv()

    own = pltpu.make_async_copy(row_buf, grid_buf.at[me_x], own_sem.at[1])
    own.start()
    for k in range(1, nx):
        pltpu.make_async_remote_copy(
            src_ref=row_buf,
            dst_ref=grid_buf.at[me_x],
            send_sem=send2.at[k],
            recv_sem=recv2.at[k],
            device_id=(lax.rem(me_x + k, nx), me_y),
            device_id_type=MESH,
        ).start()
    gather_rows(index_ref, table_ref, rows_ref, tiles // 2, tiles)
    own.wait()
    for k in range(1, nx):
        sender = lax.rem(me_x - k + nx, nx)
        copy = pltpu.make_async_remote_copy(
            src_ref=row_buf,
            dst_ref=grid_buf.at[sender],
            send_sem=send2.at[k],
            recv_sem=recv2.at[k],
            device_id=(sender, me_y),
            device_id_type=MESH,
        )
        copy.wait_send()
        copy.wait_recv()
    out_ref[...] = grid_buf[...]


def gather_counts(mine, table, index):
    nx = lax.axis_size("gx")
    ny = lax.axis_size("gy")
    lanes = 128
    listed, grid = pl.pallas_call(
        functools.partial(count_gather_kernel, nx, ny),
        out_shape=(
            jax.ShapeDtypeStruct((index.shape[0], table.shape[1]), table.dtype),
            jax.ShapeDtypeStruct((nx, ny, lanes), jnp.int32),
        ),
        in_specs=[pl.BlockSpec(memory_space=pltpu.VMEM)] * 3,
        out_specs=(pl.BlockSpec(memory_space=pltpu.VMEM), pl.BlockSpec(memory_space=pltpu.VMEM)),
        scratch_shapes=[
            pltpu.VMEM((ny, lanes), jnp.int32),
            pltpu.VMEM((nx, ny, lanes), jnp.int32),
            pltpu.SemaphoreType.DMA((ny,)),
            pltpu.SemaphoreType.DMA((ny,)),
            pltpu.SemaphoreType.DMA((nx,)),
            pltpu.SemaphoreType.DMA((nx,)),
            pltpu.SemaphoreType.DMA((2,)),
        ],
        compiler_params=pltpu.CompilerParams(collective_id=0, has_side_effects=True),
    )(index.reshape(1, -1), table, jnp.broadcast_to(mine, (1, lanes)))
    return listed, grid[:, :, 0].reshape(nx * ny)


def attention_kernel(q_ref, k_ref, v_ref, base_ref, proj_ref, up_ref, down_ref, out_ref):
    query = q_ref[...]
    keyset = k_ref[...]
    valueset = v_ref[...]
    width = query.shape[1]
    head_of = lax.broadcasted_iota(jnp.int32, (1, width), 1) // HD
    attended = jnp.zeros((query.shape[0], width), jnp.float32)
    for head in range(HEADS):
        mine = head_of == head
        scores = lax.dot_general(
            jnp.where(mine, query, jnp.zeros_like(query)),
            keyset,
            (((1,), (1,)), ((), ())),
            preferred_element_type=jnp.float32,
        ) * (1.0 / math.sqrt(HD))
        largest = jnp.max(scores, axis=-1, keepdims=True)
        expo = jnp.exp(scores - largest)
        scale = 1.0 / jnp.sum(expo, axis=-1, keepdims=True)
        mixed = jnp.dot(expo.astype(jnp.bfloat16), valueset, preferred_element_type=jnp.float32)
        attended = jnp.where(mine, mixed * scale, attended)
    middle = base_ref[...].astype(jnp.float32) + jnp.dot(
        attended.astype(jnp.bfloat16), proj_ref[...], preferred_element_type=jnp.float32
    )
    second = layer_norm(middle).astype(jnp.bfloat16)
    hidden = jax.nn.gelu(
        jnp.dot(second, up_ref[...], preferred_element_type=jnp.float32), approximate=True
    ).astype(jnp.bfloat16)
    final = middle + jnp.dot(hidden, down_ref[...], preferred_element_type=jnp.float32)
    out_ref[...] = final.astype(out_ref.dtype)


def attention_block(rows, qkv_weight, proj_weight, up_weight, down_weight):
    count, width = rows.shape
    base = rows.astype(jnp.float32)
    normed = layer_norm(base).astype(jnp.bfloat16)
    projected = jnp.dot(normed, qkv_weight, preferred_element_type=jnp.float32).astype(jnp.bfloat16)
    tile = 512
    tiles = PATCH // tile
    grid = (count // PATCH, tiles)
    return pl.pallas_call(
        attention_kernel,
        grid=grid,
        in_specs=[
            pl.BlockSpec((tile, width), lambda p, t: (p * tiles + t, 0)),
            pl.BlockSpec((PATCH, width), lambda p, t: (p, 1)),
            pl.BlockSpec((PATCH, width), lambda p, t: (p, 2)),
            pl.BlockSpec((tile, width), lambda p, t: (p * tiles + t, 0)),
            pl.BlockSpec((width, width), lambda p, t: (0, 0)),
            pl.BlockSpec(up_weight.shape, lambda p, t: (0, 0)),
            pl.BlockSpec(down_weight.shape, lambda p, t: (0, 0)),
        ],
        out_specs=pl.BlockSpec((tile, width), lambda p, t: (p * tiles + t, 0)),
        out_shape=jax.ShapeDtypeStruct((count, width), rows.dtype),
    )(projected, projected, projected, rows, proj_weight, up_weight, down_weight)


def feed_forward(middle, up_weight, down_weight):
    second = layer_norm(middle).astype(jnp.bfloat16)
    hidden = jax.nn.gelu(
        jnp.dot(second, up_weight, preferred_element_type=jnp.float32), approximate=True
    ).astype(jnp.bfloat16)
    final = middle + jnp.dot(hidden, down_weight, preferred_element_type=jnp.float32)
    return final.astype(jnp.bfloat16)


def curve_tables(count_x, count_y):
    square = count_y * count_y
    index = np.arange(square)
    coord_x = np.zeros(square, np.int64)
    coord_y = np.zeros(square, np.int64)
    remain = index.copy()
    level = 1
    while level < count_y:
        bit_x = remain // 2 % 2
        bit_y = np.bitwise_xor(remain, bit_x) % 2
        mirror = (bit_y == 0) & (bit_x == 1)
        moved_x = np.where(mirror, level - 1 - coord_x, coord_x)
        moved_y = np.where(mirror, level - 1 - coord_y, coord_y)
        turned = bit_y == 0
        coord_x = np.where(turned, moved_y, moved_x) + level * bit_x
        coord_y = np.where(turned, moved_x, moved_y) + level * bit_y
        remain = remain // 4
        level = level * 2
    position = np.arange(count_x * count_y)
    along_x = coord_x[position % square] + (position // square) * count_y
    along_y = coord_y[position % square]
    return [int(d) for d in along_x * count_y + along_y]


def conv_kernel(shifted_ref, features_ref, weight_ref, linear_ref, out_ref):
    rows = features_ref.shape[0]
    side = features_ref.shape[1]
    width = features_ref.shape[-1]
    first = pl.program_id(0) * rows
    total = jnp.zeros((rows * side, width), jnp.float32)
    for offset in range(9):
        step_x = offset // 3
        step_y = offset % 3
        window = shifted_ref[pl.ds(first + step_x, rows), pl.ds(step_y, side)].reshape(rows * side, width)
        total += jnp.dot(window, weight_ref[offset], preferred_element_type=jnp.float32)
    linear = jnp.dot(total.astype(jnp.bfloat16), linear_ref[...], preferred_element_type=jnp.float32)
    base = features_ref[...].reshape(rows * side, width).astype(jnp.float32)
    out_ref[...] = (base + layer_norm(linear)).astype(out_ref.dtype)


def encode(padded, features, conv_weight, cpe_linear):
    span_x, span_y, width = features.shape
    shifted = padded
    rows = 16
    return pl.pallas_call(
        conv_kernel,
        grid=(span_x // rows,),
        in_specs=[
            pl.BlockSpec(memory_space=pltpu.VMEM),
            pl.BlockSpec((rows, span_y, width), lambda i: (i, 0, 0)),
            pl.BlockSpec(conv_weight.shape, lambda i: (0, 0, 0)),
            pl.BlockSpec(cpe_linear.shape, lambda i: (0, 0)),
        ],
        out_specs=pl.BlockSpec((rows * span_y, width), lambda i: (i, 0)),
        out_shape=jax.ShapeDtypeStruct((span_x * span_y, width), features.dtype),
    )(shifted, features, conv_weight, cpe_linear)


def shards(
    features,
    occupied,
    voxel_order,
    conv_weight,
    cpe_linear,
    qkv_weight,
    proj_weight,
    up_weight,
    down_weight,
):
    span_x, span_y, width = features.shape
    cells = span_x * span_y
    occ_flat = occupied.reshape(cells)
    mine = jnp.sum(occ_flat, dtype=jnp.int32)
    masked = features * occupied[:, :, None].astype(jnp.bfloat16)
    padded = with_halo(masked, (("gx", 0), ("gy", 1)), 1)
    encoded = encode(padded, features, conv_weight, cpe_linear)
    order = voxel_order[0]
    voxel = jnp.arange(cells, dtype=jnp.int32)
    _, rank_of = lax.sort_key_val(order, voxel, is_stable=False)
    key = (1 - occ_flat) * cells + rank_of
    _, listed_voxel = lax.sort_key_val(key, voxel, is_stable=False)
    capacity = CAP
    list_index = jnp.arange(LIVE + 2 * capacity, dtype=jnp.int32)
    picked = jnp.where(list_index < mine, listed_voxel[: LIVE + 2 * capacity], -1)
    list_rows, counts = gather_counts(mine, encoded, picked)
    devices = counts.shape[0]
    count_x = lax.axis_size("gx")
    count_y = lax.axis_size("gy")
    here_x = lax.axis_index("gx")
    here_y = lax.axis_index("gy")
    ranks = block_curve(count_x, count_y)
    position = ranks[here_x * count_y + here_y]
    by_position = jnp.zeros((devices,), jnp.int32).at[ranks].set(counts)
    starts = jnp.cumsum(by_position, dtype=jnp.int32) - by_position
    start_here = starts[position]
    excess = start_here - position * LIVE
    beyond = start_here + mine - (position + 1) * LIVE
    slot = jnp.arange(capacity, dtype=jnp.int32)
    empty = jnp.zeros((capacity, width), jnp.bfloat16)
    extended = jnp.concatenate([empty, list_rows], axis=0)
    mine_rows = lax.dynamic_slice_in_dim(extended, capacity - excess, LIVE, 0)
    to_prev = jnp.where((slot < -excess)[:, None], list_rows[:capacity], empty)
    to_next = jnp.where(
        (slot < beyond)[:, None], lax.dynamic_slice_in_dim(list_rows, LIVE - excess, capacity, 0), empty
    )
    device_at = curve_tables(count_x, count_y)
    forward = [(device_at[p], device_at[p + 1]) for p in range(devices - 1)]
    backward = [(target, source) for source, target in forward]
    from_prev = lax.ppermute(to_next, ("gx", "gy"), forward)
    from_next = lax.ppermute(to_prev, ("gx", "gy"), backward)
    from_prev = jnp.where((slot < excess)[:, None], from_prev, empty)
    from_next = jnp.where((slot < -beyond)[:, None], from_next, empty)
    leading = jnp.concatenate(
        [from_prev, jnp.zeros((LIVE - capacity, width), jnp.bfloat16)], axis=0
    )
    trailing = lax.dynamic_slice_in_dim(
        jnp.concatenate([jnp.zeros((LIVE, width), jnp.bfloat16), from_next], axis=0),
        -beyond,
        LIVE,
        0,
    )
    owned = mine_rows + leading + trailing
    return attention_block(owned, qkv_weight, proj_weight, up_weight, down_weight)


def solution(mesh):
    return jax.shard_map(
        shards,
        mesh=mesh,
        in_specs=(
            P("gx", "gy", None),
            P("gx", "gy"),
            P(("gx", "gy"), None),
            P(),
            P(),
            P(),
            P(),
            P(),
            P(),
        ),
        out_specs=P(("gx", "gy"), None),
        check_vma=False,
    )
```

```python
import functools
import math

import jax
import numpy as np
import jax.numpy as jnp
from jax import lax
from jax.experimental import pallas as pl
from jax.experimental.pallas import tpu as pltpu
from jax.sharding import PartitionSpec as P

HEADS = 8
PATCH = 1024
LIVE = 2048
CAP = 256
HD = 32


def with_halo(block, sides, width):
    for axis, dim in sides:
        count = lax.axis_size(axis)
        forward = [(i, i + 1) for i in range(count - 1)]
        backward = [(target, source) for source, target in forward]
        low = lax.ppermute(
            lax.slice_in_dim(block, block.shape[dim] - width, None, axis=dim), axis, forward
        )
        high = lax.ppermute(lax.slice_in_dim(block, 0, width, axis=dim), axis, backward)
        block = jnp.concatenate([low, block, high], axis=dim)
    return block


def passed_along(block, axis, distance):
    devices = range(lax.axis_size(axis))
    route = [(i - distance, i) for i in devices if i - distance in devices]
    return lax.ppermute(block, axis, route)


def hilbert_points(side):
    index = jnp.arange(side * side, dtype=jnp.int32)
    coord_x = jnp.zeros((side * side,), jnp.int32)
    coord_y = jnp.zeros((side * side,), jnp.int32)
    remain = index
    level = 1
    while level < side:
        bit_x = remain // 2 % 2
        bit_y = jnp.bitwise_xor(remain, bit_x) % 2
        mirror = (bit_y == 0) & (bit_x == 1)
        moved_x = jnp.where(mirror, level - 1 - coord_x, coord_x)
        moved_y = jnp.where(mirror, level - 1 - coord_y, coord_y)
        turned = bit_y == 0
        coord_x = jnp.where(turned, moved_y, moved_x) + level * bit_x
        coord_y = jnp.where(turned, moved_x, moved_y) + level * bit_y
        remain = remain // 4
        level = level * 2
    return (coord_x, coord_y)


def block_curve(count_x, count_y):
    total = count_x * count_y
    square = count_y * count_y
    position = jnp.arange(total, dtype=jnp.int32)
    half = position // square
    inner_x, inner_y = hilbert_points(count_y)
    along_x = inner_x[position % square] + half * count_y
    along_y = inner_y[position % square]
    device = along_x * count_y + along_y
    return jnp.zeros((total,), jnp.int32).at[device].set(position)


def layer_norm(values):
    centre = values - jnp.mean(values, axis=-1, keepdims=True)
    spread = jnp.mean(centre * centre, axis=-1, keepdims=True)
    return centre * lax.rsqrt(spread + 1e-05)


def attend_patch(rows, qkv_weight, proj_weight, up_weight, down_weight):
    base = rows.astype(jnp.float32)
    normed = layer_norm(base).astype(jnp.bfloat16)
    projected = jnp.dot(normed, qkv_weight, preferred_element_type=jnp.float32).astype(jnp.bfloat16)
    width = rows.shape[1]
    count = rows.shape[0]
    query = projected[:, :width].reshape(count, HEADS, HD)
    keyset = projected[:, width : 2 * width].reshape(count, HEADS, HD)
    valueset = projected[:, 2 * width :].reshape(count, HEADS, HD)
    scores = jnp.einsum("qhd,khd->hqk", query, keyset, preferred_element_type=jnp.float32) * (
        1.0 / math.sqrt(HD)
    )
    largest = jnp.max(scores, axis=-1, keepdims=True)
    expo = jnp.exp(scores - largest)
    weights = (expo / jnp.sum(expo, axis=-1, keepdims=True)).astype(jnp.bfloat16)
    attended = jnp.einsum(
        "hqk,khd->qhd", weights, valueset, preferred_element_type=jnp.float32
    ).astype(jnp.bfloat16)
    middle = base + jnp.dot(
        attended.reshape(count, width), proj_weight, preferred_element_type=jnp.float32
    )
    second = layer_norm(middle).astype(jnp.bfloat16)
    hidden = jax.nn.gelu(
        jnp.dot(second, up_weight, preferred_element_type=jnp.float32), approximate=True
    ).astype(jnp.bfloat16)
    final = middle + jnp.dot(hidden, down_weight, preferred_element_type=jnp.float32)
    return final.astype(jnp.bfloat16)


def onehot_gather_kernel(index_ref, table_ref, out_ref, acc_ref):
    rows = index_ref.shape[0]
    chunk = 512
    wanted = index_ref[...]
    acc_ref[...] = jnp.zeros_like(acc_ref)
    for part in range(table_ref.shape[0] // chunk):
        ids = lax.broadcasted_iota(jnp.int32, (rows, chunk), 1) + part * chunk
        pick = jnp.where(wanted == ids, 1.0, 0.0).astype(jnp.bfloat16)
        acc_ref[...] += jnp.dot(
            pick, table_ref[pl.ds(part * chunk, chunk), :], preferred_element_type=jnp.float32
        )
    out_ref[...] = acc_ref[...].astype(out_ref.dtype)


def onehot_gather(table, index):
    count = index.shape[0]
    width = table.shape[1]
    tile = 256
    return pl.pallas_call(
        onehot_gather_kernel,
        grid=(count // tile,),
        in_specs=[
            pl.BlockSpec((tile, 1), lambda i: (i, 0)),
            pl.BlockSpec(table.shape, lambda i: (0, 0)),
        ],
        out_specs=pl.BlockSpec((tile, width), lambda i: (i, 0)),
        out_shape=jax.ShapeDtypeStruct((count, width), table.dtype),
        scratch_shapes=[pltpu.VMEM((tile, width), jnp.float32)],
    )(index.reshape(count, 1), table)


MESH = pl.DeviceIdType.MESH


def gather_rows(index_ref, table_ref, out_ref, first, last):
    tile = 256
    chunk = 512

    def one_tile(i, carry):
        rows = pl.ds(pl.multiple_of(i * tile, tile), tile)
        wanted = index_ref[:, rows]
        total = jnp.zeros((tile, out_ref.shape[1]), jnp.float32)
        for part in range(table_ref.shape[0] // chunk):
            ids = lax.broadcasted_iota(jnp.int32, (chunk, tile), 0) + part * chunk
            pick = jnp.where(wanted == ids, 1.0, 0.0).astype(jnp.bfloat16)
            total += lax.dot_general(
                pick,
                table_ref[pl.ds(part * chunk, chunk), :],
                (((0,), (0,)), ((), ())),
                preferred_element_type=jnp.float32,
            )
        out_ref[rows, :] = total.astype(out_ref.dtype)
        return carry

    lax.fori_loop(first, last, one_tile, 0)


def count_gather_kernel(nx, ny, index_ref, table_ref, mine_ref, rows_ref, out_ref, row_buf, grid_buf, send1, recv1, send2, recv2, own_sem):
    me_x = lax.axis_index("gx")
    me_y = lax.axis_index("gy")
    barrier = pltpu.get_barrier_semaphore()
    for k in range(1, ny):
        pl.semaphore_signal(
            barrier, inc=1, device_id=(me_x, lax.rem(me_y + k, ny)), device_id_type=MESH
        )
    for k in range(1, nx):
        pl.semaphore_signal(
            barrier, inc=1, device_id=(lax.rem(me_x + k, nx), me_y), device_id_type=MESH
        )
    pl.semaphore_wait(barrier, nx + ny - 2)

    own = pltpu.make_async_copy(mine_ref, row_buf.at[pl.ds(me_y, 1)], own_sem.at[0])
    own.start()
    for k in range(1, ny):
        pltpu.make_async_remote_copy(
            src_ref=mine_ref,
            dst_ref=row_buf.at[pl.ds(me_y, 1)],
            send_sem=send1.at[k],
            recv_sem=recv1.at[k],
            device_id=(me_x, lax.rem(me_y + k, ny)),
            device_id_type=MESH,
        ).start()
    tiles = rows_ref.shape[0] // 256
    gather_rows(index_ref, table_ref, rows_ref, 0, tiles // 2)
    own.wait()
    for k in range(1, ny):
        sender = lax.rem(me_y - k + ny, ny)
        copy = pltpu.make_async_remote_copy(
            src_ref=mine_ref,
            dst_ref=row_buf.at[pl.ds(sender, 1)],
            send_sem=send1.at[k],
            recv_sem=recv1.at[k],
            device_id=(me_x, sender),
            device_id_type=MESH,
        )
        copy.wait_send()
        copy.wait_recv()

    own = pltpu.make_async_copy(row_buf, grid_buf.at[me_x], own_sem.at[1])
    own.start()
    for k in range(1, nx):
        pltpu.make_async_remote_copy(
            src_ref=row_buf,
            dst_ref=grid_buf.at[me_x],
            send_sem=send2.at[k],
            recv_sem=recv2.at[k],
            device_id=(lax.rem(me_x + k, nx), me_y),
            device_id_type=MESH,
        ).start()
    gather_rows(index_ref, table_ref, rows_ref, tiles // 2, tiles)
    own.wait()
    for k in range(1, nx):
        sender = lax.rem(me_x - k + nx, nx)
        copy = pltpu.make_async_remote_copy(
            src_ref=row_buf,
            dst_ref=grid_buf.at[sender],
            send_sem=send2.at[k],
            recv_sem=recv2.at[k],
            device_id=(sender, me_y),
            device_id_type=MESH,
        )
        copy.wait_send()
        copy.wait_recv()
    out_ref[...] = grid_buf[...]


def gather_counts(mine, table, index):
    nx = lax.axis_size("gx")
    ny = lax.axis_size("gy")
    lanes = 128
    listed, grid = pl.pallas_call(
        functools.partial(count_gather_kernel, nx, ny),
        out_shape=(
            jax.ShapeDtypeStruct((index.shape[0], table.shape[1]), table.dtype),
            jax.ShapeDtypeStruct((nx, ny, lanes), jnp.int32),
        ),
        in_specs=[pl.BlockSpec(memory_space=pltpu.VMEM)] * 3,
        out_specs=(pl.BlockSpec(memory_space=pltpu.VMEM), pl.BlockSpec(memory_space=pltpu.VMEM)),
        scratch_shapes=[
            pltpu.VMEM((ny, lanes), jnp.int32),
            pltpu.VMEM((nx, ny, lanes), jnp.int32),
            pltpu.SemaphoreType.DMA((ny,)),
            pltpu.SemaphoreType.DMA((ny,)),
            pltpu.SemaphoreType.DMA((nx,)),
            pltpu.SemaphoreType.DMA((nx,)),
            pltpu.SemaphoreType.DMA((2,)),
        ],
        compiler_params=pltpu.CompilerParams(collective_id=0, has_side_effects=True),
    )(index.reshape(1, -1), table, jnp.broadcast_to(mine, (1, lanes)))
    return listed, grid[:, :, 0].reshape(nx * ny)


def attention_kernel(q_ref, k_ref, v_ref, base_ref, proj_ref, up_ref, down_ref, out_ref):
    query = q_ref[...]
    keyset = k_ref[...]
    valueset = v_ref[...]
    width = query.shape[1]
    head_of = lax.broadcasted_iota(jnp.int32, (1, width), 1) // HD
    attended = jnp.zeros((query.shape[0], width), jnp.float32)
    for head in range(HEADS):
        mine = head_of == head
        scores = lax.dot_general(
            jnp.where(mine, query, jnp.zeros_like(query)),
            keyset,
            (((1,), (1,)), ((), ())),
            preferred_element_type=jnp.float32,
        ) * (1.0 / math.sqrt(HD))
        largest = jnp.max(scores, axis=-1, keepdims=True)
        expo = jnp.exp(scores - largest)
        scale = 1.0 / jnp.sum(expo, axis=-1, keepdims=True)
        mixed = jnp.dot(expo.astype(jnp.bfloat16), valueset, preferred_element_type=jnp.float32)
        attended = jnp.where(mine, mixed * scale, attended)
    middle = base_ref[...].astype(jnp.float32) + jnp.dot(
        attended.astype(jnp.bfloat16), proj_ref[...], preferred_element_type=jnp.float32
    )
    second = layer_norm(middle).astype(jnp.bfloat16)
    hidden = jax.nn.gelu(
        jnp.dot(second, up_ref[...], preferred_element_type=jnp.float32), approximate=True
    ).astype(jnp.bfloat16)
    final = middle + jnp.dot(hidden, down_ref[...], preferred_element_type=jnp.float32)
    out_ref[...] = final.astype(out_ref.dtype)


def attention_block(rows, qkv_weight, proj_weight, up_weight, down_weight):
    count, width = rows.shape
    base = rows.astype(jnp.float32)
    normed = layer_norm(base).astype(jnp.bfloat16)
    projected = jnp.dot(normed, qkv_weight, preferred_element_type=jnp.float32).astype(jnp.bfloat16)
    tile = 512
    tiles = PATCH // tile
    grid = (count // PATCH, tiles)
    return pl.pallas_call(
        attention_kernel,
        grid=grid,
        in_specs=[
            pl.BlockSpec((tile, width), lambda p, t: (p * tiles + t, 0)),
            pl.BlockSpec((PATCH, width), lambda p, t: (p, 1)),
            pl.BlockSpec((PATCH, width), lambda p, t: (p, 2)),
            pl.BlockSpec((tile, width), lambda p, t: (p * tiles + t, 0)),
            pl.BlockSpec((width, width), lambda p, t: (0, 0)),
            pl.BlockSpec(up_weight.shape, lambda p, t: (0, 0)),
            pl.BlockSpec(down_weight.shape, lambda p, t: (0, 0)),
        ],
        out_specs=pl.BlockSpec((tile, width), lambda p, t: (p * tiles + t, 0)),
        out_shape=jax.ShapeDtypeStruct((count, width), rows.dtype),
    )(projected, projected, projected, rows, proj_weight, up_weight, down_weight)


def feed_forward(middle, up_weight, down_weight):
    second = layer_norm(middle).astype(jnp.bfloat16)
    hidden = jax.nn.gelu(
        jnp.dot(second, up_weight, preferred_element_type=jnp.float32), approximate=True
    ).astype(jnp.bfloat16)
    final = middle + jnp.dot(hidden, down_weight, preferred_element_type=jnp.float32)
    return final.astype(jnp.bfloat16)


def curve_tables(count_x, count_y):
    square = count_y * count_y
    index = np.arange(square)
    coord_x = np.zeros(square, np.int64)
    coord_y = np.zeros(square, np.int64)
    remain = index.copy()
    level = 1
    while level < count_y:
        bit_x = remain // 2 % 2
        bit_y = np.bitwise_xor(remain, bit_x) % 2
        mirror = (bit_y == 0) & (bit_x == 1)
        moved_x = np.where(mirror, level - 1 - coord_x, coord_x)
        moved_y = np.where(mirror, level - 1 - coord_y, coord_y)
        turned = bit_y == 0
        coord_x = np.where(turned, moved_y, moved_x) + level * bit_x
        coord_y = np.where(turned, moved_x, moved_y) + level * bit_y
        remain = remain // 4
        level = level * 2
    position = np.arange(count_x * count_y)
    along_x = coord_x[position % square] + (position // square) * count_y
    along_y = coord_y[position % square]
    return [int(d) for d in along_x * count_y + along_y]


def conv_kernel(shifted_ref, features_ref, weight_ref, linear_ref, out_ref):
    rows = features_ref.shape[0]
    side = features_ref.shape[1]
    width = features_ref.shape[-1]
    first = pl.program_id(0) * rows
    total = jnp.zeros((rows * side, width), jnp.float32)
    for offset in range(9):
        step_x = offset // 3
        step_y = offset % 3
        window = shifted_ref[pl.ds(first + step_x, rows), pl.ds(step_y, side)].reshape(rows * side, width)
        total += jnp.dot(window, weight_ref[offset], preferred_element_type=jnp.float32)
    linear = jnp.dot(total.astype(jnp.bfloat16), linear_ref[...], preferred_element_type=jnp.float32)
    base = features_ref[...].reshape(rows * side, width).astype(jnp.float32)
    out_ref[...] = (base + layer_norm(linear)).astype(out_ref.dtype)


def encode(padded, features, conv_weight, cpe_linear):
    span_x, span_y, width = features.shape
    shifted = padded
    rows = 32
    return pl.pallas_call(
        conv_kernel,
        grid=(span_x // rows,),
        in_specs=[
            pl.BlockSpec(memory_space=pltpu.VMEM),
            pl.BlockSpec((rows, span_y, width), lambda i: (i, 0, 0)),
            pl.BlockSpec(conv_weight.shape, lambda i: (0, 0, 0)),
            pl.BlockSpec(cpe_linear.shape, lambda i: (0, 0)),
        ],
        out_specs=pl.BlockSpec((rows * span_y, width), lambda i: (i, 0)),
        out_shape=jax.ShapeDtypeStruct((span_x * span_y, width), features.dtype),
    )(shifted, features, conv_weight, cpe_linear)


def shards(
    features,
    occupied,
    voxel_order,
    conv_weight,
    cpe_linear,
    qkv_weight,
    proj_weight,
    up_weight,
    down_weight,
):
    span_x, span_y, width = features.shape
    cells = span_x * span_y
    occ_flat = occupied.reshape(cells)
    mine = jnp.sum(occ_flat, dtype=jnp.int32)
    masked = features * occupied[:, :, None].astype(jnp.bfloat16)
    padded = with_halo(masked, (("gx", 0), ("gy", 1)), 1)
    encoded = encode(padded, features, conv_weight, cpe_linear)
    order = voxel_order[0]
    voxel = jnp.arange(cells, dtype=jnp.int32)
    _, rank_of = lax.sort_key_val(order, voxel, is_stable=False)
    key = (1 - occ_flat) * cells + rank_of
    _, listed_voxel = lax.sort_key_val(key, voxel, is_stable=False)
    capacity = CAP
    list_index = jnp.arange(LIVE + 2 * capacity, dtype=jnp.int32)
    picked = jnp.where(list_index < mine, listed_voxel[: LIVE + 2 * capacity], -1)
    list_rows, counts = gather_counts(mine, encoded, picked)
    devices = counts.shape[0]
    count_x = lax.axis_size("gx")
    count_y = lax.axis_size("gy")
    here_x = lax.axis_index("gx")
    here_y = lax.axis_index("gy")
    ranks = block_curve(count_x, count_y)
    position = ranks[here_x * count_y + here_y]
    by_position = jnp.zeros((devices,), jnp.int32).at[ranks].set(counts)
    starts = jnp.cumsum(by_position, dtype=jnp.int32) - by_position
    start_here = starts[position]
    excess = start_here - position * LIVE
    beyond = start_here + mine - (position + 1) * LIVE
    slot = jnp.arange(capacity, dtype=jnp.int32)
    empty = jnp.zeros((capacity, width), jnp.bfloat16)
    extended = jnp.concatenate([empty, list_rows], axis=0)
    mine_rows = lax.dynamic_slice_in_dim(extended, capacity - excess, LIVE, 0)
    to_prev = jnp.where((slot < -excess)[:, None], list_rows[:capacity], empty)
    to_next = jnp.where(
        (slot < beyond)[:, None], lax.dynamic_slice_in_dim(list_rows, LIVE - excess, capacity, 0), empty
    )
    device_at = curve_tables(count_x, count_y)
    forward = [(device_at[p], device_at[p + 1]) for p in range(devices - 1)]
    backward = [(target, source) for source, target in forward]
    from_prev = lax.ppermute(to_next, ("gx", "gy"), forward)
    from_next = lax.ppermute(to_prev, ("gx", "gy"), backward)
    from_prev = jnp.where((slot < excess)[:, None], from_prev, empty)
    from_next = jnp.where((slot < -beyond)[:, None], from_next, empty)
    leading = jnp.concatenate(
        [from_prev, jnp.zeros((LIVE - capacity, width), jnp.bfloat16)], axis=0
    )
    trailing = lax.dynamic_slice_in_dim(
        jnp.concatenate([jnp.zeros((LIVE, width), jnp.bfloat16), from_next], axis=0),
        -beyond,
        LIVE,
        0,
    )
    owned = mine_rows + leading + trailing
    return attention_block(owned, qkv_weight, proj_weight, up_weight, down_weight)


def solution(mesh):
    return jax.shard_map(
        shards,
        mesh=mesh,
        in_specs=(
            P("gx", "gy", None),
            P("gx", "gy"),
            P(("gx", "gy"), None),
            P(),
            P(),
            P(),
            P(),
            P(),
            P(),
        ),
        out_specs=P(("gx", "gy"), None),
        check_vma=False,
    )
```

```python
import functools
import math

import jax
import numpy as np
import jax.numpy as jnp
from jax import lax
from jax.experimental import pallas as pl
from jax.experimental.pallas import tpu as pltpu
from jax.sharding import PartitionSpec as P

HEADS = 8
PATCH = 1024
LIVE = 2048
CAP = 256
HD = 32


def with_halo(block, sides, width):
    for axis, dim in sides:
        count = lax.axis_size(axis)
        forward = [(i, i + 1) for i in range(count - 1)]
        backward = [(target, source) for source, target in forward]
        low = lax.ppermute(
            lax.slice_in_dim(block, block.shape[dim] - width, None, axis=dim), axis, forward
        )
        high = lax.ppermute(lax.slice_in_dim(block, 0, width, axis=dim), axis, backward)
        block = jnp.concatenate([low, block, high], axis=dim)
    return block


def passed_along(block, axis, distance):
    devices = range(lax.axis_size(axis))
    route = [(i - distance, i) for i in devices if i - distance in devices]
    return lax.ppermute(block, axis, route)


def hilbert_points(side):
    index = jnp.arange(side * side, dtype=jnp.int32)
    coord_x = jnp.zeros((side * side,), jnp.int32)
    coord_y = jnp.zeros((side * side,), jnp.int32)
    remain = index
    level = 1
    while level < side:
        bit_x = remain // 2 % 2
        bit_y = jnp.bitwise_xor(remain, bit_x) % 2
        mirror = (bit_y == 0) & (bit_x == 1)
        moved_x = jnp.where(mirror, level - 1 - coord_x, coord_x)
        moved_y = jnp.where(mirror, level - 1 - coord_y, coord_y)
        turned = bit_y == 0
        coord_x = jnp.where(turned, moved_y, moved_x) + level * bit_x
        coord_y = jnp.where(turned, moved_x, moved_y) + level * bit_y
        remain = remain // 4
        level = level * 2
    return (coord_x, coord_y)


def block_curve(count_x, count_y):
    total = count_x * count_y
    square = count_y * count_y
    position = jnp.arange(total, dtype=jnp.int32)
    half = position // square
    inner_x, inner_y = hilbert_points(count_y)
    along_x = inner_x[position % square] + half * count_y
    along_y = inner_y[position % square]
    device = along_x * count_y + along_y
    return jnp.zeros((total,), jnp.int32).at[device].set(position)


def layer_norm(values):
    centre = values - jnp.mean(values, axis=-1, keepdims=True)
    spread = jnp.mean(centre * centre, axis=-1, keepdims=True)
    return centre * lax.rsqrt(spread + 1e-05)


def attend_patch(rows, qkv_weight, proj_weight, up_weight, down_weight):
    base = rows.astype(jnp.float32)
    normed = layer_norm(base).astype(jnp.bfloat16)
    projected = jnp.dot(normed, qkv_weight, preferred_element_type=jnp.float32).astype(jnp.bfloat16)
    width = rows.shape[1]
    count = rows.shape[0]
    query = projected[:, :width].reshape(count, HEADS, HD)
    keyset = projected[:, width : 2 * width].reshape(count, HEADS, HD)
    valueset = projected[:, 2 * width :].reshape(count, HEADS, HD)
    scores = jnp.einsum("qhd,khd->hqk", query, keyset, preferred_element_type=jnp.float32) * (
        1.0 / math.sqrt(HD)
    )
    largest = jnp.max(scores, axis=-1, keepdims=True)
    expo = jnp.exp(scores - largest)
    weights = (expo / jnp.sum(expo, axis=-1, keepdims=True)).astype(jnp.bfloat16)
    attended = jnp.einsum(
        "hqk,khd->qhd", weights, valueset, preferred_element_type=jnp.float32
    ).astype(jnp.bfloat16)
    middle = base + jnp.dot(
        attended.reshape(count, width), proj_weight, preferred_element_type=jnp.float32
    )
    second = layer_norm(middle).astype(jnp.bfloat16)
    hidden = jax.nn.gelu(
        jnp.dot(second, up_weight, preferred_element_type=jnp.float32), approximate=True
    ).astype(jnp.bfloat16)
    final = middle + jnp.dot(hidden, down_weight, preferred_element_type=jnp.float32)
    return final.astype(jnp.bfloat16)


def onehot_gather_kernel(index_ref, table_ref, out_ref, acc_ref):
    rows = index_ref.shape[0]
    chunk = 512
    wanted = index_ref[...]
    acc_ref[...] = jnp.zeros_like(acc_ref)
    for part in range(table_ref.shape[0] // chunk):
        ids = lax.broadcasted_iota(jnp.int32, (rows, chunk), 1) + part * chunk
        pick = jnp.where(wanted == ids, 1.0, 0.0).astype(jnp.bfloat16)
        acc_ref[...] += jnp.dot(
            pick, table_ref[pl.ds(part * chunk, chunk), :], preferred_element_type=jnp.float32
        )
    out_ref[...] = acc_ref[...].astype(out_ref.dtype)


def onehot_gather(table, index):
    count = index.shape[0]
    width = table.shape[1]
    tile = 256
    return pl.pallas_call(
        onehot_gather_kernel,
        grid=(count // tile,),
        in_specs=[
            pl.BlockSpec((tile, 1), lambda i: (i, 0)),
            pl.BlockSpec(table.shape, lambda i: (0, 0)),
        ],
        out_specs=pl.BlockSpec((tile, width), lambda i: (i, 0)),
        out_shape=jax.ShapeDtypeStruct((count, width), table.dtype),
        scratch_shapes=[pltpu.VMEM((tile, width), jnp.float32)],
    )(index.reshape(count, 1), table)


MESH = pl.DeviceIdType.MESH


def gather_rows(index_ref, table_ref, out_ref, first, last):
    tile = 512
    chunk = 512

    def one_tile(i, carry):
        rows = pl.ds(pl.multiple_of(i * tile, tile), tile)
        wanted = index_ref[:, rows]
        total = jnp.zeros((tile, out_ref.shape[1]), jnp.float32)
        for part in range(table_ref.shape[0] // chunk):
            ids = lax.broadcasted_iota(jnp.int32, (chunk, tile), 0) + part * chunk
            pick = jnp.where(wanted == ids, 1.0, 0.0).astype(jnp.bfloat16)
            total += lax.dot_general(
                pick,
                table_ref[pl.ds(part * chunk, chunk), :],
                (((0,), (0,)), ((), ())),
                preferred_element_type=jnp.float32,
            )
        out_ref[rows, :] = total.astype(out_ref.dtype)
        return carry

    lax.fori_loop(first, last, one_tile, 0)


def count_gather_kernel(nx, ny, index_ref, table_ref, mine_ref, rows_ref, out_ref, row_buf, grid_buf, send1, recv1, send2, recv2, own_sem):
    me_x = lax.axis_index("gx")
    me_y = lax.axis_index("gy")
    barrier = pltpu.get_barrier_semaphore()
    for k in range(1, ny):
        pl.semaphore_signal(
            barrier, inc=1, device_id=(me_x, lax.rem(me_y + k, ny)), device_id_type=MESH
        )
    for k in range(1, nx):
        pl.semaphore_signal(
            barrier, inc=1, device_id=(lax.rem(me_x + k, nx), me_y), device_id_type=MESH
        )
    pl.semaphore_wait(barrier, nx + ny - 2)

    own = pltpu.make_async_copy(mine_ref, row_buf.at[pl.ds(me_y, 1)], own_sem.at[0])
    own.start()
    for k in range(1, ny):
        pltpu.make_async_remote_copy(
            src_ref=mine_ref,
            dst_ref=row_buf.at[pl.ds(me_y, 1)],
            send_sem=send1.at[k],
            recv_sem=recv1.at[k],
            device_id=(me_x, lax.rem(me_y + k, ny)),
            device_id_type=MESH,
        ).start()
    tiles = rows_ref.shape[0] // 512
    gather_rows(index_ref, table_ref, rows_ref, 0, tiles // 2)
    own.wait()
    for k in range(1, ny):
        sender = lax.rem(me_y - k + ny, ny)
        copy = pltpu.make_async_remote_copy(
            src_ref=mine_ref,
            dst_ref=row_buf.at[pl.ds(sender, 1)],
            send_sem=send1.at[k],
            recv_sem=recv1.at[k],
            device_id=(me_x, sender),
            device_id_type=MESH,
        )
        copy.wait_send()
        copy.wait_recv()

    own = pltpu.make_async_copy(row_buf, grid_buf.at[me_x], own_sem.at[1])
    own.start()
    for k in range(1, nx):
        pltpu.make_async_remote_copy(
            src_ref=row_buf,
            dst_ref=grid_buf.at[me_x],
            send_sem=send2.at[k],
            recv_sem=recv2.at[k],
            device_id=(lax.rem(me_x + k, nx), me_y),
            device_id_type=MESH,
        ).start()
    gather_rows(index_ref, table_ref, rows_ref, tiles // 2, tiles)
    own.wait()
    for k in range(1, nx):
        sender = lax.rem(me_x - k + nx, nx)
        copy = pltpu.make_async_remote_copy(
            src_ref=row_buf,
            dst_ref=grid_buf.at[sender],
            send_sem=send2.at[k],
            recv_sem=recv2.at[k],
            device_id=(sender, me_y),
            device_id_type=MESH,
        )
        copy.wait_send()
        copy.wait_recv()
    out_ref[...] = grid_buf[...]


def gather_counts(mine, table, index):
    nx = lax.axis_size("gx")
    ny = lax.axis_size("gy")
    lanes = 128
    listed, grid = pl.pallas_call(
        functools.partial(count_gather_kernel, nx, ny),
        out_shape=(
            jax.ShapeDtypeStruct((index.shape[0], table.shape[1]), table.dtype),
            jax.ShapeDtypeStruct((nx, ny, lanes), jnp.int32),
        ),
        in_specs=[pl.BlockSpec(memory_space=pltpu.VMEM)] * 3,
        out_specs=(pl.BlockSpec(memory_space=pltpu.VMEM), pl.BlockSpec(memory_space=pltpu.VMEM)),
        scratch_shapes=[
            pltpu.VMEM((ny, lanes), jnp.int32),
            pltpu.VMEM((nx, ny, lanes), jnp.int32),
            pltpu.SemaphoreType.DMA((ny,)),
            pltpu.SemaphoreType.DMA((ny,)),
            pltpu.SemaphoreType.DMA((nx,)),
            pltpu.SemaphoreType.DMA((nx,)),
            pltpu.SemaphoreType.DMA((2,)),
        ],
        compiler_params=pltpu.CompilerParams(collective_id=0, has_side_effects=True),
    )(index.reshape(1, -1), table, jnp.broadcast_to(mine, (1, lanes)))
    return listed, grid[:, :, 0].reshape(nx * ny)


def attention_kernel(q_ref, k_ref, v_ref, base_ref, proj_ref, up_ref, down_ref, out_ref):
    query = q_ref[...]
    keyset = k_ref[...]
    valueset = v_ref[...]
    width = query.shape[1]
    head_of = lax.broadcasted_iota(jnp.int32, (1, width), 1) // HD
    attended = jnp.zeros((query.shape[0], width), jnp.float32)
    for head in range(HEADS):
        mine = head_of == head
        scores = lax.dot_general(
            jnp.where(mine, query, jnp.zeros_like(query)),
            keyset,
            (((1,), (1,)), ((), ())),
            preferred_element_type=jnp.float32,
        ) * (1.0 / math.sqrt(HD))
        largest = jnp.max(scores, axis=-1, keepdims=True)
        expo = jnp.exp(scores - largest)
        scale = 1.0 / jnp.sum(expo, axis=-1, keepdims=True)
        mixed = jnp.dot(expo.astype(jnp.bfloat16), valueset, preferred_element_type=jnp.float32)
        attended = jnp.where(mine, mixed * scale, attended)
    middle = base_ref[...].astype(jnp.float32) + jnp.dot(
        attended.astype(jnp.bfloat16), proj_ref[...], preferred_element_type=jnp.float32
    )
    second = layer_norm(middle).astype(jnp.bfloat16)
    hidden = jax.nn.gelu(
        jnp.dot(second, up_ref[...], preferred_element_type=jnp.float32), approximate=True
    ).astype(jnp.bfloat16)
    final = middle + jnp.dot(hidden, down_ref[...], preferred_element_type=jnp.float32)
    out_ref[...] = final.astype(out_ref.dtype)


def attention_block(rows, qkv_weight, proj_weight, up_weight, down_weight):
    count, width = rows.shape
    base = rows.astype(jnp.float32)
    normed = layer_norm(base).astype(jnp.bfloat16)
    projected = jnp.dot(normed, qkv_weight, preferred_element_type=jnp.float32).astype(jnp.bfloat16)
    tile = 512
    tiles = PATCH // tile
    grid = (count // PATCH, tiles)
    return pl.pallas_call(
        attention_kernel,
        grid=grid,
        in_specs=[
            pl.BlockSpec((tile, width), lambda p, t: (p * tiles + t, 0)),
            pl.BlockSpec((PATCH, width), lambda p, t: (p, 1)),
            pl.BlockSpec((PATCH, width), lambda p, t: (p, 2)),
            pl.BlockSpec((tile, width), lambda p, t: (p * tiles + t, 0)),
            pl.BlockSpec((width, width), lambda p, t: (0, 0)),
            pl.BlockSpec(up_weight.shape, lambda p, t: (0, 0)),
            pl.BlockSpec(down_weight.shape, lambda p, t: (0, 0)),
        ],
        out_specs=pl.BlockSpec((tile, width), lambda p, t: (p * tiles + t, 0)),
        out_shape=jax.ShapeDtypeStruct((count, width), rows.dtype),
    )(projected, projected, projected, rows, proj_weight, up_weight, down_weight)


def feed_forward(middle, up_weight, down_weight):
    second = layer_norm(middle).astype(jnp.bfloat16)
    hidden = jax.nn.gelu(
        jnp.dot(second, up_weight, preferred_element_type=jnp.float32), approximate=True
    ).astype(jnp.bfloat16)
    final = middle + jnp.dot(hidden, down_weight, preferred_element_type=jnp.float32)
    return final.astype(jnp.bfloat16)


def curve_tables(count_x, count_y):
    square = count_y * count_y
    index = np.arange(square)
    coord_x = np.zeros(square, np.int64)
    coord_y = np.zeros(square, np.int64)
    remain = index.copy()
    level = 1
    while level < count_y:
        bit_x = remain // 2 % 2
        bit_y = np.bitwise_xor(remain, bit_x) % 2
        mirror = (bit_y == 0) & (bit_x == 1)
        moved_x = np.where(mirror, level - 1 - coord_x, coord_x)
        moved_y = np.where(mirror, level - 1 - coord_y, coord_y)
        turned = bit_y == 0
        coord_x = np.where(turned, moved_y, moved_x) + level * bit_x
        coord_y = np.where(turned, moved_x, moved_y) + level * bit_y
        remain = remain // 4
        level = level * 2
    position = np.arange(count_x * count_y)
    along_x = coord_x[position % square] + (position // square) * count_y
    along_y = coord_y[position % square]
    return [int(d) for d in along_x * count_y + along_y]


def conv_kernel(shifted_ref, features_ref, weight_ref, linear_ref, out_ref):
    rows = features_ref.shape[0]
    side = features_ref.shape[1]
    width = features_ref.shape[-1]
    first = pl.program_id(0) * rows
    total = jnp.zeros((rows * side, width), jnp.float32)
    for offset in range(9):
        step_x = offset // 3
        step_y = offset % 3
        window = shifted_ref[pl.ds(first + step_x, rows), pl.ds(step_y, side)].reshape(rows * side, width)
        total += jnp.dot(window, weight_ref[offset], preferred_element_type=jnp.float32)
    linear = jnp.dot(total.astype(jnp.bfloat16), linear_ref[...], preferred_element_type=jnp.float32)
    base = features_ref[...].reshape(rows * side, width).astype(jnp.float32)
    out_ref[...] = (base + layer_norm(linear)).astype(out_ref.dtype)


def encode(padded, features, conv_weight, cpe_linear):
    span_x, span_y, width = features.shape
    shifted = padded
    rows = 32
    return pl.pallas_call(
        conv_kernel,
        grid=(span_x // rows,),
        in_specs=[
            pl.BlockSpec(memory_space=pltpu.VMEM),
            pl.BlockSpec((rows, span_y, width), lambda i: (i, 0, 0)),
            pl.BlockSpec(conv_weight.shape, lambda i: (0, 0, 0)),
            pl.BlockSpec(cpe_linear.shape, lambda i: (0, 0)),
        ],
        out_specs=pl.BlockSpec((rows * span_y, width), lambda i: (i, 0)),
        out_shape=jax.ShapeDtypeStruct((span_x * span_y, width), features.dtype),
    )(shifted, features, conv_weight, cpe_linear)


def shards(
    features,
    occupied,
    voxel_order,
    conv_weight,
    cpe_linear,
    qkv_weight,
    proj_weight,
    up_weight,
    down_weight,
):
    span_x, span_y, width = features.shape
    cells = span_x * span_y
    occ_flat = occupied.reshape(cells)
    mine = jnp.sum(occ_flat, dtype=jnp.int32)
    masked = features * occupied[:, :, None].astype(jnp.bfloat16)
    padded = with_halo(masked, (("gx", 0), ("gy", 1)), 1)
    encoded = encode(padded, features, conv_weight, cpe_linear)
    order = voxel_order[0]
    voxel = jnp.arange(cells, dtype=jnp.int32)
    _, rank_of = lax.sort_key_val(order, voxel, is_stable=False)
    key = (1 - occ_flat) * cells + rank_of
    _, listed_voxel = lax.sort_key_val(key, voxel, is_stable=False)
    capacity = CAP
    list_index = jnp.arange(LIVE + 2 * capacity, dtype=jnp.int32)
    picked = jnp.where(list_index < mine, listed_voxel[: LIVE + 2 * capacity], -1)
    list_rows, counts = gather_counts(mine, encoded, picked)
    devices = counts.shape[0]
    count_x = lax.axis_size("gx")
    count_y = lax.axis_size("gy")
    here_x = lax.axis_index("gx")
    here_y = lax.axis_index("gy")
    ranks = block_curve(count_x, count_y)
    position = ranks[here_x * count_y + here_y]
    by_position = jnp.zeros((devices,), jnp.int32).at[ranks].set(counts)
    starts = jnp.cumsum(by_position, dtype=jnp.int32) - by_position
    start_here = starts[position]
    excess = start_here - position * LIVE
    beyond = start_here + mine - (position + 1) * LIVE
    slot = jnp.arange(capacity, dtype=jnp.int32)
    empty = jnp.zeros((capacity, width), jnp.bfloat16)
    extended = jnp.concatenate([empty, list_rows], axis=0)
    mine_rows = lax.dynamic_slice_in_dim(extended, capacity - excess, LIVE, 0)
    to_prev = jnp.where((slot < -excess)[:, None], list_rows[:capacity], empty)
    to_next = jnp.where(
        (slot < beyond)[:, None], lax.dynamic_slice_in_dim(list_rows, LIVE - excess, capacity, 0), empty
    )
    device_at = curve_tables(count_x, count_y)
    forward = [(device_at[p], device_at[p + 1]) for p in range(devices - 1)]
    backward = [(target, source) for source, target in forward]
    from_prev = lax.ppermute(to_next, ("gx", "gy"), forward)
    from_next = lax.ppermute(to_prev, ("gx", "gy"), backward)
    from_prev = jnp.where((slot < excess)[:, None], from_prev, empty)
    from_next = jnp.where((slot < -beyond)[:, None], from_next, empty)
    leading = jnp.concatenate(
        [from_prev, jnp.zeros((LIVE - capacity, width), jnp.bfloat16)], axis=0
    )
    trailing = lax.dynamic_slice_in_dim(
        jnp.concatenate([jnp.zeros((LIVE, width), jnp.bfloat16), from_next], axis=0),
        -beyond,
        LIVE,
        0,
    )
    owned = mine_rows + leading + trailing
    return attention_block(owned, qkv_weight, proj_weight, up_weight, down_weight)


def solution(mesh):
    return jax.shard_map(
        shards,
        mesh=mesh,
        in_specs=(
            P("gx", "gy", None),
            P("gx", "gy"),
            P(("gx", "gy"), None),
            P(),
            P(),
            P(),
            P(),
            P(),
            P(),
        ),
        out_specs=P(("gx", "gy"), None),
        check_vma=False,
    )
```

```python
import functools
import math

import jax
import numpy as np
import jax.numpy as jnp
from jax import lax
from jax.experimental import pallas as pl
from jax.experimental.pallas import tpu as pltpu
from jax.sharding import PartitionSpec as P

HEADS = 8
PATCH = 1024
LIVE = 2048
CAP = 256
HD = 32


def with_halo(block, sides, width):
    for axis, dim in sides:
        count = lax.axis_size(axis)
        forward = [(i, i + 1) for i in range(count - 1)]
        backward = [(target, source) for source, target in forward]
        low = lax.ppermute(
            lax.slice_in_dim(block, block.shape[dim] - width, None, axis=dim), axis, forward
        )
        high = lax.ppermute(lax.slice_in_dim(block, 0, width, axis=dim), axis, backward)
        block = jnp.concatenate([low, block, high], axis=dim)
    return block


def passed_along(block, axis, distance):
    devices = range(lax.axis_size(axis))
    route = [(i - distance, i) for i in devices if i - distance in devices]
    return lax.ppermute(block, axis, route)


def hilbert_points(side):
    index = jnp.arange(side * side, dtype=jnp.int32)
    coord_x = jnp.zeros((side * side,), jnp.int32)
    coord_y = jnp.zeros((side * side,), jnp.int32)
    remain = index
    level = 1
    while level < side:
        bit_x = remain // 2 % 2
        bit_y = jnp.bitwise_xor(remain, bit_x) % 2
        mirror = (bit_y == 0) & (bit_x == 1)
        moved_x = jnp.where(mirror, level - 1 - coord_x, coord_x)
        moved_y = jnp.where(mirror, level - 1 - coord_y, coord_y)
        turned = bit_y == 0
        coord_x = jnp.where(turned, moved_y, moved_x) + level * bit_x
        coord_y = jnp.where(turned, moved_x, moved_y) + level * bit_y
        remain = remain // 4
        level = level * 2
    return (coord_x, coord_y)


def block_curve(count_x, count_y):
    total = count_x * count_y
    square = count_y * count_y
    position = jnp.arange(total, dtype=jnp.int32)
    half = position // square
    inner_x, inner_y = hilbert_points(count_y)
    along_x = inner_x[position % square] + half * count_y
    along_y = inner_y[position % square]
    device = along_x * count_y + along_y
    return jnp.zeros((total,), jnp.int32).at[device].set(position)


def layer_norm(values):
    centre = values - jnp.mean(values, axis=-1, keepdims=True)
    spread = jnp.mean(centre * centre, axis=-1, keepdims=True)
    return centre * lax.rsqrt(spread + 1e-05)


def attend_patch(rows, qkv_weight, proj_weight, up_weight, down_weight):
    base = rows.astype(jnp.float32)
    normed = layer_norm(base).astype(jnp.bfloat16)
    projected = jnp.dot(normed, qkv_weight, preferred_element_type=jnp.float32).astype(jnp.bfloat16)
    width = rows.shape[1]
    count = rows.shape[0]
    query = projected[:, :width].reshape(count, HEADS, HD)
    keyset = projected[:, width : 2 * width].reshape(count, HEADS, HD)
    valueset = projected[:, 2 * width :].reshape(count, HEADS, HD)
    scores = jnp.einsum("qhd,khd->hqk", query, keyset, preferred_element_type=jnp.float32) * (
        1.0 / math.sqrt(HD)
    )
    largest = jnp.max(scores, axis=-1, keepdims=True)
    expo = jnp.exp(scores - largest)
    weights = (expo / jnp.sum(expo, axis=-1, keepdims=True)).astype(jnp.bfloat16)
    attended = jnp.einsum(
        "hqk,khd->qhd", weights, valueset, preferred_element_type=jnp.float32
    ).astype(jnp.bfloat16)
    middle = base + jnp.dot(
        attended.reshape(count, width), proj_weight, preferred_element_type=jnp.float32
    )
    second = layer_norm(middle).astype(jnp.bfloat16)
    hidden = jax.nn.gelu(
        jnp.dot(second, up_weight, preferred_element_type=jnp.float32), approximate=True
    ).astype(jnp.bfloat16)
    final = middle + jnp.dot(hidden, down_weight, preferred_element_type=jnp.float32)
    return final.astype(jnp.bfloat16)


def onehot_gather_kernel(index_ref, table_ref, out_ref, acc_ref):
    rows = index_ref.shape[0]
    chunk = 512
    wanted = index_ref[...]
    acc_ref[...] = jnp.zeros_like(acc_ref)
    for part in range(table_ref.shape[0] // chunk):
        ids = lax.broadcasted_iota(jnp.int32, (rows, chunk), 1) + part * chunk
        pick = jnp.where(wanted == ids, 1.0, 0.0).astype(jnp.bfloat16)
        acc_ref[...] += jnp.dot(
            pick, table_ref[pl.ds(part * chunk, chunk), :], preferred_element_type=jnp.float32
        )
    out_ref[...] = acc_ref[...].astype(out_ref.dtype)


def onehot_gather(table, index):
    count = index.shape[0]
    width = table.shape[1]
    tile = 256
    return pl.pallas_call(
        onehot_gather_kernel,
        grid=(count // tile,),
        in_specs=[
            pl.BlockSpec((tile, 1), lambda i: (i, 0)),
            pl.BlockSpec(table.shape, lambda i: (0, 0)),
        ],
        out_specs=pl.BlockSpec((tile, width), lambda i: (i, 0)),
        out_shape=jax.ShapeDtypeStruct((count, width), table.dtype),
        scratch_shapes=[pltpu.VMEM((tile, width), jnp.float32)],
    )(index.reshape(count, 1), table)


MESH = pl.DeviceIdType.MESH


def gather_rows(index_ref, table_ref, out_ref, first, last):
    tile = 512
    chunk = 1024

    def one_tile(i, carry):
        rows = pl.ds(pl.multiple_of(i * tile, tile), tile)
        wanted = index_ref[:, rows]
        total = jnp.zeros((tile, out_ref.shape[1]), jnp.float32)
        for part in range(table_ref.shape[0] // chunk):
            ids = lax.broadcasted_iota(jnp.int32, (chunk, tile), 0) + part * chunk
            pick = jnp.where(wanted == ids, 1.0, 0.0).astype(jnp.bfloat16)
            total += lax.dot_general(
                pick,
                table_ref[pl.ds(part * chunk, chunk), :],
                (((0,), (0,)), ((), ())),
                preferred_element_type=jnp.float32,
            )
        out_ref[rows, :] = total.astype(out_ref.dtype)
        return carry

    lax.fori_loop(first, last, one_tile, 0)


def count_gather_kernel(nx, ny, index_ref, table_ref, mine_ref, rows_ref, out_ref, row_buf, grid_buf, send1, recv1, send2, recv2, own_sem):
    me_x = lax.axis_index("gx")
    me_y = lax.axis_index("gy")
    barrier = pltpu.get_barrier_semaphore()
    for k in range(1, ny):
        pl.semaphore_signal(
            barrier, inc=1, device_id=(me_x, lax.rem(me_y + k, ny)), device_id_type=MESH
        )
    for k in range(1, nx):
        pl.semaphore_signal(
            barrier, inc=1, device_id=(lax.rem(me_x + k, nx), me_y), device_id_type=MESH
        )
    pl.semaphore_wait(barrier, nx + ny - 2)

    own = pltpu.make_async_copy(mine_ref, row_buf.at[pl.ds(me_y, 1)], own_sem.at[0])
    own.start()
    for k in range(1, ny):
        pltpu.make_async_remote_copy(
            src_ref=mine_ref,
            dst_ref=row_buf.at[pl.ds(me_y, 1)],
            send_sem=send1.at[k],
            recv_sem=recv1.at[k],
            device_id=(me_x, lax.rem(me_y + k, ny)),
            device_id_type=MESH,
        ).start()
    tiles = rows_ref.shape[0] // 512
    gather_rows(index_ref, table_ref, rows_ref, 0, tiles // 2)
    own.wait()
    for k in range(1, ny):
        sender = lax.rem(me_y - k + ny, ny)
        copy = pltpu.make_async_remote_copy(
            src_ref=mine_ref,
            dst_ref=row_buf.at[pl.ds(sender, 1)],
            send_sem=send1.at[k],
            recv_sem=recv1.at[k],
            device_id=(me_x, sender),
            device_id_type=MESH,
        )
        copy.wait_send()
        copy.wait_recv()

    own = pltpu.make_async_copy(row_buf, grid_buf.at[me_x], own_sem.at[1])
    own.start()
    for k in range(1, nx):
        pltpu.make_async_remote_copy(
            src_ref=row_buf,
            dst_ref=grid_buf.at[me_x],
            send_sem=send2.at[k],
            recv_sem=recv2.at[k],
            device_id=(lax.rem(me_x + k, nx), me_y),
            device_id_type=MESH,
        ).start()
    gather_rows(index_ref, table_ref, rows_ref, tiles // 2, tiles)
    own.wait()
    for k in range(1, nx):
        sender = lax.rem(me_x - k + nx, nx)
        copy = pltpu.make_async_remote_copy(
            src_ref=row_buf,
            dst_ref=grid_buf.at[sender],
            send_sem=send2.at[k],
            recv_sem=recv2.at[k],
            device_id=(sender, me_y),
            device_id_type=MESH,
        )
        copy.wait_send()
        copy.wait_recv()
    out_ref[...] = grid_buf[...]


def gather_counts(mine, table, index):
    nx = lax.axis_size("gx")
    ny = lax.axis_size("gy")
    lanes = 128
    listed, grid = pl.pallas_call(
        functools.partial(count_gather_kernel, nx, ny),
        out_shape=(
            jax.ShapeDtypeStruct((index.shape[0], table.shape[1]), table.dtype),
            jax.ShapeDtypeStruct((nx, ny, lanes), jnp.int32),
        ),
        in_specs=[pl.BlockSpec(memory_space=pltpu.VMEM)] * 3,
        out_specs=(pl.BlockSpec(memory_space=pltpu.VMEM), pl.BlockSpec(memory_space=pltpu.VMEM)),
        scratch_shapes=[
            pltpu.VMEM((ny, lanes), jnp.int32),
            pltpu.VMEM((nx, ny, lanes), jnp.int32),
            pltpu.SemaphoreType.DMA((ny,)),
            pltpu.SemaphoreType.DMA((ny,)),
            pltpu.SemaphoreType.DMA((nx,)),
            pltpu.SemaphoreType.DMA((nx,)),
            pltpu.SemaphoreType.DMA((2,)),
        ],
        compiler_params=pltpu.CompilerParams(collective_id=0, has_side_effects=True),
    )(index.reshape(1, -1), table, jnp.broadcast_to(mine, (1, lanes)))
    return listed, grid[:, :, 0].reshape(nx * ny)


def attention_kernel(q_ref, k_ref, v_ref, base_ref, proj_ref, up_ref, down_ref, out_ref):
    query = q_ref[...]
    keyset = k_ref[...]
    valueset = v_ref[...]
    width = query.shape[1]
    head_of = lax.broadcasted_iota(jnp.int32, (1, width), 1) // HD
    attended = jnp.zeros((query.shape[0], width), jnp.float32)
    for head in range(HEADS):
        mine = head_of == head
        scores = lax.dot_general(
            jnp.where(mine, query, jnp.zeros_like(query)),
            keyset,
            (((1,), (1,)), ((), ())),
            preferred_element_type=jnp.float32,
        ) * (1.0 / math.sqrt(HD))
        largest = jnp.max(scores, axis=-1, keepdims=True)
        expo = jnp.exp(scores - largest)
        scale = 1.0 / jnp.sum(expo, axis=-1, keepdims=True)
        mixed = jnp.dot(expo.astype(jnp.bfloat16), valueset, preferred_element_type=jnp.float32)
        attended = jnp.where(mine, mixed * scale, attended)
    middle = base_ref[...].astype(jnp.float32) + jnp.dot(
        attended.astype(jnp.bfloat16), proj_ref[...], preferred_element_type=jnp.float32
    )
    second = layer_norm(middle).astype(jnp.bfloat16)
    hidden = jax.nn.gelu(
        jnp.dot(second, up_ref[...], preferred_element_type=jnp.float32), approximate=True
    ).astype(jnp.bfloat16)
    final = middle + jnp.dot(hidden, down_ref[...], preferred_element_type=jnp.float32)
    out_ref[...] = final.astype(out_ref.dtype)


def attention_block(rows, qkv_weight, proj_weight, up_weight, down_weight):
    count, width = rows.shape
    base = rows.astype(jnp.float32)
    normed = layer_norm(base).astype(jnp.bfloat16)
    projected = jnp.dot(normed, qkv_weight, preferred_element_type=jnp.float32).astype(jnp.bfloat16)
    tile = 512
    tiles = PATCH // tile
    grid = (count // PATCH, tiles)
    return pl.pallas_call(
        attention_kernel,
        grid=grid,
        in_specs=[
            pl.BlockSpec((tile, width), lambda p, t: (p * tiles + t, 0)),
            pl.BlockSpec((PATCH, width), lambda p, t: (p, 1)),
            pl.BlockSpec((PATCH, width), lambda p, t: (p, 2)),
            pl.BlockSpec((tile, width), lambda p, t: (p * tiles + t, 0)),
            pl.BlockSpec((width, width), lambda p, t: (0, 0)),
            pl.BlockSpec(up_weight.shape, lambda p, t: (0, 0)),
            pl.BlockSpec(down_weight.shape, lambda p, t: (0, 0)),
        ],
        out_specs=pl.BlockSpec((tile, width), lambda p, t: (p * tiles + t, 0)),
        out_shape=jax.ShapeDtypeStruct((count, width), rows.dtype),
    )(projected, projected, projected, rows, proj_weight, up_weight, down_weight)


def feed_forward(middle, up_weight, down_weight):
    second = layer_norm(middle).astype(jnp.bfloat16)
    hidden = jax.nn.gelu(
        jnp.dot(second, up_weight, preferred_element_type=jnp.float32), approximate=True
    ).astype(jnp.bfloat16)
    final = middle + jnp.dot(hidden, down_weight, preferred_element_type=jnp.float32)
    return final.astype(jnp.bfloat16)


def curve_tables(count_x, count_y):
    square = count_y * count_y
    index = np.arange(square)
    coord_x = np.zeros(square, np.int64)
    coord_y = np.zeros(square, np.int64)
    remain = index.copy()
    level = 1
    while level < count_y:
        bit_x = remain // 2 % 2
        bit_y = np.bitwise_xor(remain, bit_x) % 2
        mirror = (bit_y == 0) & (bit_x == 1)
        moved_x = np.where(mirror, level - 1 - coord_x, coord_x)
        moved_y = np.where(mirror, level - 1 - coord_y, coord_y)
        turned = bit_y == 0
        coord_x = np.where(turned, moved_y, moved_x) + level * bit_x
        coord_y = np.where(turned, moved_x, moved_y) + level * bit_y
        remain = remain // 4
        level = level * 2
    position = np.arange(count_x * count_y)
    along_x = coord_x[position % square] + (position // square) * count_y
    along_y = coord_y[position % square]
    return [int(d) for d in along_x * count_y + along_y]


def conv_kernel(shifted_ref, features_ref, weight_ref, linear_ref, out_ref):
    rows = features_ref.shape[0]
    side = features_ref.shape[1]
    width = features_ref.shape[-1]
    first = pl.program_id(0) * rows
    total = jnp.zeros((rows * side, width), jnp.float32)
    for offset in range(9):
        step_x = offset // 3
        step_y = offset % 3
        window = shifted_ref[pl.ds(first + step_x, rows), pl.ds(step_y, side)].reshape(rows * side, width)
        total += jnp.dot(window, weight_ref[offset], preferred_element_type=jnp.float32)
    linear = jnp.dot(total.astype(jnp.bfloat16), linear_ref[...], preferred_element_type=jnp.float32)
    base = features_ref[...].reshape(rows * side, width).astype(jnp.float32)
    out_ref[...] = (base + layer_norm(linear)).astype(out_ref.dtype)


def encode(padded, features, conv_weight, cpe_linear):
    span_x, span_y, width = features.shape
    shifted = padded
    rows = 32
    return pl.pallas_call(
        conv_kernel,
        grid=(span_x // rows,),
        in_specs=[
            pl.BlockSpec(memory_space=pltpu.VMEM),
            pl.BlockSpec((rows, span_y, width), lambda i: (i, 0, 0)),
            pl.BlockSpec(conv_weight.shape, lambda i: (0, 0, 0)),
            pl.BlockSpec(cpe_linear.shape, lambda i: (0, 0)),
        ],
        out_specs=pl.BlockSpec((rows * span_y, width), lambda i: (i, 0)),
        out_shape=jax.ShapeDtypeStruct((span_x * span_y, width), features.dtype),
    )(shifted, features, conv_weight, cpe_linear)


def shards(
    features,
    occupied,
    voxel_order,
    conv_weight,
    cpe_linear,
    qkv_weight,
    proj_weight,
    up_weight,
    down_weight,
):
    span_x, span_y, width = features.shape
    cells = span_x * span_y
    occ_flat = occupied.reshape(cells)
    mine = jnp.sum(occ_flat, dtype=jnp.int32)
    masked = features * occupied[:, :, None].astype(jnp.bfloat16)
    padded = with_halo(masked, (("gx", 0), ("gy", 1)), 1)
    encoded = encode(padded, features, conv_weight, cpe_linear)
    order = voxel_order[0]
    voxel = jnp.arange(cells, dtype=jnp.int32)
    _, rank_of = lax.sort_key_val(order, voxel, is_stable=False)
    key = (1 - occ_flat) * cells + rank_of
    _, listed_voxel = lax.sort_key_val(key, voxel, is_stable=False)
    capacity = CAP
    list_index = jnp.arange(LIVE + 2 * capacity, dtype=jnp.int32)
    picked = jnp.where(list_index < mine, listed_voxel[: LIVE + 2 * capacity], -1)
    list_rows, counts = gather_counts(mine, encoded, picked)
    devices = counts.shape[0]
    count_x = lax.axis_size("gx")
    count_y = lax.axis_size("gy")
    here_x = lax.axis_index("gx")
    here_y = lax.axis_index("gy")
    ranks = block_curve(count_x, count_y)
    position = ranks[here_x * count_y + here_y]
    by_position = jnp.zeros((devices,), jnp.int32).at[ranks].set(counts)
    starts = jnp.cumsum(by_position, dtype=jnp.int32) - by_position
    start_here = starts[position]
    excess = start_here - position * LIVE
    beyond = start_here + mine - (position + 1) * LIVE
    slot = jnp.arange(capacity, dtype=jnp.int32)
    empty = jnp.zeros((capacity, width), jnp.bfloat16)
    extended = jnp.concatenate([empty, list_rows], axis=0)
    mine_rows = lax.dynamic_slice_in_dim(extended, capacity - excess, LIVE, 0)
    to_prev = jnp.where((slot < -excess)[:, None], list_rows[:capacity], empty)
    to_next = jnp.where(
        (slot < beyond)[:, None], lax.dynamic_slice_in_dim(list_rows, LIVE - excess, capacity, 0), empty
    )
    device_at = curve_tables(count_x, count_y)
    forward = [(device_at[p], device_at[p + 1]) for p in range(devices - 1)]
    backward = [(target, source) for source, target in forward]
    from_prev = lax.ppermute(to_next, ("gx", "gy"), forward)
    from_next = lax.ppermute(to_prev, ("gx", "gy"), backward)
    from_prev = jnp.where((slot < excess)[:, None], from_prev, empty)
    from_next = jnp.where((slot < -beyond)[:, None], from_next, empty)
    leading = jnp.concatenate(
        [from_prev, jnp.zeros((LIVE - capacity, width), jnp.bfloat16)], axis=0
    )
    trailing = lax.dynamic_slice_in_dim(
        jnp.concatenate([jnp.zeros((LIVE, width), jnp.bfloat16), from_next], axis=0),
        -beyond,
        LIVE,
        0,
    )
    owned = mine_rows + leading + trailing
    return attention_block(owned, qkv_weight, proj_weight, up_weight, down_weight)


def solution(mesh):
    return jax.shard_map(
        shards,
        mesh=mesh,
        in_specs=(
            P("gx", "gy", None),
            P("gx", "gy"),
            P(("gx", "gy"), None),
            P(),
            P(),
            P(),
            P(),
            P(),
            P(),
        ),
        out_specs=P(("gx", "gy"), None),
        check_vma=False,
    )
```
